128 devices in a mesh: req: 16 (over z, x_hi, core), head: 8 (over y, x_lo).
Axes of the slice: x: 4 (x_hi: 2, x_lo: 2; x = x_hi * 2 + x_lo), y: 4, z: 4, core: 2. Of those that a mesh axis runs over, the one named last changes fastest.
Arguments:
- hidden_in: bfloat16 [128, 8192], P('head', 'req'), may hold values from -40 to 40
- attn_gain: bfloat16 [8192], P('req'), may hold values from 0.5 to 1.5
- w_qkv: bfloat16 [8192, 10240], P('req', 'head'), may hold values from -0.0625 to 0.0625
- w_out: bfloat16 [8192, 8192], P('head', 'req'), may hold values from -0.0625 to 0.0625
- k_cache: bfloat16 [128, 4096, 1024], P('req', None, 'head'), may hold values from -400 to 400
- v_cache: bfloat16 [128, 4096, 1024], P('req', None, 'head'), may hold values from -6 to 6
- lengths: int32 [128], P('req'), may hold values from 1 to 4096, 135168 in all
Outputs:
- hidden_out: bfloat16 [128, 8192], P('head', 'req')
The draws below stay inside these ranges and needn't reach their ends.
Inputs may be any that keep to these rules, and one draw needn't show every extreme that they name: One request holds exactly 4096 tokens; the lengths add up to 135168.
All inputs are finite; a program needn't handle non-finite values. No bound on the sum of `lengths` on one device may be relied on, other than what follows from the above.
Results may differ from the reference program's by a relative error of at most 0.0055.
Values may be sent and summed in bfloat16 or wider, within the bound.
A program may use at most 64 MiB of HBM per device.

```python
import math
import jax
import jax.numpy as jnp
import numpy as np
from jax import lax

D = 8192
KVH = 8
GROUP = 8
HD = 128
MAXLEN = 4096
REQS = 128
TOTAL_LEN = 135168


def draw_hidden_in(key, part):
    first_key = jax.random.fold_in(key, 0)
    column_scale = 0.5 + jnp.arange(D, dtype=jnp.float32) / D
    noise_draw = jax.random.normal(first_key, (REQS, D), jnp.float32)
    return jnp.clip(noise_draw * column_scale[None, :], -40.0, 40.0).astype(jnp.bfloat16)


def draw_k_cache(key, part):
    first_key = jax.random.fold_in(jax.random.fold_in(key, 7), 0)
    noise_draw = jax.random.normal(first_key, (REQS, MAXLEN, KVH * HD), jnp.float32)
    return jnp.clip(noise_draw, -400.0, 400.0).astype(jnp.bfloat16)


def levels(own_key, extent, cuts, smallest, top_value):
    def one(axis_at, parts):
        heights = jax.random.uniform(jax.random.fold_in(jax.random.fold_in(own_key, 6), axis_at), (parts,), jnp.float32, smallest / len(cuts), top_value / len(cuts))
        return jnp.repeat(jnp.exp(heights), extent[axis_at] // parts).reshape((-1,) + (1,) * (len(extent) - axis_at - 1))

    level = one(*cuts[0])
    for cut in cuts[1:]:
        level = level * one(*cut)
    return level


def length_profile(amount, total, limit, skew):
    loads = [(1 << 20) // math.isqrt(rank ** skew) + 1 for rank in range(2, amount + 1)]
    rest, given = total - limit - (amount - 1), [1] * (amount - 1)
    while rest > 0:
        candidates = [i for i in range(amount - 1) if given[i] < limit]
        pool, remaining = sum([loads[i] for i in candidates]), rest
        for i in candidates:
            more = min(limit - given[i], max(1, remaining * loads[i] // pool), rest)
            given[i] = given[i] + more
            rest = rest - more
    return np.array([limit] + given)


def ragged(stream_key, amount, total, reach, slope):
    if amount == 2:
        one = jax.random.randint(stream_key, (), max(1, total - reach), min(reach, total - 1) + 1)
        return jnp.stack([one, total - one])
    sizes = jnp.asarray(length_profile(amount, total, reach, slope), jnp.int32)
    twos = (amount - 1) // 2
    giver, sink = sizes[1:1 + 2 * twos:2], sizes[2:2 + 2 * twos:2]
    slack = jnp.minimum(giver - 1, reach - sink)
    shifted = jax.random.randint(jax.random.fold_in(stream_key, 1), (twos,), 0, 1 << 20) % (slack + 1)
    sizes = sizes.at[1:1 + 2 * twos:2].set(giver - shifted).at[2:2 + 2 * twos:2].set(sink + shifted)
    return sizes[jax.random.permutation(jax.random.fold_in(stream_key, 2), amount)]


def scatter_about(own_key, dims, spread, bound, cuts=(), kind=jnp.bfloat16):
    values = jax.random.normal(own_key, dims, jnp.float32) * spread
    if len(cuts) > 0:
        values = levels(own_key, dims, cuts, -0.22, 0.18) * values
    return jnp.clip(values, min=-bound, max=bound).astype(kind)


def setup_inputs(seed: int = 0) -> dict:
    key_of = jax.random.split(jax.random.key(seed), 8)
    hidden_in = draw_hidden_in(jax.random.fold_in(key_of[7], 71), 0)
    attn_gain = jnp.clip(0.5 + 1.0 * jax.random.uniform(key_of[1], (D,), jnp.float32) ** levels(key_of[1], (D,), ((0, 16),), -0.2, 0.2), 0.5, 1.5).astype(jnp.bfloat16)
    w_qkv = scatter_about(key_of[2], (D, KVH * (GROUP + 2) * HD), D ** -0.5, 0.0625, ((0, 16), (1, 8)))
    w_out = scatter_about(key_of[3], (KVH * GROUP * HD, D), (KVH * GROUP * HD) ** -0.5, 0.0625, ((0, 8), (1, 16)))
    k_cache = draw_k_cache(jax.random.fold_in(key_of[7], 71), 0)
    v_cache = scatter_about(key_of[5], (REQS, MAXLEN, KVH * HD), 1.0, 6.0, ((0, 16), (2, 8)))
    lengths = ragged(key_of[6], REQS, TOTAL_LEN, MAXLEN, 3).astype(jnp.int32)
    return dict(hidden_in=hidden_in, attn_gain=attn_gain, w_qkv=w_qkv, w_out=w_out, k_cache=k_cache, v_cache=v_cache, lengths=lengths)


epsilon = 1e-05
rope_base = 500000.0

def rotate(vectors, positions):
    halfway = vectors.shape[-1] // 2
    frequency = jnp.exp(-jnp.log(rope_base) * 2.0 * jnp.arange(halfway, dtype=jnp.float32) / vectors.shape[-1])
    angles = positions.astype(jnp.float32)[:, None] * frequency[None, :]
    target_shape = (angles.shape[0],) + (1,) * (vectors.ndim - 2) + (halfway,)
    cosine = jnp.cos(angles).reshape(target_shape)
    sine_part = jnp.sin(angles).reshape(target_shape)
    first = vectors[..., :halfway]
    second = vectors[..., halfway:]
    return jnp.concatenate([first * cosine - second * sine_part, second * cosine + first * sine_part], axis=-1)

def reference(hidden_in, attn_gain, w_qkv, w_out, k_cache, v_cache, lengths):
    states = hidden_in.astype(jnp.float32)
    mean_square = lax.optimization_barrier(jnp.mean(states * states, axis=1, keepdims=True))
    normed = (states * lax.rsqrt(mean_square + epsilon) * attn_gain.astype(jnp.float32)[None, :]).astype(jnp.bfloat16)
    projected = jnp.dot(normed, w_qkv, preferred_element_type=jnp.float32).reshape(REQS, KVH, GROUP + 2, HD)
    queries = lax.optimization_barrier(rotate(projected[:, :, :GROUP], lengths).astype(jnp.bfloat16))
    new_keys = lax.optimization_barrier(rotate(projected[:, :, GROUP], lengths).astype(jnp.bfloat16))
    new_values = lax.optimization_barrier(projected[:, :, GROUP + 1].astype(jnp.bfloat16))
    factor = HD ** (-0.5)
    positions = jnp.arange(MAXLEN, dtype=jnp.int32)
    inside = positions[None, :] < lengths[:, None]

    def one_head(number):
        cached_keys = lax.dynamic_slice_in_dim(k_cache, number * HD, HD, 2).astype(jnp.float32)
        cached_values = lax.dynamic_slice_in_dim(v_cache, number * HD, HD, 2).astype(jnp.float32)
        head_queries = lax.dynamic_index_in_dim(queries, number, 1, keepdims=False).astype(jnp.float32)
        head_key = lax.dynamic_index_in_dim(new_keys, number, 1, keepdims=False).astype(jnp.float32)
        head_value = lax.dynamic_index_in_dim(new_values, number, 1, keepdims=False).astype(jnp.float32)
        scores = jnp.einsum('bgd,bpd->bgp', head_queries, cached_keys) * factor
        scores = jnp.where(inside[:, None, :], scores, -1e+30)
        own_score = jnp.einsum('bgd,bd->bg', head_queries, head_key) * factor
        running = jnp.maximum(lax.optimization_barrier(jnp.max(scores, axis=2)), own_score)
        weights = jnp.where(inside[:, None, :], jnp.exp(scores - running[:, :, None]), 0.0)
        own_weight = jnp.exp(own_score - running)
        totals = lax.optimization_barrier(jnp.sum(weights, axis=2)) + own_weight
        probs = lax.optimization_barrier((weights / totals[:, :, None]).astype(jnp.bfloat16)).astype(jnp.float32)
        own_prob = lax.optimization_barrier((own_weight / totals).astype(jnp.bfloat16)).astype(jnp.float32)
        mixed = jnp.einsum('bgp,bpd->bgd', probs, cached_values) + own_prob[:, :, None] * head_value[:, None, :]
        return mixed.astype(jnp.bfloat16)
    heads_out = lax.map(one_head, jnp.arange(KVH, dtype=jnp.int32))
    attended = jnp.transpose(heads_out, (1, 0, 2, 3)).reshape(REQS, KVH * GROUP * HD)
    output = jnp.dot(attended, w_out, preferred_element_type=jnp.float32)
    return (states + output).astype(jnp.bfloat16)
```

```python
import jax
import jax.numpy as jnp
from jax import lax
from jax.sharding import PartitionSpec as P

D = 8192
GROUP = 8
HD = 128


epsilon = 1e-05
rope_base = 500000.0


def rotate(vectors, positions):
    halfway = vectors.shape[-1] // 2
    frequency = jnp.exp(
        -jnp.log(rope_base) * 2.0 * jnp.arange(halfway, dtype=jnp.float32) / vectors.shape[-1]
    )
    angles = positions.astype(jnp.float32)[:, None] * frequency[None, :]
    target_shape = (angles.shape[0],) + (1,) * (vectors.ndim - 2) + (halfway,)
    cosine = jnp.cos(angles).reshape(target_shape)
    sine_part = jnp.sin(angles).reshape(target_shape)
    first = vectors[..., :halfway]
    second = vectors[..., halfway:]
    return jnp.concatenate(
        [first * cosine - second * sine_part, second * cosine + first * sine_part], axis=-1
    )


def own_part(own_score, running, totals, new_values):
    own_prob = lax.optimization_barrier(
        (jnp.exp(own_score - running) / totals).astype(jnp.bfloat16)
    )
    return own_prob.astype(jnp.float32)[..., None] * new_values.astype(jnp.float32)[:, :, None, :]


def attend_padded(queries, new_keys, new_values, cached_keys, cached_values, lengths, factor):
    slots = cached_keys.shape[1]
    inside = jnp.arange(slots, dtype=jnp.int32)[None, :] < lengths[:, None]
    scores = (
        jnp.einsum("rkgd,rpkd->rkgp", queries, cached_keys, preferred_element_type=jnp.float32)
        * factor
    )
    scores = jnp.where(inside[:, None, None, :], scores, -1e30)
    own_score = (
        jnp.einsum("rkgd,rkd->rkg", queries, new_keys, preferred_element_type=jnp.float32) * factor
    )
    running = jnp.maximum(jnp.max(scores, axis=3), own_score)
    weights = jnp.where(inside[:, None, None, :], jnp.exp(scores - running[..., None]), 0.0)
    totals = jnp.sum(weights, axis=3) + jnp.exp(own_score - running)
    probs = (weights / totals[..., None]).astype(jnp.bfloat16)
    mixed = jnp.einsum("rkgp,rpkd->rkgd", probs, cached_values, preferred_element_type=jnp.float32)
    mixed = mixed + own_part(own_score, running, totals, new_values)
    return mixed.astype(jnp.bfloat16)


def local(hidden_in, attn_gain, w_qkv, w_out, k_cache, v_cache, lengths):
    states = hidden_in.astype(jnp.float32)
    every_row = lax.all_gather(hidden_in, "head", axis=0, tiled=True).astype(jnp.float32)
    scaled = (every_row * attn_gain.astype(jnp.float32)[None, :]).astype(jnp.bfloat16)
    partial_square = jnp.sum(every_row * every_row, axis=1)
    partial = jnp.dot(scaled, w_qkv, preferred_element_type=jnp.float32)
    columns = partial.shape[1]
    packed = jnp.concatenate(
        [partial, jnp.broadcast_to(partial_square[:, None], (partial.shape[0], 128))], axis=1
    )
    summed = lax.psum_scatter(packed, "req", scatter_dimension=0, tiled=True)
    mean_square = summed[:, columns] / D
    own_count = k_cache.shape[0]
    slots = k_cache.shape[1]
    local_heads = k_cache.shape[2] // HD
    projected = summed[:, :columns] * lax.rsqrt(mean_square + epsilon)[:, None]
    projected = projected.reshape(own_count, local_heads, GROUP + 2, HD)
    queries = rotate(projected[:, :, :GROUP], lengths).astype(jnp.bfloat16)
    new_keys = rotate(projected[:, :, GROUP], lengths).astype(jnp.bfloat16)
    new_values = projected[:, :, GROUP + 1].astype(jnp.bfloat16)
    cached_keys = k_cache.reshape(own_count, slots, local_heads, HD)
    cached_values = v_cache.reshape(own_count, slots, local_heads, HD)
    factor = HD ** (-0.5)
    attended = attend_padded(
        queries, new_keys, new_values, cached_keys, cached_values, lengths, factor
    )
    flat_rows = attended.reshape(own_count, local_heads * GROUP * HD)
    gathered = lax.all_gather(flat_rows, "req", axis=0, tiled=True)
    output = lax.psum_scatter(
        jnp.dot(gathered, w_out, preferred_element_type=jnp.float32),
        "head",
        scatter_dimension=0,
        tiled=True,
    )
    return (states + output).astype(jnp.bfloat16)


def solution(mesh):
    return jax.shard_map(
        local,
        mesh=mesh,
        in_specs=(
            P("head", "req"),
            P("req"),
            P("req", "head"),
            P("head", "req"),
            P("req", None, "head"),
            P("req", None, "head"),
            P("req"),
        ),
        out_specs=P("head", "req"),
        check_vma=False,
    )
```

```python
import functools

import jax
import jax.numpy as jnp
from jax import lax
from jax.experimental import pallas as pl
from jax.experimental.pallas import tpu as pltpu
from jax.sharding import PartitionSpec as P

D = 8192
GROUP = 8
HD = 128


epsilon = 1e-05
rope_base = 500000.0


def rotate(vectors, positions):
    halfway = vectors.shape[-1] // 2
    frequency = jnp.exp(
        -jnp.log(rope_base) * 2.0 * jnp.arange(halfway, dtype=jnp.float32) / vectors.shape[-1]
    )
    angles = positions.astype(jnp.float32)[:, None] * frequency[None, :]
    target_shape = (angles.shape[0],) + (1,) * (vectors.ndim - 2) + (halfway,)
    cosine = jnp.cos(angles).reshape(target_shape)
    sine_part = jnp.sin(angles).reshape(target_shape)
    first = vectors[..., :halfway]
    second = vectors[..., halfway:]
    return jnp.concatenate(
        [first * cosine - second * sine_part, second * cosine + first * sine_part], axis=-1
    )


def own_part(own_score, running, totals, new_values):
    own_prob = lax.optimization_barrier(
        (jnp.exp(own_score - running) / totals).astype(jnp.bfloat16)
    )
    return own_prob.astype(jnp.float32)[..., None] * new_values.astype(jnp.float32)[:, :, None, :]


def attend_padded(queries, new_keys, new_values, cached_keys, cached_values, lengths, factor):
    slots = cached_keys.shape[1]
    inside = jnp.arange(slots, dtype=jnp.int32)[None, :] < lengths[:, None]
    scores = (
        jnp.einsum("rkgd,rpkd->rkgp", queries, cached_keys, preferred_element_type=jnp.float32)
        * factor
    )
    scores = jnp.where(inside[:, None, None, :], scores, -1e30)
    own_score = (
        jnp.einsum("rkgd,rkd->rkg", queries, new_keys, preferred_element_type=jnp.float32) * factor
    )
    running = jnp.maximum(jnp.max(scores, axis=3), own_score)
    weights = jnp.where(inside[:, None, None, :], jnp.exp(scores - running[..., None]), 0.0)
    totals = jnp.sum(weights, axis=3) + jnp.exp(own_score - running)
    probs = (weights / totals[..., None]).astype(jnp.bfloat16)
    mixed = jnp.einsum("rkgp,rpkd->rkgd", probs, cached_values, preferred_element_type=jnp.float32)
    mixed = mixed + own_part(own_score, running, totals, new_values)
    return mixed.astype(jnp.bfloat16)


def exchange_kernel(axis, n, reduce, x_ref, o_ref, buf, send_sems, recv_sems):
    me = lax.axis_index(axis)
    barrier = pltpu.get_barrier_semaphore()
    for k in range(1, n):
        pl.semaphore_signal(
            barrier, inc=1, device_id={axis: lax.rem(me + k, n)},
            device_id_type=pl.DeviceIdType.MESH,
        )
    pl.semaphore_wait(barrier, n - 1)
    sends = []
    for k in range(1, n):
        peer = lax.rem(me + k, n)
        copy = pltpu.make_async_remote_copy(
            src_ref=x_ref.at[peer],
            dst_ref=buf.at[me],
            send_sem=send_sems.at[k],
            recv_sem=recv_sems.at[k],
            device_id={axis: peer},
            device_id_type=pl.DeviceIdType.MESH,
        )
        copy.start()
        sends.append(copy)
    for k in range(1, n):
        source = lax.rem(me + n - k, n)
        arrival = pltpu.make_async_remote_copy(
            src_ref=x_ref.at[source],
            dst_ref=buf.at[source],
            send_sem=send_sems.at[k],
            recv_sem=recv_sems.at[k],
            device_id={axis: source},
            device_id_type=pl.DeviceIdType.MESH,
        )
        arrival.wait_recv()
    for copy in sends:
        copy.wait_send()
    if reduce:
        total = x_ref[me].astype(jnp.float32)
        for k in range(1, n):
            total = total + buf[lax.rem(me + n - k, n)].astype(jnp.float32)
        o_ref[...] = total.astype(o_ref.dtype)
    else:
        for k in range(1, n):
            source = lax.rem(me + n - k, n)
            o_ref[source] = buf[source]
        o_ref[me] = x_ref[me]


def exchange(x, axis, n, reduce, collective_id):
    out_shape = x.shape[1:] if reduce else x.shape
    return pl.pallas_call(
        functools.partial(exchange_kernel, axis, n, reduce),
        out_shape=jax.ShapeDtypeStruct(out_shape, x.dtype),
        in_specs=[pl.BlockSpec(memory_space=pltpu.VMEM)],
        out_specs=pl.BlockSpec(memory_space=pltpu.VMEM),
        scratch_shapes=[
            pltpu.VMEM(x.shape, x.dtype),
            pltpu.SemaphoreType.DMA((n,)),
            pltpu.SemaphoreType.DMA((n,)),
        ],
        compiler_params=pltpu.CompilerParams(collective_id=collective_id, has_side_effects=True),
    )(x)


def local(req_n, head_n, hidden_in, attn_gain, w_qkv, w_out, k_cache, v_cache, lengths):
    states = hidden_in.astype(jnp.float32)
    rows = hidden_in.shape[0]
    copies = jnp.broadcast_to(hidden_in[None], (head_n,) + hidden_in.shape)
    every_row = exchange(copies, "head", head_n, False, 0)
    every_row = every_row.reshape(head_n * rows, hidden_in.shape[1]).astype(jnp.float32)
    scaled = (every_row * attn_gain.astype(jnp.float32)[None, :]).astype(jnp.bfloat16)
    partial_square = jnp.sum(every_row * every_row, axis=1)
    partial = jnp.dot(scaled, w_qkv, preferred_element_type=jnp.float32)
    columns = partial.shape[1]
    packed = jnp.concatenate(
        [partial, jnp.broadcast_to(partial_square[:, None], (partial.shape[0], 128))], axis=1
    )
    own_count = k_cache.shape[0]
    summed = exchange(packed.reshape(req_n, own_count, columns + 128), "req", req_n, True, 1)
    mean_square = summed[:, columns] / D
    slots = k_cache.shape[1]
    local_heads = k_cache.shape[2] // HD
    projected = summed[:, :columns] * lax.rsqrt(mean_square + epsilon)[:, None]
    projected = projected.reshape(own_count, local_heads, GROUP + 2, HD)
    queries = rotate(projected[:, :, :GROUP], lengths).astype(jnp.bfloat16)
    new_keys = rotate(projected[:, :, GROUP], lengths).astype(jnp.bfloat16)
    new_values = projected[:, :, GROUP + 1].astype(jnp.bfloat16)
    cached_keys = k_cache.reshape(own_count, slots, local_heads, HD)
    cached_values = v_cache.reshape(own_count, slots, local_heads, HD)
    factor = HD ** (-0.5)
    attended = attend_padded(
        queries, new_keys, new_values, cached_keys, cached_values, lengths, factor
    )
    flat_rows = attended.reshape(own_count, local_heads * GROUP * HD)
    gathered = exchange(
        jnp.broadcast_to(flat_rows[None], (req_n,) + flat_rows.shape), "req", req_n, False, 2
    )
    gathered = gathered.reshape(req_n * own_count, flat_rows.shape[1])
    product = jnp.dot(gathered, w_out, preferred_element_type=jnp.float32)
    output = exchange(product.reshape(head_n, rows, product.shape[1]), "head", head_n, True, 3)
    return (states + output).astype(jnp.bfloat16)


def solution(mesh):
    return jax.shard_map(
        functools.partial(local, mesh.shape["req"], mesh.shape["head"]),
        mesh=mesh,
        in_specs=(
            P("head", "req"),
            P("req"),
            P("req", "head"),
            P("head", "req"),
            P("req", None, "head"),
            P("req", None, "head"),
            P("req"),
        ),
        out_specs=P("head", "req"),
        check_vma=False,
    )
```

```python
import functools

import jax
import jax.numpy as jnp
from jax import lax
from jax.experimental import pallas as pl
from jax.experimental.pallas import tpu as pltpu
from jax.sharding import PartitionSpec as P

D = 8192
GROUP = 8
HD = 128


epsilon = 1e-05
rope_base = 500000.0


def rotate(vectors, positions):
    halfway = vectors.shape[-1] // 2
    frequency = jnp.exp(
        -jnp.log(rope_base) * 2.0 * jnp.arange(halfway, dtype=jnp.float32) / vectors.shape[-1]
    )
    angles = positions.astype(jnp.float32)[:, None] * frequency[None, :]
    target_shape = (angles.shape[0],) + (1,) * (vectors.ndim - 2) + (halfway,)
    cosine = jnp.cos(angles).reshape(target_shape)
    sine_part = jnp.sin(angles).reshape(target_shape)
    first = vectors[..., :halfway]
    second = vectors[..., halfway:]
    return jnp.concatenate(
        [first * cosine - second * sine_part, second * cosine + first * sine_part], axis=-1
    )


def own_part(own_score, running, totals, new_values):
    own_prob = lax.optimization_barrier(
        (jnp.exp(own_score - running) / totals).astype(jnp.bfloat16)
    )
    return own_prob.astype(jnp.float32)[..., None] * new_values.astype(jnp.float32)[:, :, None, :]


def attend_padded(queries, new_keys, new_values, cached_keys, cached_values, lengths, factor):
    slots = cached_keys.shape[1]
    inside = jnp.arange(slots, dtype=jnp.int32)[None, :] < lengths[:, None]
    scores = (
        jnp.einsum("rkgd,rpkd->rkgp", queries, cached_keys, preferred_element_type=jnp.float32)
        * factor
    )
    scores = jnp.where(inside[:, None, None, :], scores, -1e30)
    own_score = (
        jnp.einsum("rkgd,rkd->rkg", queries, new_keys, preferred_element_type=jnp.float32) * factor
    )
    running = jnp.maximum(jnp.max(scores, axis=3), own_score)
    weights = jnp.where(inside[:, None, None, :], jnp.exp(scores - running[..., None]), 0.0)
    totals = jnp.sum(weights, axis=3) + jnp.exp(own_score - running)
    probs = (weights / totals[..., None]).astype(jnp.bfloat16)
    mixed = jnp.einsum("rkgp,rpkd->rkgd", probs, cached_values, preferred_element_type=jnp.float32)
    mixed = mixed + own_part(own_score, running, totals, new_values)
    return mixed.astype(jnp.bfloat16)


def greet(peers):
    barrier = pltpu.get_barrier_semaphore()
    for axis, me, n in peers:
        for k in range(1, n):
            pl.semaphore_signal(
                barrier, inc=1, device_id={axis: lax.rem(me + k, n)},
                device_id_type=pl.DeviceIdType.MESH,
            )
    pl.semaphore_wait(barrier, sum(n - 1 for _, _, n in peers))


def send_all(axis, me, n, block_of, dst, send_sems, recv_sems):
    sends = []
    for k in range(1, n):
        peer = lax.rem(me + k, n)
        copy = pltpu.make_async_remote_copy(
            src_ref=block_of(peer),
            dst_ref=dst.at[me],
            send_sem=send_sems.at[k],
            recv_sem=recv_sems.at[k],
            device_id={axis: peer},
            device_id_type=pl.DeviceIdType.MESH,
        )
        copy.start()
        sends.append(copy)
    return sends


def receive_all(axis, me, n, block_of, dst, send_sems, recv_sems, sends):
    for k in range(1, n):
        source = lax.rem(me + n - k, n)
        arrival = pltpu.make_async_remote_copy(
            src_ref=block_of(source),
            dst_ref=dst.at[source],
            send_sem=send_sems.at[k],
            recv_sem=recv_sems.at[k],
            device_id={axis: source},
            device_id_type=pl.DeviceIdType.MESH,
        )
        arrival.wait_recv()
    for copy in sends:
        copy.wait_send()


def project_kernel(req_n, head_n, x_ref, gain_ref, w_ref, o_ref,
                   rows_buf, part, sums_buf, sems):
    me_head = lax.axis_index("head")
    me_req = lax.axis_index("req")
    greet((("head", me_head, head_n), ("req", me_req, req_n)))
    own = lambda peer: x_ref
    sends = send_all("head", me_head, head_n, own, rows_buf, sems.at[0], sems.at[1])
    receive_all("head", me_head, head_n, own, rows_buf, sems.at[0], sems.at[1], sends)
    rows_buf[me_head] = x_ref[...]
    block_rows = x_ref.shape[0]
    states = rows_buf[...].reshape(head_n * block_rows, x_ref.shape[1]).astype(jnp.float32)
    scaled = (states * gain_ref[...].astype(jnp.float32)).astype(jnp.bfloat16)
    columns = w_ref.shape[1]
    part[:, :columns] = jnp.dot(scaled, w_ref[...], preferred_element_type=jnp.float32)
    square = jnp.sum(states * states, axis=1, keepdims=True)
    part[:, columns:] = jnp.broadcast_to(square, (square.shape[0], part.shape[1] - columns))
    count = o_ref.shape[0]
    chunk = lambda peer: part.at[pl.ds(pl.multiple_of(peer * count, count), count)]
    sends = send_all("req", me_req, req_n, chunk, sums_buf, sems.at[2], sems.at[3])
    receive_all("req", me_req, req_n, chunk, sums_buf, sems.at[2], sems.at[3], sends)
    total = part[pl.ds(pl.multiple_of(me_req * count, count), count), :]
    for k in range(1, req_n):
        total = total + sums_buf[lax.rem(me_req + req_n - k, req_n)]
    o_ref[...] = total


def project(hidden_in, gain, w_qkv, req_n, head_n, count):
    rows, width = hidden_in.shape
    columns = w_qkv.shape[1] + 128
    return pl.pallas_call(
        functools.partial(project_kernel, req_n, head_n),
        out_shape=jax.ShapeDtypeStruct((count, columns), jnp.float32),
        in_specs=[pl.BlockSpec(memory_space=pltpu.VMEM)] * 3,
        out_specs=pl.BlockSpec(memory_space=pltpu.VMEM),
        scratch_shapes=[
            pltpu.VMEM((head_n, rows, width), hidden_in.dtype),
            pltpu.VMEM((req_n * count, columns), jnp.float32),
            pltpu.VMEM((req_n, count, columns), jnp.float32),
            pltpu.SemaphoreType.DMA((4, max(req_n, head_n))),
        ],
        compiler_params=pltpu.CompilerParams(collective_id=0, has_side_effects=True),
    )(hidden_in, gain.reshape(1, width), w_qkv)


def output_kernel(req_n, head_n, a_ref, w_ref, s_ref, o_ref, att_buf, part, sums_buf, sems):
    me_head = lax.axis_index("head")
    me_req = lax.axis_index("req")
    greet((("req", me_req, req_n), ("head", me_head, head_n)))
    own = lambda peer: a_ref
    sends = send_all("req", me_req, req_n, own, att_buf, sems.at[0], sems.at[1])
    receive_all("req", me_req, req_n, own, att_buf, sems.at[0], sems.at[1], sends)
    att_buf[me_req] = a_ref[...]
    every = jnp.concatenate(
        [att_buf[s].astype(jnp.float32) for s in range(req_n)], axis=0
    ).astype(jnp.bfloat16)
    part[...] = jnp.dot(every, w_ref[...], preferred_element_type=jnp.float32)
    rows = o_ref.shape[0]
    chunk = lambda peer: part.at[pl.ds(pl.multiple_of(peer * rows, rows), rows)]
    sends = send_all("head", me_head, head_n, chunk, sums_buf, sems.at[2], sems.at[3])
    receive_all("head", me_head, head_n, chunk, sums_buf, sems.at[2], sems.at[3], sends)
    total = part[pl.ds(pl.multiple_of(me_head * rows, rows), rows), :]
    for k in range(1, head_n):
        total = total + sums_buf[lax.rem(me_head + head_n - k, head_n)]
    o_ref[...] = (s_ref[...].astype(jnp.float32) + total).astype(o_ref.dtype)


def output_block(attended, w_out, hidden_in, req_n, head_n):
    count, width = attended.shape
    rows, columns = hidden_in.shape
    return pl.pallas_call(
        functools.partial(output_kernel, req_n, head_n),
        out_shape=jax.ShapeDtypeStruct((rows, columns), hidden_in.dtype),
        in_specs=[pl.BlockSpec(memory_space=pltpu.VMEM)] * 3,
        out_specs=pl.BlockSpec(memory_space=pltpu.VMEM),
        scratch_shapes=[
            pltpu.VMEM((req_n, count, width), attended.dtype),
            pltpu.VMEM((head_n * rows, columns), jnp.float32),
            pltpu.VMEM((head_n, rows, columns), jnp.float32),
            pltpu.SemaphoreType.DMA((4, max(req_n, head_n))),
        ],
        compiler_params=pltpu.CompilerParams(collective_id=1, has_side_effects=True),
    )(attended, w_out, hidden_in)


def local(req_n, head_n, hidden_in, attn_gain, w_qkv, w_out, k_cache, v_cache, lengths):
    own_count = k_cache.shape[0]
    summed = project(hidden_in, attn_gain, w_qkv, req_n, head_n, own_count)
    columns = w_qkv.shape[1]
    mean_square = summed[:, columns] / D
    slots = k_cache.shape[1]
    local_heads = k_cache.shape[2] // HD
    projected = summed[:, :columns] * lax.rsqrt(mean_square + epsilon)[:, None]
    projected = projected.reshape(own_count, local_heads, GROUP + 2, HD)
    queries = rotate(projected[:, :, :GROUP], lengths).astype(jnp.bfloat16)
    new_keys = rotate(projected[:, :, GROUP], lengths).astype(jnp.bfloat16)
    new_values = projected[:, :, GROUP + 1].astype(jnp.bfloat16)
    cached_keys = k_cache.reshape(own_count, slots, local_heads, HD)
    cached_values = v_cache.reshape(own_count, slots, local_heads, HD)
    factor = HD ** (-0.5)
    attended = attend_padded(
        queries, new_keys, new_values, cached_keys, cached_values, lengths, factor
    )
    flat_rows = attended.reshape(own_count, local_heads * GROUP * HD)
    return output_block(flat_rows, w_out, hidden_in, req_n, head_n)


def solution(mesh):
    return jax.shard_map(
        functools.partial(local, mesh.shape["req"], mesh.shape["head"]),
        mesh=mesh,
        in_specs=(
            P("head", "req"),
            P("req"),
            P("req", "head"),
            P("head", "req"),
            P("req", None, "head"),
            P("req", None, "head"),
            P("req"),
        ),
        out_specs=P("head", "req"),
        check_vma=False,
    )
```

```python
import functools

import jax
import jax.numpy as jnp
from jax import lax
from jax.experimental import pallas as pl
from jax.experimental.pallas import tpu as pltpu
from jax.sharding import PartitionSpec as P

D = 8192
GROUP = 8
HD = 128


epsilon = 1e-05
rope_base = 500000.0


def rotate(vectors, positions):
    halfway = vectors.shape[-1] // 2
    frequency = jnp.exp(
        -jnp.log(rope_base) * 2.0 * jnp.arange(halfway, dtype=jnp.float32) / vectors.shape[-1]
    )
    angles = positions.astype(jnp.float32)[:, None] * frequency[None, :]
    target_shape = (angles.shape[0],) + (1,) * (vectors.ndim - 2) + (halfway,)
    cosine = jnp.cos(angles).reshape(target_shape)
    sine_part = jnp.sin(angles).reshape(target_shape)
    first = vectors[..., :halfway]
    second = vectors[..., halfway:]
    return jnp.concatenate(
        [first * cosine - second * sine_part, second * cosine + first * sine_part], axis=-1
    )


def own_part(own_score, running, totals, new_values):
    own_prob = lax.optimization_barrier(
        (jnp.exp(own_score - running) / totals).astype(jnp.bfloat16)
    )
    return own_prob.astype(jnp.float32)[..., None] * new_values.astype(jnp.float32)[:, :, None, :]


def attend_padded(queries, new_keys, new_values, cached_keys, cached_values, lengths, factor):
    slots = cached_keys.shape[1]
    inside = jnp.arange(slots, dtype=jnp.int32)[None, :] < lengths[:, None]
    scores = (
        jnp.einsum("rkgd,rpkd->rkgp", queries, cached_keys, preferred_element_type=jnp.float32)
        * factor
    )
    scores = jnp.where(inside[:, None, None, :], scores, -1e30)
    own_score = (
        jnp.einsum("rkgd,rkd->rkg", queries, new_keys, preferred_element_type=jnp.float32) * factor
    )
    running = jnp.maximum(jnp.max(scores, axis=3), own_score)
    weights = jnp.where(inside[:, None, None, :], jnp.exp(scores - running[..., None]), 0.0)
    totals = jnp.sum(weights, axis=3) + jnp.exp(own_score - running)
    probs = (weights / totals[..., None]).astype(jnp.bfloat16)
    mixed = jnp.einsum("rkgp,rpkd->rkgd", probs, cached_values, preferred_element_type=jnp.float32)
    mixed = mixed + own_part(own_score, running, totals, new_values)
    return mixed.astype(jnp.bfloat16)


def greet(peers):
    barrier = pltpu.get_barrier_semaphore()
    for axis, me, n in peers:
        for k in range(1, n):
            pl.semaphore_signal(
                barrier, inc=1, device_id={axis: lax.rem(me + k, n)},
                device_id_type=pl.DeviceIdType.MESH,
            )
    pl.semaphore_wait(barrier, sum(n - 1 for _, _, n in peers))


def send_all(axis, me, n, block_of, dst, send_sems, recv_sems):
    sends = []
    for k in range(1, n):
        peer = lax.rem(me + k, n)
        copy = pltpu.make_async_remote_copy(
            src_ref=block_of(peer),
            dst_ref=dst.at[me],
            send_sem=send_sems.at[k],
            recv_sem=recv_sems.at[k],
            device_id={axis: peer},
            device_id_type=pl.DeviceIdType.MESH,
        )
        copy.start()
        sends.append(copy)
    return sends


def receive_all(axis, me, n, block_of, dst, send_sems, recv_sems, sends):
    for k in range(1, n):
        source = lax.rem(me + n - k, n)
        arrival = pltpu.make_async_remote_copy(
            src_ref=block_of(source),
            dst_ref=dst.at[source],
            send_sem=send_sems.at[k],
            recv_sem=recv_sems.at[k],
            device_id={axis: source},
            device_id_type=pl.DeviceIdType.MESH,
        )
        arrival.wait_recv()
    for copy in sends:
        copy.wait_send()


def project_kernel(req_n, head_n, x_ref, gain_ref, w_ref, o_ref,
                   rows_buf, part, sums_buf, sems):
    me_head = lax.axis_index("head")
    me_req = lax.axis_index("req")
    greet((("head", me_head, head_n), ("req", me_req, req_n)))
    own = lambda peer: x_ref
    sends = send_all("head", me_head, head_n, own, rows_buf, sems.at[0], sems.at[1])
    receive_all("head", me_head, head_n, own, rows_buf, sems.at[0], sems.at[1], sends)
    rows_buf[me_head] = x_ref[...]
    block_rows = x_ref.shape[0]
    states = rows_buf[...].reshape(head_n * block_rows, x_ref.shape[1]).astype(jnp.float32)
    scaled = (states * gain_ref[...].astype(jnp.float32)[None, :]).astype(jnp.bfloat16)
    columns = w_ref.shape[1]
    part[:, :columns] = jnp.dot(scaled, w_ref[...], preferred_element_type=jnp.float32)
    square = jnp.sum(states * states, axis=1, keepdims=True)
    part[:, columns:] = jnp.broadcast_to(square, (square.shape[0], part.shape[1] - columns))
    count = o_ref.shape[0]
    chunk = lambda peer: part.at[pl.ds(pl.multiple_of(peer * count, count), count)]
    sends = send_all("req", me_req, req_n, chunk, sums_buf, sems.at[2], sems.at[3])
    receive_all("req", me_req, req_n, chunk, sums_buf, sems.at[2], sems.at[3], sends)
    total = part[pl.ds(pl.multiple_of(me_req * count, count), count), :]
    for k in range(1, req_n):
        total = total + sums_buf[lax.rem(me_req + req_n - k, req_n)]
    mean_square = total[:, columns:columns + 1] / D
    o_ref[...] = total[:, :columns] * lax.rsqrt(mean_square + epsilon)


def project(hidden_in, gain, w_qkv, req_n, head_n, count):
    rows, width = hidden_in.shape
    columns = w_qkv.shape[1] + 128
    return pl.pallas_call(
        functools.partial(project_kernel, req_n, head_n),
        out_shape=jax.ShapeDtypeStruct((count, w_qkv.shape[1]), jnp.float32),
        in_specs=[pl.BlockSpec(memory_space=pltpu.VMEM)] * 3,
        out_specs=pl.BlockSpec(memory_space=pltpu.VMEM),
        scratch_shapes=[
            pltpu.VMEM((head_n, rows, width), hidden_in.dtype),
            pltpu.VMEM((req_n * count, columns), jnp.float32),
            pltpu.VMEM((req_n, count, columns), jnp.float32),
            pltpu.SemaphoreType.DMA((4, max(req_n, head_n))),
        ],
        compiler_params=pltpu.CompilerParams(collective_id=0, has_side_effects=True),
    )(hidden_in, gain, w_qkv)


def output_kernel(req_n, head_n, a_ref, w_ref, s_ref, o_ref, att_buf, part, sums_buf, sems):
    me_head = lax.axis_index("head")
    me_req = lax.axis_index("req")
    greet((("req", me_req, req_n), ("head", me_head, head_n)))
    own = lambda peer: a_ref
    sends = send_all("req", me_req, req_n, own, att_buf, sems.at[0], sems.at[1])
    receive_all("req", me_req, req_n, own, att_buf, sems.at[0], sems.at[1], sends)
    att_buf[me_req] = a_ref[...]
    every = jnp.concatenate(
        [att_buf[s].astype(jnp.float32) for s in range(req_n)], axis=0
    ).astype(jnp.bfloat16)
    part[...] = jnp.dot(every, w_ref[...], preferred_element_type=jnp.float32)
    rows = o_ref.shape[0]
    chunk = lambda peer: part.at[pl.ds(pl.multiple_of(peer * rows, rows), rows)]
    sends = send_all("head", me_head, head_n, chunk, sums_buf, sems.at[2], sems.at[3])
    receive_all("head", me_head, head_n, chunk, sums_buf, sems.at[2], sems.at[3], sends)
    total = part[pl.ds(pl.multiple_of(me_head * rows, rows), rows), :]
    for k in range(1, head_n):
        total = total + sums_buf[lax.rem(me_head + head_n - k, head_n)]
    o_ref[...] = (s_ref[...].astype(jnp.float32) + total).astype(o_ref.dtype)


def output_block(attended, w_out, hidden_in, req_n, head_n):
    count, width = attended.shape
    rows, columns = hidden_in.shape
    return pl.pallas_call(
        functools.partial(output_kernel, req_n, head_n),
        out_shape=jax.ShapeDtypeStruct((rows, columns), hidden_in.dtype),
        in_specs=[pl.BlockSpec(memory_space=pltpu.VMEM)] * 3,
        out_specs=pl.BlockSpec(memory_space=pltpu.VMEM),
        scratch_shapes=[
            pltpu.VMEM((req_n, count, width), attended.dtype),
            pltpu.VMEM((head_n * rows, columns), jnp.float32),
            pltpu.VMEM((head_n, rows, columns), jnp.float32),
            pltpu.SemaphoreType.DMA((4, max(req_n, head_n))),
        ],
        compiler_params=pltpu.CompilerParams(collective_id=1, has_side_effects=True),
    )(attended, w_out, hidden_in)


def local(req_n, head_n, hidden_in, attn_gain, w_qkv, w_out, k_cache, v_cache, lengths):
    own_count = k_cache.shape[0]
    projected = project(hidden_in, attn_gain, w_qkv, req_n, head_n, own_count)
    slots = k_cache.shape[1]
    local_heads = k_cache.shape[2] // HD
    projected = projected.reshape(own_count, local_heads, GROUP + 2, HD)
    queries = rotate(projected[:, :, :GROUP], lengths).astype(jnp.bfloat16)
    new_keys = rotate(projected[:, :, GROUP], lengths).astype(jnp.bfloat16)
    new_values = projected[:, :, GROUP + 1].astype(jnp.bfloat16)
    cached_keys = k_cache.reshape(own_count, slots, local_heads, HD)
    cached_values = v_cache.reshape(own_count, slots, local_heads, HD)
    factor = HD ** (-0.5)
    attended = attend_padded(
        queries, new_keys, new_values, cached_keys, cached_values, lengths, factor
    )
    flat_rows = attended.reshape(own_count, local_heads * GROUP * HD)
    return output_block(flat_rows, w_out, hidden_in, req_n, head_n)


def solution(mesh):
    return jax.shard_map(
        functools.partial(local, mesh.shape["req"], mesh.shape["head"]),
        mesh=mesh,
        in_specs=(
            P("head", "req"),
            P("req"),
            P("req", "head"),
            P("head", "req"),
            P("req", None, "head"),
            P("req", None, "head"),
            P("req"),
        ),
        out_specs=P("head", "req"),
        check_vma=False,
    )
```

```python
import functools

import jax
import jax.numpy as jnp
from jax import lax
from jax.experimental import pallas as pl
from jax.experimental.pallas import tpu as pltpu
from jax.sharding import PartitionSpec as P

D = 8192
GROUP = 8
HD = 128


epsilon = 1e-05
rope_base = 500000.0


def rotate(vectors, positions):
    halfway = vectors.shape[-1] // 2
    frequency = jnp.exp(
        -jnp.log(rope_base) * 2.0 * jnp.arange(halfway, dtype=jnp.float32) / vectors.shape[-1]
    )
    angles = positions.astype(jnp.float32)[:, None] * frequency[None, :]
    target_shape = (angles.shape[0],) + (1,) * (vectors.ndim - 2) + (halfway,)
    cosine = jnp.cos(angles).reshape(target_shape)
    sine_part = jnp.sin(angles).reshape(target_shape)
    first = vectors[..., :halfway]
    second = vectors[..., halfway:]
    return jnp.concatenate(
        [first * cosine - second * sine_part, second * cosine + first * sine_part], axis=-1
    )


def own_part(own_score, running, totals, new_values):
    own_prob = lax.optimization_barrier(
        (jnp.exp(own_score - running) / totals).astype(jnp.bfloat16)
    )
    return own_prob.astype(jnp.float32)[..., None] * new_values.astype(jnp.float32)[:, :, None, :]


def attend_padded(queries, new_keys, new_values, cached_keys, cached_values, lengths, factor):
    slots = cached_keys.shape[1]
    inside = jnp.arange(slots, dtype=jnp.int32)[None, :] < lengths[:, None]
    scores = (
        jnp.einsum("rkgd,rpkd->rkgp", queries, cached_keys, preferred_element_type=jnp.float32)
        * factor
    )
    scores = jnp.where(inside[:, None, None, :], scores, -1e30)
    own_score = (
        jnp.einsum("rkgd,rkd->rkg", queries, new_keys, preferred_element_type=jnp.float32) * factor
    )
    running = jnp.maximum(jnp.max(scores, axis=3), own_score)
    weights = jnp.where(inside[:, None, None, :], jnp.exp(scores - running[..., None]), 0.0)
    totals = jnp.sum(weights, axis=3) + jnp.exp(own_score - running)
    probs = (weights / totals[..., None]).astype(jnp.bfloat16)
    mixed = jnp.einsum("rkgp,rpkd->rkgd", probs, cached_values, preferred_element_type=jnp.float32)
    mixed = mixed + own_part(own_score, running, totals, new_values)
    return mixed.astype(jnp.bfloat16)


def greet(peers):
    barrier = pltpu.get_barrier_semaphore()
    for axis, me, n in peers:
        for k in range(1, n):
            pl.semaphore_signal(
                barrier, inc=1, device_id={axis: lax.rem(me + k, n)},
                device_id_type=pl.DeviceIdType.MESH,
            )
    pl.semaphore_wait(barrier, sum(n - 1 for _, _, n in peers))


def send_all(axis, me, n, block_of, dst, send_sems, recv_sems):
    sends = []
    for k in range(1, n):
        peer = lax.rem(me + k, n)
        copy = pltpu.make_async_remote_copy(
            src_ref=block_of(peer),
            dst_ref=dst.at[me],
            send_sem=send_sems.at[k],
            recv_sem=recv_sems.at[k],
            device_id={axis: peer},
            device_id_type=pl.DeviceIdType.MESH,
        )
        copy.start()
        sends.append(copy)
    return sends


def receive_all(axis, me, n, block_of, dst, send_sems, recv_sems, sends):
    for k in range(1, n):
        source = lax.rem(me + n - k, n)
        arrival = pltpu.make_async_remote_copy(
            src_ref=block_of(source),
            dst_ref=dst.at[source],
            send_sem=send_sems.at[k],
            recv_sem=recv_sems.at[k],
            device_id={axis: source},
            device_id_type=pl.DeviceIdType.MESH,
        )
        arrival.wait_recv()
    for copy in sends:
        copy.wait_send()


def project_kernel(req_n, head_n, x_ref, gain_ref, w_ref, o_ref,
                   rows_buf, part, pair_buf, mixed, sums_buf, sems):
    me_head = lax.axis_index("head")
    me_req = lax.axis_index("req")
    chips = req_n // 2
    me_core = lax.rem(me_req, 2)
    me_chip = me_req // 2
    partner = me_req + 1 - 2 * me_core
    barrier = pltpu.get_barrier_semaphore()
    for k in range(1, head_n):
        pl.semaphore_signal(
            barrier, inc=1, device_id={"head": lax.rem(me_head + k, head_n)},
            device_id_type=pl.DeviceIdType.MESH,
        )
    pl.semaphore_signal(
        barrier, inc=1, device_id={"req": partner}, device_id_type=pl.DeviceIdType.MESH
    )
    for k in range(1, chips):
        pl.semaphore_signal(
            barrier, inc=1, device_id={"req": lax.rem(me_chip + k, chips) * 2 + me_core},
            device_id_type=pl.DeviceIdType.MESH,
        )
    pl.semaphore_wait(barrier, head_n - 1 + chips)
    own = lambda peer: x_ref
    sends = send_all("head", me_head, head_n, own, rows_buf, sems.at[0], sems.at[1])
    receive_all("head", me_head, head_n, own, rows_buf, sems.at[0], sems.at[1], sends)
    rows_buf[me_head] = x_ref[...]
    block_rows = x_ref.shape[0]
    states = rows_buf[...].reshape(head_n * block_rows, x_ref.shape[1]).astype(jnp.float32)
    scaled = (states * gain_ref[...].astype(jnp.float32)[None, :]).astype(jnp.bfloat16)
    columns = w_ref.shape[1]
    square = jnp.sum(states * states, axis=1, keepdims=True)
    packed = jnp.concatenate(
        [jnp.dot(scaled, w_ref[...], preferred_element_type=jnp.float32),
         jnp.broadcast_to(square, (square.shape[0], part.shape[-1] - columns))],
        axis=1,
    )
    count = o_ref.shape[0]
    packed = packed.reshape(chips, 2, count, part.shape[-1])
    part[0] = packed[:, 0]
    part[1] = packed[:, 1]
    pair = pltpu.make_async_remote_copy(
        src_ref=part.at[1 - me_core],
        dst_ref=pair_buf,
        send_sem=sems.at[2, 0],
        recv_sem=sems.at[3, 0],
        device_id={"req": partner},
        device_id_type=pl.DeviceIdType.MESH,
    )
    pair.start()
    pair.wait()
    mixed[...] = part[me_core] + pair_buf[...]
    sends = []
    for k in range(1, chips):
        chip = lax.rem(me_chip + k, chips)
        copy = pltpu.make_async_remote_copy(
            src_ref=mixed.at[chip],
            dst_ref=sums_buf.at[me_chip],
            send_sem=sems.at[2, k],
            recv_sem=sems.at[3, k],
            device_id={"req": chip * 2 + me_core},
            device_id_type=pl.DeviceIdType.MESH,
        )
        copy.start()
        sends.append(copy)
    for k in range(1, chips):
        chip = lax.rem(me_chip + chips - k, chips)
        arrival = pltpu.make_async_remote_copy(
            src_ref=mixed.at[chip],
            dst_ref=sums_buf.at[chip],
            send_sem=sems.at[2, k],
            recv_sem=sems.at[3, k],
            device_id={"req": chip * 2 + me_core},
            device_id_type=pl.DeviceIdType.MESH,
        )
        arrival.wait_recv()
    for copy in sends:
        copy.wait_send()
    total = mixed[me_chip]
    for k in range(1, chips):
        total = total + sums_buf[lax.rem(me_chip + chips - k, chips)]
    mean_square = total[:, columns:columns + 1] / D
    o_ref[...] = total[:, :columns] * lax.rsqrt(mean_square + epsilon)


def project(hidden_in, gain, w_qkv, req_n, head_n, count):
    rows, width = hidden_in.shape
    columns = w_qkv.shape[1] + 128
    return pl.pallas_call(
        functools.partial(project_kernel, req_n, head_n),
        out_shape=jax.ShapeDtypeStruct((count, w_qkv.shape[1]), jnp.float32),
        in_specs=[pl.BlockSpec(memory_space=pltpu.VMEM)] * 3,
        out_specs=pl.BlockSpec(memory_space=pltpu.VMEM),
        scratch_shapes=[
            pltpu.VMEM((head_n, rows, width), hidden_in.dtype),
            pltpu.VMEM((2, req_n // 2, count, columns), jnp.float32),
            pltpu.VMEM((req_n // 2, count, columns), jnp.float32),
            pltpu.VMEM((req_n // 2, count, columns), jnp.float32),
            pltpu.VMEM((req_n // 2, count, columns), jnp.float32),
            pltpu.SemaphoreType.DMA((4, max(req_n, head_n))),
        ],
        compiler_params=pltpu.CompilerParams(collective_id=0, has_side_effects=True),
    )(hidden_in, gain, w_qkv)


def output_kernel(req_n, head_n, a_ref, w_ref, s_ref, o_ref, att_buf, part, sums_buf, sems):
    me_head = lax.axis_index("head")
    me_req = lax.axis_index("req")
    greet((("req", me_req, req_n), ("head", me_head, head_n)))
    own = lambda peer: a_ref
    sends = send_all("req", me_req, req_n, own, att_buf, sems.at[0], sems.at[1])
    receive_all("req", me_req, req_n, own, att_buf, sems.at[0], sems.at[1], sends)
    att_buf[me_req] = a_ref[...]
    every = jnp.concatenate(
        [att_buf[s].astype(jnp.float32) for s in range(req_n)], axis=0
    ).astype(jnp.bfloat16)
    part[...] = jnp.dot(every, w_ref[...], preferred_element_type=jnp.float32)
    rows = o_ref.shape[0]
    chunk = lambda peer: part.at[pl.ds(pl.multiple_of(peer * rows, rows), rows)]
    sends = send_all("head", me_head, head_n, chunk, sums_buf, sems.at[2], sems.at[3])
    receive_all("head", me_head, head_n, chunk, sums_buf, sems.at[2], sems.at[3], sends)
    total = part[pl.ds(pl.multiple_of(me_head * rows, rows), rows), :]
    for k in range(1, head_n):
        total = total + sums_buf[lax.rem(me_head + head_n - k, head_n)]
    o_ref[...] = (s_ref[...].astype(jnp.float32) + total).astype(o_ref.dtype)


def output_block(attended, w_out, hidden_in, req_n, head_n):
    count, width = attended.shape
    rows, columns = hidden_in.shape
    return pl.pallas_call(
        functools.partial(output_kernel, req_n, head_n),
        out_shape=jax.ShapeDtypeStruct((rows, columns), hidden_in.dtype),
        in_specs=[pl.BlockSpec(memory_space=pltpu.VMEM)] * 3,
        out_specs=pl.BlockSpec(memory_space=pltpu.VMEM),
        scratch_shapes=[
            pltpu.VMEM((req_n, count, width), attended.dtype),
            pltpu.VMEM((head_n * rows, columns), jnp.float32),
            pltpu.VMEM((head_n, rows, columns), jnp.float32),
            pltpu.SemaphoreType.DMA((4, max(req_n, head_n))),
        ],
        compiler_params=pltpu.CompilerParams(collective_id=1, has_side_effects=True),
    )(attended, w_out, hidden_in)


def local(req_n, head_n, hidden_in, attn_gain, w_qkv, w_out, k_cache, v_cache, lengths):
    own_count = k_cache.shape[0]
    projected = project(hidden_in, attn_gain, w_qkv, req_n, head_n, own_count)
    slots = k_cache.shape[1]
    local_heads = k_cache.shape[2] // HD
    projected = projected.reshape(own_count, local_heads, GROUP + 2, HD)
    queries = rotate(projected[:, :, :GROUP], lengths).astype(jnp.bfloat16)
    new_keys = rotate(projected[:, :, GROUP], lengths).astype(jnp.bfloat16)
    new_values = projected[:, :, GROUP + 1].astype(jnp.bfloat16)
    cached_keys = k_cache.reshape(own_count, slots, local_heads, HD)
    cached_values = v_cache.reshape(own_count, slots, local_heads, HD)
    factor = HD ** (-0.5)
    attended = attend_padded(
        queries, new_keys, new_values, cached_keys, cached_values, lengths, factor
    )
    flat_rows = attended.reshape(own_count, local_heads * GROUP * HD)
    return output_block(flat_rows, w_out, hidden_in, req_n, head_n)


def solution(mesh):
    return jax.shard_map(
        functools.partial(local, mesh.shape["req"], mesh.shape["head"]),
        mesh=mesh,
        in_specs=(
            P("head", "req"),
            P("req"),
            P("req", "head"),
            P("head", "req"),
            P("req", None, "head"),
            P("req", None, "head"),
            P("req"),
        ),
        out_specs=P("head", "req"),
        check_vma=False,
    )
```

```python
import functools

import jax
import jax.numpy as jnp
from jax import lax
from jax.experimental import pallas as pl
from jax.experimental.pallas import tpu as pltpu
from jax.sharding import PartitionSpec as P

D = 8192
GROUP = 8
HD = 128


epsilon = 1e-05
rope_base = 500000.0


def rotate(vectors, positions):
    halfway = vectors.shape[-1] // 2
    frequency = jnp.exp(
        -jnp.log(rope_base) * 2.0 * jnp.arange(halfway, dtype=jnp.float32) / vectors.shape[-1]
    )
    angles = positions.astype(jnp.float32)[:, None] * frequency[None, :]
    target_shape = (angles.shape[0],) + (1,) * (vectors.ndim - 2) + (halfway,)
    cosine = jnp.cos(angles).reshape(target_shape)
    sine_part = jnp.sin(angles).reshape(target_shape)
    first = vectors[..., :halfway]
    second = vectors[..., halfway:]
    return jnp.concatenate(
        [first * cosine - second * sine_part, second * cosine + first * sine_part], axis=-1
    )


def own_part(own_score, running, totals, new_values):
    own_prob = lax.optimization_barrier(
        (jnp.exp(own_score - running) / totals).astype(jnp.bfloat16)
    )
    return own_prob.astype(jnp.float32)[..., None] * new_values.astype(jnp.float32)[:, :, None, :]


def attend_padded(queries, new_keys, new_values, cached_keys, cached_values, lengths, factor):
    slots = cached_keys.shape[1]
    inside = jnp.arange(slots, dtype=jnp.int32)[None, :] < lengths[:, None]
    scores = (
        jnp.einsum("rkgd,rpkd->rkgp", queries, cached_keys, preferred_element_type=jnp.float32)
        * factor
    )
    scores = jnp.where(inside[:, None, None, :], scores, -1e30)
    own_score = (
        jnp.einsum("rkgd,rkd->rkg", queries, new_keys, preferred_element_type=jnp.float32) * factor
    )
    running = jnp.maximum(jnp.max(scores, axis=3), own_score)
    weights = jnp.where(inside[:, None, None, :], jnp.exp(scores - running[..., None]), 0.0)
    totals = jnp.sum(weights, axis=3) + jnp.exp(own_score - running)
    probs = (weights / totals[..., None]).astype(jnp.bfloat16)
    mixed = jnp.einsum("rkgp,rpkd->rkgd", probs, cached_values, preferred_element_type=jnp.float32)
    mixed = mixed + own_part(own_score, running, totals, new_values)
    return mixed.astype(jnp.bfloat16)


def greet(peers):
    barrier = pltpu.get_barrier_semaphore()
    for axis, me, n in peers:
        for k in range(1, n):
            pl.semaphore_signal(
                barrier, inc=1, device_id={axis: lax.rem(me + k, n)},
                device_id_type=pl.DeviceIdType.MESH,
            )
    pl.semaphore_wait(barrier, sum(n - 1 for _, _, n in peers))


def send_all(axis, me, n, block_of, dst, send_sems, recv_sems):
    sends = []
    for k in range(1, n):
        peer = lax.rem(me + k, n)
        copy = pltpu.make_async_remote_copy(
            src_ref=block_of(peer),
            dst_ref=dst.at[me],
            send_sem=send_sems.at[k],
            recv_sem=recv_sems.at[k],
            device_id={axis: peer},
            device_id_type=pl.DeviceIdType.MESH,
        )
        copy.start()
        sends.append(copy)
    return sends


def receive_all(axis, me, n, block_of, dst, send_sems, recv_sems, sends):
    for k in range(1, n):
        source = lax.rem(me + n - k, n)
        arrival = pltpu.make_async_remote_copy(
            src_ref=block_of(source),
            dst_ref=dst.at[source],
            send_sem=send_sems.at[k],
            recv_sem=recv_sems.at[k],
            device_id={axis: source},
            device_id_type=pl.DeviceIdType.MESH,
        )
        arrival.wait_recv()
    for copy in sends:
        copy.wait_send()


def project_kernel(req_n, head_n, x_ref, gain_ref, w_ref, o_ref,
                   rows_buf, part, pair_buf, mixed, sums_buf, sems):
    me_head = lax.axis_index("head")
    me_req = lax.axis_index("req")
    chips = req_n // 2
    me_core = lax.rem(me_req, 2)
    me_chip = me_req // 2
    partner = me_req + 1 - 2 * me_core
    own = lambda peer: x_ref
    sends = send_all("head", me_head, head_n, own, rows_buf, sems.at[0], sems.at[1])
    receive_all("head", me_head, head_n, own, rows_buf, sems.at[0], sems.at[1], sends)
    rows_buf[me_head] = x_ref[...]
    block_rows = x_ref.shape[0]
    states = rows_buf[...].reshape(head_n * block_rows, x_ref.shape[1]).astype(jnp.float32)
    scaled = (states * gain_ref[...].astype(jnp.float32)[None, :]).astype(jnp.bfloat16)
    columns = w_ref.shape[1]
    square = jnp.sum(states * states, axis=1, keepdims=True)
    packed = jnp.concatenate(
        [jnp.dot(scaled, w_ref[...], preferred_element_type=jnp.float32),
         jnp.broadcast_to(square, (square.shape[0], part.shape[-1] - columns))],
        axis=1,
    )
    count = o_ref.shape[0]
    packed = packed.reshape(chips, 2, count, part.shape[-1])
    part[0] = packed[:, 0]
    part[1] = packed[:, 1]
    pair = pltpu.make_async_remote_copy(
        src_ref=part.at[1 - me_core],
        dst_ref=pair_buf,
        send_sem=sems.at[2, 0],
        recv_sem=sems.at[3, 0],
        device_id={"req": partner},
        device_id_type=pl.DeviceIdType.MESH,
    )
    pair.start()
    pair.wait()
    mixed[...] = part[me_core] + pair_buf[...]
    sends = []
    for k in range(1, chips):
        chip = lax.rem(me_chip + k, chips)
        copy = pltpu.make_async_remote_copy(
            src_ref=mixed.at[chip],
            dst_ref=sums_buf.at[me_chip],
            send_sem=sems.at[2, k],
            recv_sem=sems.at[3, k],
            device_id={"req": chip * 2 + me_core},
            device_id_type=pl.DeviceIdType.MESH,
        )
        copy.start()
        sends.append(copy)
    for k in range(1, chips):
        chip = lax.rem(me_chip + chips - k, chips)
        arrival = pltpu.make_async_remote_copy(
            src_ref=mixed.at[chip],
            dst_ref=sums_buf.at[chip],
            send_sem=sems.at[2, k],
            recv_sem=sems.at[3, k],
            device_id={"req": chip * 2 + me_core},
            device_id_type=pl.DeviceIdType.MESH,
        )
        arrival.wait_recv()
    for copy in sends:
        copy.wait_send()
    total = mixed[me_chip]
    for k in range(1, chips):
        total = total + sums_buf[lax.rem(me_chip + chips - k, chips)]
    mean_square = total[:, columns:columns + 1] / D
    o_ref[...] = total[:, :columns] * lax.rsqrt(mean_square + epsilon)


def project(hidden_in, gain, w_qkv, req_n, head_n, count):
    rows, width = hidden_in.shape
    columns = w_qkv.shape[1] + 128
    return pl.pallas_call(
        functools.partial(project_kernel, req_n, head_n),
        out_shape=jax.ShapeDtypeStruct((count, w_qkv.shape[1]), jnp.float32),
        in_specs=[pl.BlockSpec(memory_space=pltpu.VMEM)] * 3,
        out_specs=pl.BlockSpec(memory_space=pltpu.VMEM),
        scratch_shapes=[
            pltpu.VMEM((head_n, rows, width), hidden_in.dtype),
            pltpu.VMEM((2, req_n // 2, count, columns), jnp.float32),
            pltpu.VMEM((req_n // 2, count, columns), jnp.float32),
            pltpu.VMEM((req_n // 2, count, columns), jnp.float32),
            pltpu.VMEM((req_n // 2, count, columns), jnp.float32),
            pltpu.SemaphoreType.DMA((4, max(req_n, head_n))),
        ],
        compiler_params=pltpu.CompilerParams(has_side_effects=True),
    )(hidden_in, gain, w_qkv)


def output_kernel(req_n, head_n, a_ref, w_ref, s_ref, o_ref, att_buf, part, sums_buf, sems):
    me_head = lax.axis_index("head")
    me_req = lax.axis_index("req")
    own = lambda peer: a_ref
    sends = send_all("req", me_req, req_n, own, att_buf, sems.at[0], sems.at[1])
    receive_all("req", me_req, req_n, own, att_buf, sems.at[0], sems.at[1], sends)
    att_buf[me_req] = a_ref[...]
    every = jnp.concatenate(
        [att_buf[s].astype(jnp.float32) for s in range(req_n)], axis=0
    ).astype(jnp.bfloat16)
    part[...] = jnp.dot(every, w_ref[...], preferred_element_type=jnp.float32)
    rows = o_ref.shape[0]
    chunk = lambda peer: part.at[pl.ds(pl.multiple_of(peer * rows, rows), rows)]
    sends = send_all("head", me_head, head_n, chunk, sums_buf, sems.at[2], sems.at[3])
    receive_all("head", me_head, head_n, chunk, sums_buf, sems.at[2], sems.at[3], sends)
    total = part[pl.ds(pl.multiple_of(me_head * rows, rows), rows), :]
    for k in range(1, head_n):
        total = total + sums_buf[lax.rem(me_head + head_n - k, head_n)]
    o_ref[...] = (s_ref[...].astype(jnp.float32) + total).astype(o_ref.dtype)


def output_block(attended, w_out, hidden_in, req_n, head_n):
    count, width = attended.shape
    rows, columns = hidden_in.shape
    return pl.pallas_call(
        functools.partial(output_kernel, req_n, head_n),
        out_shape=jax.ShapeDtypeStruct((rows, columns), hidden_in.dtype),
        in_specs=[pl.BlockSpec(memory_space=pltpu.VMEM)] * 3,
        out_specs=pl.BlockSpec(memory_space=pltpu.VMEM),
        scratch_shapes=[
            pltpu.VMEM((req_n, count, width), attended.dtype),
            pltpu.VMEM((head_n * rows, columns), jnp.float32),
            pltpu.VMEM((head_n, rows, columns), jnp.float32),
            pltpu.SemaphoreType.DMA((4, max(req_n, head_n))),
        ],
        compiler_params=pltpu.CompilerParams(has_side_effects=True),
    )(attended, w_out, hidden_in)


def local(req_n, head_n, hidden_in, attn_gain, w_qkv, w_out, k_cache, v_cache, lengths):
    own_count = k_cache.shape[0]
    projected = project(hidden_in, attn_gain, w_qkv, req_n, head_n, own_count)
    slots = k_cache.shape[1]
    local_heads = k_cache.shape[2] // HD
    projected = projected.reshape(own_count, local_heads, GROUP + 2, HD)
    queries = rotate(projected[:, :, :GROUP], lengths).astype(jnp.bfloat16)
    new_keys = rotate(projected[:, :, GROUP], lengths).astype(jnp.bfloat16)
    new_values = projected[:, :, GROUP + 1].astype(jnp.bfloat16)
    cached_keys = k_cache.reshape(own_count, slots, local_heads, HD)
    cached_values = v_cache.reshape(own_count, slots, local_heads, HD)
    factor = HD ** (-0.5)
    attended = attend_padded(
        queries, new_keys, new_values, cached_keys, cached_values, lengths, factor
    )
    flat_rows = attended.reshape(own_count, local_heads * GROUP * HD)
    return output_block(flat_rows, w_out, hidden_in, req_n, head_n)


def solution(mesh):
    return jax.shard_map(
        functools.partial(local, mesh.shape["req"], mesh.shape["head"]),
        mesh=mesh,
        in_specs=(
            P("head", "req"),
            P("req"),
            P("req", "head"),
            P("head", "req"),
            P("req", None, "head"),
            P("req", None, "head"),
            P("req"),
        ),
        out_specs=P("head", "req"),
        check_vma=False,
    )
```

```python
import functools

import jax
import jax.numpy as jnp
from jax import lax
from jax.experimental import pallas as pl
from jax.experimental.pallas import tpu as pltpu
from jax.sharding import PartitionSpec as P

D = 8192
GROUP = 8
HD = 128


epsilon = 1e-05
rope_base = 500000.0


def rotate(vectors, positions):
    halfway = vectors.shape[-1] // 2
    frequency = jnp.exp(
        -jnp.log(rope_base) * 2.0 * jnp.arange(halfway, dtype=jnp.float32) / vectors.shape[-1]
    )
    angles = positions.astype(jnp.float32)[:, None] * frequency[None, :]
    target_shape = (angles.shape[0],) + (1,) * (vectors.ndim - 2) + (halfway,)
    cosine = jnp.cos(angles).reshape(target_shape)
    sine_part = jnp.sin(angles).reshape(target_shape)
    first = vectors[..., :halfway]
    second = vectors[..., halfway:]
    return jnp.concatenate(
        [first * cosine - second * sine_part, second * cosine + first * sine_part], axis=-1
    )


def own_part(own_score, running, totals, new_values):
    own_prob = lax.optimization_barrier(
        (jnp.exp(own_score - running) / totals).astype(jnp.bfloat16)
    )
    return own_prob.astype(jnp.float32)[..., None] * new_values.astype(jnp.float32)[:, :, None, :]


def attend_padded(queries, new_keys, new_values, cached_keys, cached_values, lengths, factor):
    slots = cached_keys.shape[1]
    inside = jnp.arange(slots, dtype=jnp.int32)[None, :] < lengths[:, None]
    scores = (
        jnp.einsum("rkgd,rpkd->rkgp", queries, cached_keys, preferred_element_type=jnp.float32)
        * factor
    )
    scores = jnp.where(inside[:, None, None, :], scores, -1e30)
    own_score = (
        jnp.einsum("rkgd,rkd->rkg", queries, new_keys, preferred_element_type=jnp.float32) * factor
    )
    running = jnp.maximum(jnp.max(scores, axis=3), own_score)
    weights = jnp.where(inside[:, None, None, :], jnp.exp(scores - running[..., None]), 0.0)
    totals = jnp.sum(weights, axis=3) + jnp.exp(own_score - running)
    probs = (weights / totals[..., None]).astype(jnp.bfloat16)
    mixed = jnp.einsum("rkgp,rpkd->rkgd", probs, cached_values, preferred_element_type=jnp.float32)
    mixed = mixed + own_part(own_score, running, totals, new_values)
    return mixed.astype(jnp.bfloat16)


def greet(peers):
    barrier = pltpu.get_barrier_semaphore()
    for axis, me, n in peers:
        for k in range(1, n):
            pl.semaphore_signal(
                barrier, inc=1, device_id={axis: lax.rem(me + k, n)},
                device_id_type=pl.DeviceIdType.MESH,
            )
    pl.semaphore_wait(barrier, sum(n - 1 for _, _, n in peers))


def send_all(axis, me, n, block_of, dst, send_sems, recv_sems):
    sends = []
    for k in range(1, n):
        peer = lax.rem(me + k, n)
        copy = pltpu.make_async_remote_copy(
            src_ref=block_of(peer),
            dst_ref=dst.at[me],
            send_sem=send_sems.at[k],
            recv_sem=recv_sems.at[k],
            device_id={axis: peer},
            device_id_type=pl.DeviceIdType.MESH,
        )
        copy.start()
        sends.append(copy)
    return sends


def receive_all(axis, me, n, block_of, dst, send_sems, recv_sems, sends):
    for k in range(1, n):
        source = lax.rem(me + n - k, n)
        arrival = pltpu.make_async_remote_copy(
            src_ref=block_of(source),
            dst_ref=dst.at[source],
            send_sem=send_sems.at[k],
            recv_sem=recv_sems.at[k],
            device_id={axis: source},
            device_id_type=pl.DeviceIdType.MESH,
        )
        arrival.wait_recv()
    for copy in sends:
        copy.wait_send()


def project_kernel(req_n, head_n, x_ref, gain_ref, w_ref, o_ref,
                   rows_buf, part, pair_buf, mixed, sums_buf, sems):
    me_head = lax.axis_index("head")
    me_req = lax.axis_index("req")
    chips = req_n // 2
    me_core = lax.rem(me_req, 2)
    me_chip = me_req // 2
    partner = me_req + 1 - 2 * me_core
    barrier = pltpu.get_barrier_semaphore()
    for k in range(1, head_n):
        pl.semaphore_signal(
            barrier, inc=1, device_id={"head": lax.rem(me_head + k, head_n)},
            device_id_type=pl.DeviceIdType.MESH,
        )
    pl.semaphore_signal(
        barrier, inc=1, device_id={"req": partner}, device_id_type=pl.DeviceIdType.MESH
    )
    for k in range(1, chips):
        pl.semaphore_signal(
            barrier, inc=1, device_id={"req": lax.rem(me_chip + k, chips) * 2 + me_core},
            device_id_type=pl.DeviceIdType.MESH,
        )
    pl.semaphore_wait(barrier, head_n - 1 + chips)
    own = lambda peer: x_ref
    sends = send_all("head", me_head, head_n, own, rows_buf, sems.at[0], sems.at[1])
    receive_all("head", me_head, head_n, own, rows_buf, sems.at[0], sems.at[1], sends)
    rows_buf[me_head] = x_ref[...]
    block_rows = x_ref.shape[0]
    states = rows_buf[...].reshape(head_n * block_rows, x_ref.shape[1]).astype(jnp.float32)
    scaled = (states * gain_ref[...].astype(jnp.float32)[None, :]).astype(jnp.bfloat16)
    columns = w_ref.shape[1]
    square = jnp.sum(states * states, axis=1, keepdims=True)
    packed = jnp.concatenate(
        [jnp.dot(scaled, w_ref[...], preferred_element_type=jnp.float32),
         jnp.broadcast_to(square, (square.shape[0], part.shape[-1] - columns))],
        axis=1,
    )
    count = o_ref.shape[0]
    packed = packed.reshape(chips, 2, count, part.shape[-1])
    part[0] = packed[:, 0]
    part[1] = packed[:, 1]
    pair = pltpu.make_async_remote_copy(
        src_ref=part.at[1 - me_core],
        dst_ref=pair_buf,
        send_sem=sems.at[2, 0],
        recv_sem=sems.at[3, 0],
        device_id={"req": partner},
        device_id_type=pl.DeviceIdType.MESH,
    )
    pair.start()
    pair.wait()
    mixed[...] = part[me_core] + pair_buf[...]
    sends = []
    for k in range(1, chips):
        chip = lax.rem(me_chip + k, chips)
        copy = pltpu.make_async_remote_copy(
            src_ref=mixed.at[chip],
            dst_ref=sums_buf.at[me_chip],
            send_sem=sems.at[2, k],
            recv_sem=sems.at[3, k],
            device_id={"req": chip * 2 + me_core},
            device_id_type=pl.DeviceIdType.MESH,
        )
        copy.start()
        sends.append(copy)
    for k in range(1, chips):
        chip = lax.rem(me_chip + chips - k, chips)
        arrival = pltpu.make_async_remote_copy(
            src_ref=mixed.at[chip],
            dst_ref=sums_buf.at[chip],
            send_sem=sems.at[2, k],
            recv_sem=sems.at[3, k],
            device_id={"req": chip * 2 + me_core},
            device_id_type=pl.DeviceIdType.MESH,
        )
        arrival.wait_recv()
    for copy in sends:
        copy.wait_send()
    total = mixed[me_chip]
    for k in range(1, chips):
        total = total + sums_buf[lax.rem(me_chip + chips - k, chips)]
    mean_square = total[:, columns:columns + 1] / D
    o_ref[...] = total[:, :columns] * lax.rsqrt(mean_square + epsilon)


def project(hidden_in, gain, w_qkv, req_n, head_n, count):
    rows, width = hidden_in.shape
    columns = w_qkv.shape[1] + 128
    return pl.pallas_call(
        functools.partial(project_kernel, req_n, head_n),
        out_shape=jax.ShapeDtypeStruct((count, w_qkv.shape[1]), jnp.float32),
        in_specs=[pl.BlockSpec(memory_space=pltpu.VMEM)] * 3,
        out_specs=pl.BlockSpec(memory_space=pltpu.VMEM),
        scratch_shapes=[
            pltpu.VMEM((head_n, rows, width), hidden_in.dtype),
            pltpu.VMEM((2, req_n // 2, count, columns), jnp.float32),
            pltpu.VMEM((req_n // 2, count, columns), jnp.float32),
            pltpu.VMEM((req_n // 2, count, columns), jnp.float32),
            pltpu.VMEM((req_n // 2, count, columns), jnp.float32),
            pltpu.SemaphoreType.DMA((4, max(req_n, head_n))),
        ],
        compiler_params=pltpu.CompilerParams(collective_id=0, has_side_effects=True),
    )(hidden_in, gain, w_qkv)


def output_kernel(req_n, head_n, a_ref, w_ref, s_ref, o_ref, att_buf, part, sums_buf, sems):
    me_head = lax.axis_index("head")
    me_req = lax.axis_index("req")
    greet((("req", me_req, req_n), ("head", me_head, head_n)))
    own = lambda peer: a_ref
    sends = send_all("req", me_req, req_n, own, att_buf, sems.at[0], sems.at[1])
    receive_all("req", me_req, req_n, own, att_buf, sems.at[0], sems.at[1], sends)
    att_buf[me_req] = a_ref[...]
    every = jnp.concatenate(
        [att_buf[s].astype(jnp.float32) for s in range(req_n)], axis=0
    ).astype(jnp.bfloat16)
    part[...] = jnp.dot(every, w_ref[...], preferred_element_type=jnp.float32)
    rows = o_ref.shape[0]
    chunk = lambda peer: part.at[pl.ds(pl.multiple_of(peer * rows, rows), rows)]
    sends = send_all("head", me_head, head_n, chunk, sums_buf, sems.at[2], sems.at[3])
    receive_all("head", me_head, head_n, chunk, sums_buf, sems.at[2], sems.at[3], sends)
    total = part[pl.ds(pl.multiple_of(me_head * rows, rows), rows), :]
    for k in range(1, head_n):
        total = total + sums_buf[lax.rem(me_head + head_n - k, head_n)]
    o_ref[...] = (s_ref[...].astype(jnp.float32) + total).astype(o_ref.dtype)


def output_block(attended, w_out, hidden_in, req_n, head_n):
    count, width = attended.shape
    rows, columns = hidden_in.shape
    return pl.pallas_call(
        functools.partial(output_kernel, req_n, head_n),
        out_shape=jax.ShapeDtypeStruct((rows, columns), hidden_in.dtype),
        in_specs=[pl.BlockSpec(memory_space=pltpu.VMEM)] * 3,
        out_specs=pl.BlockSpec(memory_space=pltpu.VMEM),
        scratch_shapes=[
            pltpu.VMEM((req_n, count, width), attended.dtype),
            pltpu.VMEM((head_n * rows, columns), jnp.float32),
            pltpu.VMEM((head_n, rows, columns), jnp.float32),
            pltpu.SemaphoreType.DMA((4, max(req_n, head_n))),
        ],
        compiler_params=pltpu.CompilerParams(collective_id=1, has_side_effects=True),
    )(attended, w_out, hidden_in)


CHUNK = 512


def attend_kernel(len_ref, q_ref, nk_ref, nv_ref, k_hbm, v_hbm, o_ref,
                  keys, values, scores, rows, flat, sems):
    count, slots = k_hbm.shape[0], k_hbm.shape[1]
    chunks = slots // CHUNK
    factor = HD ** (-0.5)

    def chunk_copy(kind, b, c):
        source = (k_hbm, v_hbm)[kind].at[b, pl.ds(c * CHUNK, CHUNK)]
        target = (keys, values)[kind].at[b, pl.ds(c * CHUNK, CHUNK)]
        return pltpu.make_async_copy(source, target, sems.at[kind, b, c])

    for b in range(count):
        live = (len_ref[b] + CHUNK - 1) // CHUNK
        for kind in range(2):
            for c in range(chunks):
                @pl.when(c < live)
                def _():
                    chunk_copy(kind, b, c).start()
    for b in range(count):
        length = len_ref[b]
        live = (length + CHUNK - 1) // CHUNK
        q = q_ref[b]
        for c in range(chunks):
            @pl.when(c < live)
            def _():
                chunk_copy(0, b, c).wait()
                scores[:, pl.ds(c * CHUNK, CHUNK)] = lax.dot_general(
                    q, keys[b, pl.ds(c * CHUNK, CHUNK), :],
                    (((1,), (1,)), ((), ())), preferred_element_type=jnp.float32,
                ) * factor
        inside = lax.broadcasted_iota(jnp.int32, scores.shape, 1) < length
        masked = jnp.where(inside, scores[...], -1e30)
        own = jnp.sum(
            q.astype(jnp.float32) * nk_ref[pl.ds(b, 1), :].astype(jnp.float32),
            axis=1, keepdims=True,
        ) * factor
        running = jnp.maximum(jnp.max(masked, axis=1, keepdims=True), own)
        weights = jnp.where(inside, jnp.exp(masked - running), 0.0)
        own_weight = jnp.exp(own - running)
        totals = jnp.sum(weights, axis=1, keepdims=True) + own_weight
        scores[...] = (weights / totals).astype(jnp.bfloat16).astype(jnp.float32)
        own_prob = (own_weight / totals).astype(jnp.bfloat16).astype(jnp.float32)
        rows[b] = own_prob * nv_ref[pl.ds(b, 1), :].astype(jnp.float32)
        for c in range(chunks):
            @pl.when(c < live)
            def _():
                chunk_copy(1, b, c).wait()
                rows[b] += jnp.dot(
                    scores[:, pl.ds(c * CHUNK, CHUNK)].astype(jnp.bfloat16),
                    values[b, pl.ds(c * CHUNK, CHUNK), :],
                    preferred_element_type=jnp.float32,
                )
    for b in range(count):
        mixed = rows[b].astype(jnp.bfloat16).astype(jnp.float32)
        for g in range(mixed.shape[0]):
            flat[pl.ds(b, 1), pl.ds(g * HD, HD)] = mixed[g:g + 1, :]
    o_ref[...] = flat[...].astype(o_ref.dtype)


def attend(queries, new_keys, new_values, k_cache, v_cache, lengths):
    count, slots, width = k_cache.shape
    groups = queries.shape[1]
    return pl.pallas_call(
        attend_kernel,
        out_shape=jax.ShapeDtypeStruct((count, groups * width), jnp.bfloat16),
        in_specs=[pl.BlockSpec(memory_space=pltpu.SMEM)]
        + [pl.BlockSpec(memory_space=pltpu.VMEM)] * 3
        + [pl.BlockSpec(memory_space=pl.ANY)] * 2,
        out_specs=pl.BlockSpec(memory_space=pltpu.VMEM),
        scratch_shapes=[
            pltpu.VMEM(k_cache.shape, k_cache.dtype),
            pltpu.VMEM(v_cache.shape, v_cache.dtype),
            pltpu.VMEM((groups, slots), jnp.float32),
            pltpu.VMEM((count, groups, width), jnp.float32),
            pltpu.VMEM((count, groups * width), jnp.float32),
            pltpu.SemaphoreType.DMA((2, count, slots // CHUNK)),
        ],
        compiler_params=pltpu.CompilerParams(vmem_limit_bytes=48 * 1024 * 1024),
    )(lengths, queries, new_keys, new_values, k_cache, v_cache)


def local(req_n, head_n, hidden_in, attn_gain, w_qkv, w_out, k_cache, v_cache, lengths):
    own_count = k_cache.shape[0]
    projected = project(hidden_in, attn_gain, w_qkv, req_n, head_n, own_count)
    slots = k_cache.shape[1]
    local_heads = k_cache.shape[2] // HD
    projected = projected.reshape(own_count, local_heads, GROUP + 2, HD)
    queries = rotate(projected[:, 0, :GROUP], lengths).astype(jnp.bfloat16)
    new_keys = rotate(projected[:, 0, GROUP], lengths).astype(jnp.bfloat16)
    new_values = projected[:, 0, GROUP + 1].astype(jnp.bfloat16)
    flat_rows = attend(queries, new_keys, new_values, k_cache, v_cache, lengths)
    return output_block(flat_rows, w_out, hidden_in, req_n, head_n)


def solution(mesh):
    return jax.shard_map(
        functools.partial(local, mesh.shape["req"], mesh.shape["head"]),
        mesh=mesh,
        in_specs=(
            P("head", "req"),
            P("req"),
            P("req", "head"),
            P("head", "req"),
            P("req", None, "head"),
            P("req", None, "head"),
            P("req"),
        ),
        out_specs=P("head", "req"),
        check_vma=False,
    )
```

```python
import functools

import jax
import jax.numpy as jnp
from jax import lax
from jax.experimental import pallas as pl
from jax.experimental.pallas import tpu as pltpu
from jax.sharding import PartitionSpec as P

D = 8192
GROUP = 8
HD = 128


epsilon = 1e-05
rope_base = 500000.0


def rotate(vectors, positions):
    halfway = vectors.shape[-1] // 2
    frequency = jnp.exp(
        -jnp.log(rope_base) * 2.0 * jnp.arange(halfway, dtype=jnp.float32) / vectors.shape[-1]
    )
    angles = positions.astype(jnp.float32)[:, None] * frequency[None, :]
    target_shape = (angles.shape[0],) + (1,) * (vectors.ndim - 2) + (halfway,)
    cosine = jnp.cos(angles).reshape(target_shape)
    sine_part = jnp.sin(angles).reshape(target_shape)
    first = vectors[..., :halfway]
    second = vectors[..., halfway:]
    return jnp.concatenate(
        [first * cosine - second * sine_part, second * cosine + first * sine_part], axis=-1
    )


def own_part(own_score, running, totals, new_values):
    own_prob = lax.optimization_barrier(
        (jnp.exp(own_score - running) / totals).astype(jnp.bfloat16)
    )
    return own_prob.astype(jnp.float32)[..., None] * new_values.astype(jnp.float32)[:, :, None, :]


def attend_padded(queries, new_keys, new_values, cached_keys, cached_values, lengths, factor):
    slots = cached_keys.shape[1]
    inside = jnp.arange(slots, dtype=jnp.int32)[None, :] < lengths[:, None]
    scores = (
        jnp.einsum("rkgd,rpkd->rkgp", queries, cached_keys, preferred_element_type=jnp.float32)
        * factor
    )
    scores = jnp.where(inside[:, None, None, :], scores, -1e30)
    own_score = (
        jnp.einsum("rkgd,rkd->rkg", queries, new_keys, preferred_element_type=jnp.float32) * factor
    )
    running = jnp.maximum(jnp.max(scores, axis=3), own_score)
    weights = jnp.where(inside[:, None, None, :], jnp.exp(scores - running[..., None]), 0.0)
    totals = jnp.sum(weights, axis=3) + jnp.exp(own_score - running)
    probs = (weights / totals[..., None]).astype(jnp.bfloat16)
    mixed = jnp.einsum("rkgp,rpkd->rkgd", probs, cached_values, preferred_element_type=jnp.float32)
    mixed = mixed + own_part(own_score, running, totals, new_values)
    return mixed.astype(jnp.bfloat16)


def greet(peers):
    barrier = pltpu.get_barrier_semaphore()
    for axis, me, n in peers:
        for k in range(1, n):
            pl.semaphore_signal(
                barrier, inc=1, device_id={axis: lax.rem(me + k, n)},
                device_id_type=pl.DeviceIdType.MESH,
            )
    pl.semaphore_wait(barrier, sum(n - 1 for _, _, n in peers))


def send_all(axis, me, n, block_of, dst, send_sems, recv_sems):
    sends = []
    for k in range(1, n):
        peer = lax.rem(me + k, n)
        copy = pltpu.make_async_remote_copy(
            src_ref=block_of(peer),
            dst_ref=dst.at[me],
            send_sem=send_sems.at[k],
            recv_sem=recv_sems.at[k],
            device_id={axis: peer},
            device_id_type=pl.DeviceIdType.MESH,
        )
        copy.start()
        sends.append(copy)
    return sends


def receive_all(axis, me, n, block_of, dst, send_sems, recv_sems, sends):
    for k in range(1, n):
        source = lax.rem(me + n - k, n)
        arrival = pltpu.make_async_remote_copy(
            src_ref=block_of(source),
            dst_ref=dst.at[source],
            send_sem=send_sems.at[k],
            recv_sem=recv_sems.at[k],
            device_id={axis: source},
            device_id_type=pl.DeviceIdType.MESH,
        )
        arrival.wait_recv()
    for copy in sends:
        copy.wait_send()


def project_kernel(req_n, head_n, x_ref, gain_ref, w_ref, cos_ref, sin_ref, q_ref, k_ref, v_ref,
                   rows_buf, part, pair_buf, mixed, sums_buf, sems):
    me_head = lax.axis_index("head")
    me_req = lax.axis_index("req")
    chips = req_n // 2
    me_core = lax.rem(me_req, 2)
    me_chip = me_req // 2
    partner = me_req + 1 - 2 * me_core
    barrier = pltpu.get_barrier_semaphore()
    for k in range(1, head_n):
        pl.semaphore_signal(
            barrier, inc=1, device_id={"head": lax.rem(me_head + k, head_n)},
            device_id_type=pl.DeviceIdType.MESH,
        )
    pl.semaphore_signal(
        barrier, inc=1, device_id={"req": partner}, device_id_type=pl.DeviceIdType.MESH
    )
    for k in range(1, chips):
        pl.semaphore_signal(
            barrier, inc=1, device_id={"req": lax.rem(me_chip + k, chips) * 2 + me_core},
            device_id_type=pl.DeviceIdType.MESH,
        )
    pl.semaphore_wait(barrier, head_n - 1 + chips)
    own = lambda peer: x_ref
    sends = send_all("head", me_head, head_n, own, rows_buf, sems.at[0], sems.at[1])
    receive_all("head", me_head, head_n, own, rows_buf, sems.at[0], sems.at[1], sends)
    rows_buf[me_head] = x_ref[...]
    block_rows = x_ref.shape[0]
    states = rows_buf[...].reshape(head_n * block_rows, x_ref.shape[1]).astype(jnp.float32)
    scaled = (states * gain_ref[...].astype(jnp.float32)[None, :]).astype(jnp.bfloat16)
    columns = w_ref.shape[1]
    square = jnp.sum(states * states, axis=1, keepdims=True)
    packed = jnp.concatenate(
        [jnp.dot(scaled, w_ref[...], preferred_element_type=jnp.float32),
         jnp.broadcast_to(square, (square.shape[0], part.shape[-1] - columns))],
        axis=1,
    )
    count = k_ref.shape[0]
    packed = packed.reshape(chips, 2, count, part.shape[-1])
    part[0] = packed[:, 0]
    part[1] = packed[:, 1]
    pair = pltpu.make_async_remote_copy(
        src_ref=part.at[1 - me_core],
        dst_ref=pair_buf,
        send_sem=sems.at[2, 0],
        recv_sem=sems.at[3, 0],
        device_id={"req": partner},
        device_id_type=pl.DeviceIdType.MESH,
    )
    pair.start()
    pair.wait()
    mixed[...] = part[me_core] + pair_buf[...]
    sends = []
    for k in range(1, chips):
        chip = lax.rem(me_chip + k, chips)
        copy = pltpu.make_async_remote_copy(
            src_ref=mixed.at[chip],
            dst_ref=sums_buf.at[me_chip],
            send_sem=sems.at[2, k],
            recv_sem=sems.at[3, k],
            device_id={"req": chip * 2 + me_core},
            device_id_type=pl.DeviceIdType.MESH,
        )
        copy.start()
        sends.append(copy)
    for k in range(1, chips):
        chip = lax.rem(me_chip + chips - k, chips)
        arrival = pltpu.make_async_remote_copy(
            src_ref=mixed.at[chip],
            dst_ref=sums_buf.at[chip],
            send_sem=sems.at[2, k],
            recv_sem=sems.at[3, k],
            device_id={"req": chip * 2 + me_core},
            device_id_type=pl.DeviceIdType.MESH,
        )
        arrival.wait_recv()
    for copy in sends:
        copy.wait_send()
    total = mixed[me_chip]
    for k in range(1, chips):
        total = total + sums_buf[lax.rem(me_chip + chips - k, chips)]
    mean_square = total[:, columns:columns + 1] / D
    projected = total[:, :columns] * lax.rsqrt(mean_square + epsilon)
    cosine, sine = cos_ref[...], sin_ref[...]
    rotated = lambda block: block * cosine + pltpu.roll(block, HD // 2, 1) * sine
    for g in range(GROUP):
        q_ref[g] = rotated(projected[:, g * HD:(g + 1) * HD]).astype(jnp.bfloat16).astype(jnp.float32)
    k_ref[...] = rotated(projected[:, GROUP * HD:(GROUP + 1) * HD]).astype(k_ref.dtype)
    v_ref[...] = projected[:, (GROUP + 1) * HD:].astype(v_ref.dtype)


def project(hidden_in, gain, w_qkv, lengths, req_n, head_n, count):
    rows, width = hidden_in.shape
    columns = w_qkv.shape[1] + 128
    halfway = HD // 2
    frequency = jnp.exp(
        -jnp.log(rope_base) * 2.0 * jnp.arange(halfway, dtype=jnp.float32) / HD
    )
    angles = lengths.astype(jnp.float32)[:, None] * frequency[None, :]
    cosine = jnp.concatenate([jnp.cos(angles), jnp.cos(angles)], axis=1)
    sine = jnp.concatenate([-jnp.sin(angles), jnp.sin(angles)], axis=1)
    return pl.pallas_call(
        functools.partial(project_kernel, req_n, head_n),
        out_shape=(
            jax.ShapeDtypeStruct((GROUP, count, HD), jnp.float32),
            jax.ShapeDtypeStruct((count, HD), jnp.bfloat16),
            jax.ShapeDtypeStruct((count, HD), jnp.bfloat16),
        ),
        in_specs=[pl.BlockSpec(memory_space=pltpu.VMEM)] * 5,
        out_specs=(pl.BlockSpec(memory_space=pltpu.VMEM),) * 3,
        scratch_shapes=[
            pltpu.VMEM((head_n, rows, width), hidden_in.dtype),
            pltpu.VMEM((2, req_n // 2, count, columns), jnp.float32),
            pltpu.VMEM((req_n // 2, count, columns), jnp.float32),
            pltpu.VMEM((req_n // 2, count, columns), jnp.float32),
            pltpu.VMEM((req_n // 2, count, columns), jnp.float32),
            pltpu.SemaphoreType.DMA((4, max(req_n, head_n))),
        ],
        compiler_params=pltpu.CompilerParams(collective_id=0, has_side_effects=True),
    )(hidden_in, gain, w_qkv, cosine, sine)


def output_kernel(req_n, head_n, a_ref, w_ref, s_ref, o_ref, att_buf, part, sums_buf, sems):
    me_head = lax.axis_index("head")
    me_req = lax.axis_index("req")
    greet((("req", me_req, req_n), ("head", me_head, head_n)))
    own = lambda peer: a_ref
    sends = send_all("req", me_req, req_n, own, att_buf, sems.at[0], sems.at[1])
    receive_all("req", me_req, req_n, own, att_buf, sems.at[0], sems.at[1], sends)
    att_buf[me_req] = a_ref[...]
    every = jnp.concatenate(
        [att_buf[s].astype(jnp.float32) for s in range(req_n)], axis=0
    ).astype(jnp.bfloat16)
    part[...] = jnp.dot(every, w_ref[...], preferred_element_type=jnp.float32)
    rows = o_ref.shape[0]
    chunk = lambda peer: part.at[pl.ds(pl.multiple_of(peer * rows, rows), rows)]
    sends = send_all("head", me_head, head_n, chunk, sums_buf, sems.at[2], sems.at[3])
    receive_all("head", me_head, head_n, chunk, sums_buf, sems.at[2], sems.at[3], sends)
    total = part[pl.ds(pl.multiple_of(me_head * rows, rows), rows), :]
    for k in range(1, head_n):
        total = total + sums_buf[lax.rem(me_head + head_n - k, head_n)]
    o_ref[...] = (s_ref[...].astype(jnp.float32) + total).astype(o_ref.dtype)


def output_block(attended, w_out, hidden_in, req_n, head_n):
    count, width = attended.shape
    rows, columns = hidden_in.shape
    return pl.pallas_call(
        functools.partial(output_kernel, req_n, head_n),
        out_shape=jax.ShapeDtypeStruct((rows, columns), hidden_in.dtype),
        in_specs=[pl.BlockSpec(memory_space=pltpu.VMEM)] * 3,
        out_specs=pl.BlockSpec(memory_space=pltpu.VMEM),
        scratch_shapes=[
            pltpu.VMEM((req_n, count, width), attended.dtype),
            pltpu.VMEM((head_n * rows, columns), jnp.float32),
            pltpu.VMEM((head_n, rows, columns), jnp.float32),
            pltpu.SemaphoreType.DMA((4, max(req_n, head_n))),
        ],
        compiler_params=pltpu.CompilerParams(collective_id=1, has_side_effects=True),
    )(attended, w_out, hidden_in)


def local(req_n, head_n, hidden_in, attn_gain, w_qkv, w_out, k_cache, v_cache, lengths):
    own_count = k_cache.shape[0]
    queries, new_keys, new_values = project(
        hidden_in, attn_gain, w_qkv, lengths, req_n, head_n, own_count
    )
    slots = k_cache.shape[1]
    local_heads = k_cache.shape[2] // HD
    queries = jnp.transpose(queries.astype(jnp.bfloat16), (1, 0, 2))[:, None]
    new_keys = new_keys[:, None]
    new_values = new_values[:, None]
    cached_keys = k_cache.reshape(own_count, slots, local_heads, HD)
    cached_values = v_cache.reshape(own_count, slots, local_heads, HD)
    factor = HD ** (-0.5)
    attended = attend_padded(
        queries, new_keys, new_values, cached_keys, cached_values, lengths, factor
    )
    flat_rows = attended.reshape(own_count, local_heads * GROUP * HD)
    return output_block(flat_rows, w_out, hidden_in, req_n, head_n)


def solution(mesh):
    return jax.shard_map(
        functools.partial(local, mesh.shape["req"], mesh.shape["head"]),
        mesh=mesh,
        in_specs=(
            P("head", "req"),
            P("req"),
            P("req", "head"),
            P("head", "req"),
            P("req", None, "head"),
            P("req", None, "head"),
            P("req"),
        ),
        out_specs=P("head", "req"),
        check_vma=False,
    )
```

```python
import functools

import jax
import jax.numpy as jnp
from jax import lax
from jax.experimental import pallas as pl
from jax.experimental.pallas import tpu as pltpu
from jax.sharding import PartitionSpec as P

D = 8192
GROUP = 8
HD = 128


epsilon = 1e-05
rope_base = 500000.0


def rotate(vectors, positions):
    halfway = vectors.shape[-1] // 2
    frequency = jnp.exp(
        -jnp.log(rope_base) * 2.0 * jnp.arange(halfway, dtype=jnp.float32) / vectors.shape[-1]
    )
    angles = positions.astype(jnp.float32)[:, None] * frequency[None, :]
    target_shape = (angles.shape[0],) + (1,) * (vectors.ndim - 2) + (halfway,)
    cosine = jnp.cos(angles).reshape(target_shape)
    sine_part = jnp.sin(angles).reshape(target_shape)
    first = vectors[..., :halfway]
    second = vectors[..., halfway:]
    return jnp.concatenate(
        [first * cosine - second * sine_part, second * cosine + first * sine_part], axis=-1
    )


def own_part(own_score, running, totals, new_values):
    own_prob = lax.optimization_barrier(
        (jnp.exp(own_score - running) / totals).astype(jnp.bfloat16)
    )
    return own_prob.astype(jnp.float32)[..., None] * new_values.astype(jnp.float32)[:, :, None, :]


def attend_padded(queries, new_keys, new_values, cached_keys, cached_values, lengths, factor):
    slots = cached_keys.shape[1]
    inside = jnp.arange(slots, dtype=jnp.int32)[None, :] < lengths[:, None]
    scores = (
        jnp.einsum("rkgd,rpkd->rkgp", queries, cached_keys, preferred_element_type=jnp.float32)
        * factor
    )
    scores = jnp.where(inside[:, None, None, :], scores, -1e30)
    own_score = (
        jnp.einsum("rkgd,rkd->rkg", queries, new_keys, preferred_element_type=jnp.float32) * factor
    )
    running = jnp.maximum(jnp.max(scores, axis=3), own_score)
    weights = jnp.where(inside[:, None, None, :], jnp.exp(scores - running[..., None]), 0.0)
    totals = jnp.sum(weights, axis=3) + jnp.exp(own_score - running)
    probs = (weights / totals[..., None]).astype(jnp.bfloat16)
    mixed = jnp.einsum("rkgp,rpkd->rkgd", probs, cached_values, preferred_element_type=jnp.float32)
    mixed = mixed + own_part(own_score, running, totals, new_values)
    return mixed.astype(jnp.bfloat16)


def greet(peers):
    barrier = pltpu.get_barrier_semaphore()
    for axis, me, n in peers:
        for k in range(1, n):
            pl.semaphore_signal(
                barrier, inc=1, device_id={axis: lax.rem(me + k, n)},
                device_id_type=pl.DeviceIdType.MESH,
            )
    pl.semaphore_wait(barrier, sum(n - 1 for _, _, n in peers))


def send_all(axis, me, n, block_of, dst, send_sems, recv_sems):
    sends = []
    for k in range(1, n):
        peer = lax.rem(me + k, n)
        copy = pltpu.make_async_remote_copy(
            src_ref=block_of(peer),
            dst_ref=dst.at[me],
            send_sem=send_sems.at[k],
            recv_sem=recv_sems.at[k],
            device_id={axis: peer},
            device_id_type=pl.DeviceIdType.MESH,
        )
        copy.start()
        sends.append(copy)
    return sends


def receive_all(axis, me, n, block_of, dst, send_sems, recv_sems, sends):
    for k in range(1, n):
        source = lax.rem(me + n - k, n)
        arrival = pltpu.make_async_remote_copy(
            src_ref=block_of(source),
            dst_ref=dst.at[source],
            send_sem=send_sems.at[k],
            recv_sem=recv_sems.at[k],
            device_id={axis: source},
            device_id_type=pl.DeviceIdType.MESH,
        )
        arrival.wait_recv()
    for copy in sends:
        copy.wait_send()


def project_kernel(req_n, head_n, x_ref, gain_ref, w_hbm, cos_ref, sin_ref, q_ref, k_ref, v_ref,
                   w_ref, rows_buf, part, pair_buf, mixed, sums_buf, sems, w_sem):
    me_head = lax.axis_index("head")
    me_req = lax.axis_index("req")
    chips = req_n // 2
    me_core = lax.rem(me_req, 2)
    me_chip = me_req // 2
    partner = me_req + 1 - 2 * me_core
    w_copy = pltpu.make_async_copy(w_hbm, w_ref, w_sem)
    w_copy.start()
    barrier = pltpu.get_barrier_semaphore()
    for k in range(1, head_n):
        pl.semaphore_signal(
            barrier, inc=1, device_id={"head": lax.rem(me_head + k, head_n)},
            device_id_type=pl.DeviceIdType.MESH,
        )
    pl.semaphore_signal(
        barrier, inc=1, device_id={"req": partner}, device_id_type=pl.DeviceIdType.MESH
    )
    for k in range(1, chips):
        pl.semaphore_signal(
            barrier, inc=1, device_id={"req": lax.rem(me_chip + k, chips) * 2 + me_core},
            device_id_type=pl.DeviceIdType.MESH,
        )
    pl.semaphore_wait(barrier, head_n - 1 + chips)
    own = lambda peer: x_ref
    sends = send_all("head", me_head, head_n, own, rows_buf, sems.at[0], sems.at[1])
    receive_all("head", me_head, head_n, own, rows_buf, sems.at[0], sems.at[1], sends)
    rows_buf[me_head] = x_ref[...]
    block_rows = x_ref.shape[0]
    states = rows_buf[...].reshape(head_n * block_rows, x_ref.shape[1]).astype(jnp.float32)
    scaled = (states * gain_ref[...].astype(jnp.float32)[None, :]).astype(jnp.bfloat16)
    columns = w_ref.shape[1]
    square = jnp.sum(states * states, axis=1, keepdims=True)
    w_copy.wait()
    packed = jnp.concatenate(
        [jnp.dot(scaled, w_ref[...], preferred_element_type=jnp.float32),
         jnp.broadcast_to(square, (square.shape[0], part.shape[-1] - columns))],
        axis=1,
    )
    count = k_ref.shape[0]
    packed = packed.reshape(chips, 2, count, part.shape[-1])
    part[0] = packed[:, 0]
    part[1] = packed[:, 1]
    pair = pltpu.make_async_remote_copy(
        src_ref=part.at[1 - me_core],
        dst_ref=pair_buf,
        send_sem=sems.at[2, 0],
        recv_sem=sems.at[3, 0],
        device_id={"req": partner},
        device_id_type=pl.DeviceIdType.MESH,
    )
    pair.start()
    pair.wait()
    mixed[...] = part[me_core] + pair_buf[...]
    sends = []
    for k in range(1, chips):
        chip = lax.rem(me_chip + k, chips)
        copy = pltpu.make_async_remote_copy(
            src_ref=mixed.at[chip],
            dst_ref=sums_buf.at[me_chip],
            send_sem=sems.at[2, k],
            recv_sem=sems.at[3, k],
            device_id={"req": chip * 2 + me_core},
            device_id_type=pl.DeviceIdType.MESH,
        )
        copy.start()
        sends.append(copy)
    for k in range(1, chips):
        chip = lax.rem(me_chip + chips - k, chips)
        arrival = pltpu.make_async_remote_copy(
            src_ref=mixed.at[chip],
            dst_ref=sums_buf.at[chip],
            send_sem=sems.at[2, k],
            recv_sem=sems.at[3, k],
            device_id={"req": chip * 2 + me_core},
            device_id_type=pl.DeviceIdType.MESH,
        )
        arrival.wait_recv()
    for copy in sends:
        copy.wait_send()
    total = mixed[me_chip]
    for k in range(1, chips):
        total = total + sums_buf[lax.rem(me_chip + chips - k, chips)]
    mean_square = total[:, columns:columns + 1] / D
    projected = total[:, :columns] * lax.rsqrt(mean_square + epsilon)
    cosine, sine = cos_ref[...], sin_ref[...]
    rotated = lambda block: block * cosine + pltpu.roll(block, HD // 2, 1) * sine
    for g in range(GROUP):
        q_ref[g] = rotated(projected[:, g * HD:(g + 1) * HD]).astype(jnp.bfloat16).astype(jnp.float32)
    k_ref[...] = rotated(projected[:, GROUP * HD:(GROUP + 1) * HD]).astype(k_ref.dtype)
    v_ref[...] = projected[:, (GROUP + 1) * HD:].astype(v_ref.dtype)


def project(hidden_in, gain, w_qkv, lengths, req_n, head_n, count):
    rows, width = hidden_in.shape
    columns = w_qkv.shape[1] + 128
    halfway = HD // 2
    frequency = jnp.exp(
        -jnp.log(rope_base) * 2.0 * jnp.arange(halfway, dtype=jnp.float32) / HD
    )
    angles = lengths.astype(jnp.float32)[:, None] * frequency[None, :]
    cosine = jnp.concatenate([jnp.cos(angles), jnp.cos(angles)], axis=1)
    sine = jnp.concatenate([-jnp.sin(angles), jnp.sin(angles)], axis=1)
    return pl.pallas_call(
        functools.partial(project_kernel, req_n, head_n),
        out_shape=(
            jax.ShapeDtypeStruct((GROUP, count, HD), jnp.float32),
            jax.ShapeDtypeStruct((count, HD), jnp.bfloat16),
            jax.ShapeDtypeStruct((count, HD), jnp.bfloat16),
        ),
        in_specs=[pl.BlockSpec(memory_space=pltpu.VMEM)] * 2
        + [pl.BlockSpec(memory_space=pl.ANY)]
        + [pl.BlockSpec(memory_space=pltpu.VMEM)] * 2,
        out_specs=(pl.BlockSpec(memory_space=pltpu.VMEM),) * 3,
        scratch_shapes=[
            pltpu.VMEM(w_qkv.shape, w_qkv.dtype),
            pltpu.VMEM((head_n, rows, width), hidden_in.dtype),
            pltpu.VMEM((2, req_n // 2, count, columns), jnp.float32),
            pltpu.VMEM((req_n // 2, count, columns), jnp.float32),
            pltpu.VMEM((req_n // 2, count, columns), jnp.float32),
            pltpu.VMEM((req_n // 2, count, columns), jnp.float32),
            pltpu.SemaphoreType.DMA((4, max(req_n, head_n))),
            pltpu.SemaphoreType.DMA(()),
        ],
        compiler_params=pltpu.CompilerParams(collective_id=0, has_side_effects=True),
    )(hidden_in, gain, w_qkv, cosine, sine)


def output_kernel(req_n, head_n, a_ref, w_hbm, s_ref, o_ref, w_ref, att_buf, part, sums_buf,
                  sems, w_sem):
    me_head = lax.axis_index("head")
    me_req = lax.axis_index("req")
    w_copy = pltpu.make_async_copy(w_hbm, w_ref, w_sem)
    w_copy.start()
    greet((("req", me_req, req_n), ("head", me_head, head_n)))
    own = lambda peer: a_ref
    sends = send_all("req", me_req, req_n, own, att_buf, sems.at[0], sems.at[1])
    receive_all("req", me_req, req_n, own, att_buf, sems.at[0], sems.at[1], sends)
    att_buf[me_req] = a_ref[...]
    every = jnp.concatenate(
        [att_buf[s].astype(jnp.float32) for s in range(req_n)], axis=0
    ).astype(jnp.bfloat16)
    w_copy.wait()
    part[...] = jnp.dot(every, w_ref[...], preferred_element_type=jnp.float32)
    rows = o_ref.shape[0]
    chunk = lambda peer: part.at[pl.ds(pl.multiple_of(peer * rows, rows), rows)]
    sends = send_all("head", me_head, head_n, chunk, sums_buf, sems.at[2], sems.at[3])
    receive_all("head", me_head, head_n, chunk, sums_buf, sems.at[2], sems.at[3], sends)
    total = part[pl.ds(pl.multiple_of(me_head * rows, rows), rows), :]
    for k in range(1, head_n):
        total = total + sums_buf[lax.rem(me_head + head_n - k, head_n)]
    o_ref[...] = (s_ref[...].astype(jnp.float32) + total).astype(o_ref.dtype)


def output_block(attended, w_out, hidden_in, req_n, head_n):
    count, width = attended.shape
    rows, columns = hidden_in.shape
    return pl.pallas_call(
        functools.partial(output_kernel, req_n, head_n),
        out_shape=jax.ShapeDtypeStruct((rows, columns), hidden_in.dtype),
        in_specs=[
            pl.BlockSpec(memory_space=pltpu.VMEM),
            pl.BlockSpec(memory_space=pl.ANY),
            pl.BlockSpec(memory_space=pltpu.VMEM),
        ],
        out_specs=pl.BlockSpec(memory_space=pltpu.VMEM),
        scratch_shapes=[
            pltpu.VMEM(w_out.shape, w_out.dtype),
            pltpu.VMEM((req_n, count, width), attended.dtype),
            pltpu.VMEM((head_n * rows, columns), jnp.float32),
            pltpu.VMEM((head_n, rows, columns), jnp.float32),
            pltpu.SemaphoreType.DMA((4, max(req_n, head_n))),
            pltpu.SemaphoreType.DMA(()),
        ],
        compiler_params=pltpu.CompilerParams(collective_id=1, has_side_effects=True),
    )(attended, w_out, hidden_in)


def local(req_n, head_n, hidden_in, attn_gain, w_qkv, w_out, k_cache, v_cache, lengths):
    own_count = k_cache.shape[0]
    queries, new_keys, new_values = project(
        hidden_in, attn_gain, w_qkv, lengths, req_n, head_n, own_count
    )
    slots = k_cache.shape[1]
    local_heads = k_cache.shape[2] // HD
    queries = jnp.transpose(queries.astype(jnp.bfloat16), (1, 0, 2))[:, None]
    new_keys = new_keys[:, None]
    new_values = new_values[:, None]
    cached_keys = k_cache.reshape(own_count, slots, local_heads, HD)
    cached_values = v_cache.reshape(own_count, slots, local_heads, HD)
    factor = HD ** (-0.5)
    attended = attend_padded(
        queries, new_keys, new_values, cached_keys, cached_values, lengths, factor
    )
    flat_rows = attended.reshape(own_count, local_heads * GROUP * HD)
    return output_block(flat_rows, w_out, hidden_in, req_n, head_n)


def solution(mesh):
    return jax.shard_map(
        functools.partial(local, mesh.shape["req"], mesh.shape["head"]),
        mesh=mesh,
        in_specs=(
            P("head", "req"),
            P("req"),
            P("req", "head"),
            P("head", "req"),
            P("req", None, "head"),
            P("req", None, "head"),
            P("req"),
        ),
        out_specs=P("head", "req"),
        check_vma=False,
    )
```

```python
import functools

import jax
import jax.numpy as jnp
from jax import lax
from jax.experimental import pallas as pl
from jax.experimental.pallas import tpu as pltpu
from jax.sharding import PartitionSpec as P

D = 8192
GROUP = 8
HD = 128


epsilon = 1e-05
rope_base = 500000.0


def rotate(vectors, positions):
    halfway = vectors.shape[-1] // 2
    frequency = jnp.exp(
        -jnp.log(rope_base) * 2.0 * jnp.arange(halfway, dtype=jnp.float32) / vectors.shape[-1]
    )
    angles = positions.astype(jnp.float32)[:, None] * frequency[None, :]
    target_shape = (angles.shape[0],) + (1,) * (vectors.ndim - 2) + (halfway,)
    cosine = jnp.cos(angles).reshape(target_shape)
    sine_part = jnp.sin(angles).reshape(target_shape)
    first = vectors[..., :halfway]
    second = vectors[..., halfway:]
    return jnp.concatenate(
        [first * cosine - second * sine_part, second * cosine + first * sine_part], axis=-1
    )


def own_part(own_score, running, totals, new_values):
    own_prob = lax.optimization_barrier(
        (jnp.exp(own_score - running) / totals).astype(jnp.bfloat16)
    )
    return own_prob.astype(jnp.float32)[..., None] * new_values.astype(jnp.float32)[:, :, None, :]


def attend_padded(queries, new_keys, new_values, cached_keys, cached_values, lengths, factor):
    slots = cached_keys.shape[1]
    inside = jnp.arange(slots, dtype=jnp.int32)[None, :] < lengths[:, None]
    scores = (
        jnp.einsum("rkgd,rpkd->rkgp", queries, cached_keys, preferred_element_type=jnp.float32)
        * factor
    )
    scores = jnp.where(inside[:, None, None, :], scores, -1e30)
    own_score = (
        jnp.einsum("rkgd,rkd->rkg", queries, new_keys, preferred_element_type=jnp.float32) * factor
    )
    running = jnp.maximum(jnp.max(scores, axis=3), own_score)
    weights = jnp.where(inside[:, None, None, :], jnp.exp(scores - running[..., None]), 0.0)
    totals = jnp.sum(weights, axis=3) + jnp.exp(own_score - running)
    probs = (weights / totals[..., None]).astype(jnp.bfloat16)
    mixed = jnp.einsum("rkgp,rpkd->rkgd", probs, cached_values, preferred_element_type=jnp.float32)
    mixed = mixed + own_part(own_score, running, totals, new_values)
    return mixed.astype(jnp.bfloat16)


def greet(peers):
    barrier = pltpu.get_barrier_semaphore()
    for axis, me, n in peers:
        for k in range(1, n):
            pl.semaphore_signal(
                barrier, inc=1, device_id={axis: lax.rem(me + k, n)},
                device_id_type=pl.DeviceIdType.MESH,
            )
    pl.semaphore_wait(barrier, sum(n - 1 for _, _, n in peers))


def send_all(axis, me, n, block_of, dst, send_sems, recv_sems):
    sends = []
    for k in range(1, n):
        peer = lax.rem(me + k, n)
        copy = pltpu.make_async_remote_copy(
            src_ref=block_of(peer),
            dst_ref=dst.at[me],
            send_sem=send_sems.at[k],
            recv_sem=recv_sems.at[k],
            device_id={axis: peer},
            device_id_type=pl.DeviceIdType.MESH,
        )
        copy.start()
        sends.append(copy)
    return sends


def receive_all(axis, me, n, block_of, dst, send_sems, recv_sems, sends):
    for k in range(1, n):
        source = lax.rem(me + n - k, n)
        arrival = pltpu.make_async_remote_copy(
            src_ref=block_of(source),
            dst_ref=dst.at[source],
            send_sem=send_sems.at[k],
            recv_sem=recv_sems.at[k],
            device_id={axis: source},
            device_id_type=pl.DeviceIdType.MESH,
        )
        arrival.wait_recv()
    for copy in sends:
        copy.wait_send()


def project_kernel(req_n, head_n, x_ref, gain_ref, w_hbm, cos_ref, sin_ref, q_ref, k_ref, v_ref,
                   w_ref, rows_buf, part, pair_buf, mixed, sums_buf, sems, w_sem):
    me_head = lax.axis_index("head")
    me_req = lax.axis_index("req")
    chips = req_n // 2
    me_core = lax.rem(me_req, 2)
    me_chip = me_req // 2
    partner = me_req + 1 - 2 * me_core
    w_copy = pltpu.make_async_copy(w_hbm, w_ref, w_sem)
    w_copy.start()
    barrier = pltpu.get_barrier_semaphore()
    for k in range(1, head_n):
        pl.semaphore_signal(
            barrier, inc=1, device_id={"head": lax.rem(me_head + k, head_n)},
            device_id_type=pl.DeviceIdType.MESH,
        )
    pl.semaphore_signal(
        barrier, inc=1, device_id={"req": partner}, device_id_type=pl.DeviceIdType.MESH
    )
    for k in range(1, chips):
        pl.semaphore_signal(
            barrier, inc=1, device_id={"req": lax.rem(me_chip + k, chips) * 2 + me_core},
            device_id_type=pl.DeviceIdType.MESH,
        )
    pl.semaphore_wait(barrier, head_n - 1 + chips)
    own = lambda peer: x_ref
    sends = send_all("head", me_head, head_n, own, rows_buf, sems.at[0], sems.at[1])
    receive_all("head", me_head, head_n, own, rows_buf, sems.at[0], sems.at[1], sends)
    rows_buf[me_head] = x_ref[...]
    block_rows = x_ref.shape[0]
    states = rows_buf[...].reshape(head_n * block_rows, x_ref.shape[1]).astype(jnp.float32)
    scaled = (states * gain_ref[...].astype(jnp.float32)[None, :]).astype(jnp.bfloat16)
    columns = w_ref.shape[1]
    square = jnp.sum(states * states, axis=1, keepdims=True)
    w_copy.wait()
    packed = jnp.concatenate(
        [jnp.dot(scaled, w_ref[...], preferred_element_type=jnp.float32),
         jnp.broadcast_to(square, (square.shape[0], part.shape[-1] - columns))],
        axis=1,
    )
    count = k_ref.shape[0]
    packed = packed.reshape(chips, 2, count, part.shape[-1])
    part[0] = packed[:, 0]
    part[1] = packed[:, 1]
    pair = pltpu.make_async_remote_copy(
        src_ref=part.at[1 - me_core],
        dst_ref=pair_buf,
        send_sem=sems.at[2, 0],
        recv_sem=sems.at[3, 0],
        device_id={"req": partner},
        device_id_type=pl.DeviceIdType.MESH,
    )
    pair.start()
    pair.wait()
    mixed[...] = part[me_core] + pair_buf[...]
    sends = []
    for k in range(1, chips):
        chip = lax.rem(me_chip + k, chips)
        copy = pltpu.make_async_remote_copy(
            src_ref=mixed.at[chip],
            dst_ref=sums_buf.at[me_chip],
            send_sem=sems.at[2, k],
            recv_sem=sems.at[3, k],
            device_id={"req": chip * 2 + me_core},
            device_id_type=pl.DeviceIdType.MESH,
        )
        copy.start()
        sends.append(copy)
    for k in range(1, chips):
        chip = lax.rem(me_chip + chips - k, chips)
        arrival = pltpu.make_async_remote_copy(
            src_ref=mixed.at[chip],
            dst_ref=sums_buf.at[chip],
            send_sem=sems.at[2, k],
            recv_sem=sems.at[3, k],
            device_id={"req": chip * 2 + me_core},
            device_id_type=pl.DeviceIdType.MESH,
        )
        arrival.wait_recv()
    for copy in sends:
        copy.wait_send()
    total = mixed[me_chip]
    for k in range(1, chips):
        total = total + sums_buf[lax.rem(me_chip + chips - k, chips)]
    mean_square = total[:, columns:columns + 1] / D
    projected = total[:, :columns] * lax.rsqrt(mean_square + epsilon)
    cosine, sine = cos_ref[...], sin_ref[...]
    rotated = lambda block: block * cosine + pltpu.roll(block, HD // 2, 1) * sine
    for g in range(GROUP):
        q_ref[g] = rotated(projected[:, g * HD:(g + 1) * HD]).astype(jnp.bfloat16).astype(jnp.float32)
    k_ref[...] = rotated(projected[:, GROUP * HD:(GROUP + 1) * HD]).astype(k_ref.dtype)
    v_ref[...] = projected[:, (GROUP + 1) * HD:].astype(v_ref.dtype)


def project(hidden_in, gain, w_qkv, lengths, req_n, head_n, count):
    rows, width = hidden_in.shape
    columns = w_qkv.shape[1] + 128
    halfway = HD // 2
    frequency = jnp.exp(
        -jnp.log(rope_base) * 2.0 * jnp.arange(halfway, dtype=jnp.float32) / HD
    )
    angles = lengths.astype(jnp.float32)[:, None] * frequency[None, :]
    cosine = jnp.concatenate([jnp.cos(angles), jnp.cos(angles)], axis=1)
    sine = jnp.concatenate([-jnp.sin(angles), jnp.sin(angles)], axis=1)
    return pl.pallas_call(
        functools.partial(project_kernel, req_n, head_n),
        out_shape=(
            jax.ShapeDtypeStruct((GROUP, count, HD), jnp.float32),
            jax.ShapeDtypeStruct((count, HD), jnp.bfloat16),
            jax.ShapeDtypeStruct((count, HD), jnp.bfloat16),
        ),
        in_specs=[pl.BlockSpec(memory_space=pltpu.VMEM)] * 2
        + [pl.BlockSpec(memory_space=pl.ANY)]
        + [pl.BlockSpec(memory_space=pltpu.VMEM)] * 2,
        out_specs=(pl.BlockSpec(memory_space=pltpu.VMEM),) * 3,
        scratch_shapes=[
            pltpu.VMEM(w_qkv.shape, w_qkv.dtype),
            pltpu.VMEM((head_n, rows, width), hidden_in.dtype),
            pltpu.VMEM((2, req_n // 2, count, columns), jnp.float32),
            pltpu.VMEM((req_n // 2, count, columns), jnp.float32),
            pltpu.VMEM((req_n // 2, count, columns), jnp.float32),
            pltpu.VMEM((req_n // 2, count, columns), jnp.float32),
            pltpu.SemaphoreType.DMA((4, max(req_n, head_n))),
            pltpu.SemaphoreType.DMA(()),
        ],
        compiler_params=pltpu.CompilerParams(
            collective_id=0, has_side_effects=True, vmem_limit_bytes=12 * 1024 * 1024
        ),
    )(hidden_in, gain, w_qkv, cosine, sine)


def output_kernel(req_n, head_n, a_ref, w_hbm, s_ref, o_ref, w_ref, att_buf, part, sums_buf,
                  sems, w_sem):
    me_head = lax.axis_index("head")
    me_req = lax.axis_index("req")
    w_copy = pltpu.make_async_copy(w_hbm, w_ref, w_sem)
    w_copy.start()
    greet((("req", me_req, req_n), ("head", me_head, head_n)))
    own = lambda peer: a_ref
    sends = send_all("req", me_req, req_n, own, att_buf, sems.at[0], sems.at[1])
    receive_all("req", me_req, req_n, own, att_buf, sems.at[0], sems.at[1], sends)
    att_buf[me_req] = a_ref[...]
    every = jnp.concatenate(
        [att_buf[s].astype(jnp.float32) for s in range(req_n)], axis=0
    ).astype(jnp.bfloat16)
    w_copy.wait()
    part[...] = jnp.dot(every, w_ref[...], preferred_element_type=jnp.float32)
    rows = o_ref.shape[0]
    chunk = lambda peer: part.at[pl.ds(pl.multiple_of(peer * rows, rows), rows)]
    sends = send_all("head", me_head, head_n, chunk, sums_buf, sems.at[2], sems.at[3])
    receive_all("head", me_head, head_n, chunk, sums_buf, sems.at[2], sems.at[3], sends)
    total = part[pl.ds(pl.multiple_of(me_head * rows, rows), rows), :]
    for k in range(1, head_n):
        total = total + sums_buf[lax.rem(me_head + head_n - k, head_n)]
    o_ref[...] = (s_ref[...].astype(jnp.float32) + total).astype(o_ref.dtype)


def output_block(attended, w_out, hidden_in, req_n, head_n):
    count, width = attended.shape
    rows, columns = hidden_in.shape
    return pl.pallas_call(
        functools.partial(output_kernel, req_n, head_n),
        out_shape=jax.ShapeDtypeStruct((rows, columns), hidden_in.dtype),
        in_specs=[
            pl.BlockSpec(memory_space=pltpu.VMEM),
            pl.BlockSpec(memory_space=pl.ANY),
            pl.BlockSpec(memory_space=pltpu.VMEM),
        ],
        out_specs=pl.BlockSpec(memory_space=pltpu.VMEM),
        scratch_shapes=[
            pltpu.VMEM(w_out.shape, w_out.dtype),
            pltpu.VMEM((req_n, count, width), attended.dtype),
            pltpu.VMEM((head_n * rows, columns), jnp.float32),
            pltpu.VMEM((head_n, rows, columns), jnp.float32),
            pltpu.SemaphoreType.DMA((4, max(req_n, head_n))),
            pltpu.SemaphoreType.DMA(()),
        ],
        compiler_params=pltpu.CompilerParams(
            collective_id=1, has_side_effects=True, vmem_limit_bytes=12 * 1024 * 1024
        ),
    )(attended, w_out, hidden_in)


def local(req_n, head_n, hidden_in, attn_gain, w_qkv, w_out, k_cache, v_cache, lengths):
    own_count = k_cache.shape[0]
    queries, new_keys, new_values = project(
        hidden_in, attn_gain, w_qkv, lengths, req_n, head_n, own_count
    )
    slots = k_cache.shape[1]
    local_heads = k_cache.shape[2] // HD
    queries = jnp.transpose(queries.astype(jnp.bfloat16), (1, 0, 2))[:, None]
    new_keys = new_keys[:, None]
    new_values = new_values[:, None]
    cached_keys = k_cache.reshape(own_count, slots, local_heads, HD)
    cached_values = v_cache.reshape(own_count, slots, local_heads, HD)
    factor = HD ** (-0.5)
    attended = attend_padded(
        queries, new_keys, new_values, cached_keys, cached_values, lengths, factor
    )
    flat_rows = attended.reshape(own_count, local_heads * GROUP * HD)
    return output_block(flat_rows, w_out, hidden_in, req_n, head_n)


def solution(mesh):
    return jax.shard_map(
        functools.partial(local, mesh.shape["req"], mesh.shape["head"]),
        mesh=mesh,
        in_specs=(
            P("head", "req"),
            P("req"),
            P("req", "head"),
            P("head", "req"),
            P("req", None, "head"),
            P("req", None, "head"),
            P("req"),
        ),
        out_specs=P("head", "req"),
        check_vma=False,
    )
```

```python
import functools

import jax
import jax.numpy as jnp
from jax import lax
from jax.experimental import pallas as pl
from jax.experimental.pallas import tpu as pltpu
from jax.sharding import PartitionSpec as P

D = 8192
GROUP = 8
HD = 128


epsilon = 1e-05
rope_base = 500000.0


def rotate(vectors, positions):
    halfway = vectors.shape[-1] // 2
    frequency = jnp.exp(
        -jnp.log(rope_base) * 2.0 * jnp.arange(halfway, dtype=jnp.float32) / vectors.shape[-1]
    )
    angles = positions.astype(jnp.float32)[:, None] * frequency[None, :]
    target_shape = (angles.shape[0],) + (1,) * (vectors.ndim - 2) + (halfway,)
    cosine = jnp.cos(angles).reshape(target_shape)
    sine_part = jnp.sin(angles).reshape(target_shape)
    first = vectors[..., :halfway]
    second = vectors[..., halfway:]
    return jnp.concatenate(
        [first * cosine - second * sine_part, second * cosine + first * sine_part], axis=-1
    )


def own_part(own_score, running, totals, new_values):
    own_prob = lax.optimization_barrier(
        (jnp.exp(own_score - running) / totals).astype(jnp.bfloat16)
    )
    return own_prob.astype(jnp.float32)[..., None] * new_values.astype(jnp.float32)[:, :, None, :]


def attend_padded(queries, new_keys, new_values, cached_keys, cached_values, lengths, factor):
    slots = cached_keys.shape[1]
    inside = jnp.arange(slots, dtype=jnp.int32)[None, :] < lengths[:, None]
    scores = (
        jnp.einsum("rkgd,rpkd->rkgp", queries, cached_keys, preferred_element_type=jnp.float32)
        * factor
    )
    scores = jnp.where(inside[:, None, None, :], scores, -1e30)
    own_score = (
        jnp.einsum("rkgd,rkd->rkg", queries, new_keys, preferred_element_type=jnp.float32) * factor
    )
    running = jnp.maximum(jnp.max(scores, axis=3), own_score)
    weights = jnp.where(inside[:, None, None, :], jnp.exp(scores - running[..., None]), 0.0)
    totals = jnp.sum(weights, axis=3) + jnp.exp(own_score - running)
    probs = (weights / totals[..., None]).astype(jnp.bfloat16)
    mixed = jnp.einsum("rkgp,rpkd->rkgd", probs, cached_values, preferred_element_type=jnp.float32)
    mixed = mixed + own_part(own_score, running, totals, new_values)
    return mixed.astype(jnp.bfloat16)


def greet(peers):
    barrier = pltpu.get_barrier_semaphore()
    for axis, me, n in peers:
        for k in range(1, n):
            pl.semaphore_signal(
                barrier, inc=1, device_id={axis: lax.rem(me + k, n)},
                device_id_type=pl.DeviceIdType.MESH,
            )
    pl.semaphore_wait(barrier, sum(n - 1 for _, _, n in peers))


def send_all(axis, me, n, block_of, dst, send_sems, recv_sems):
    sends = []
    for k in range(1, n):
        peer = lax.rem(me + k, n)
        copy = pltpu.make_async_remote_copy(
            src_ref=block_of(peer),
            dst_ref=dst.at[me],
            send_sem=send_sems.at[k],
            recv_sem=recv_sems.at[k],
            device_id={axis: peer},
            device_id_type=pl.DeviceIdType.MESH,
        )
        copy.start()
        sends.append(copy)
    return sends


def receive_all(axis, me, n, block_of, dst, send_sems, recv_sems, sends):
    for k in range(1, n):
        source = lax.rem(me + n - k, n)
        arrival = pltpu.make_async_remote_copy(
            src_ref=block_of(source),
            dst_ref=dst.at[source],
            send_sem=send_sems.at[k],
            recv_sem=recv_sems.at[k],
            device_id={axis: source},
            device_id_type=pl.DeviceIdType.MESH,
        )
        arrival.wait_recv()
    for copy in sends:
        copy.wait_send()


def project_kernel(req_n, head_n, x_ref, gain_ref, w_hbm, cos_ref, sin_ref, keys_hbm, values_hbm,
                   q_ref, k_ref, v_ref, keys_ref, values_ref,
                   w_ref, rows_buf, part, pair_buf, mixed, sums_buf, sems, w_sem, key_sem):
    me_head = lax.axis_index("head")
    me_req = lax.axis_index("req")
    chips = req_n // 2
    me_core = lax.rem(me_req, 2)
    me_chip = me_req // 2
    partner = me_req + 1 - 2 * me_core
    w_copy = pltpu.make_async_copy(w_hbm, w_ref, w_sem)
    w_copy.start()
    key_copy = pltpu.make_async_copy(keys_hbm, keys_ref, key_sem.at[0])
    key_copy.start()
    value_copy = pltpu.make_async_copy(values_hbm, values_ref, key_sem.at[1])
    value_copy.start()
    barrier = pltpu.get_barrier_semaphore()
    for k in range(1, head_n):
        pl.semaphore_signal(
            barrier, inc=1, device_id={"head": lax.rem(me_head + k, head_n)},
            device_id_type=pl.DeviceIdType.MESH,
        )
    pl.semaphore_signal(
        barrier, inc=1, device_id={"req": partner}, device_id_type=pl.DeviceIdType.MESH
    )
    for k in range(1, chips):
        pl.semaphore_signal(
            barrier, inc=1, device_id={"req": lax.rem(me_chip + k, chips) * 2 + me_core},
            device_id_type=pl.DeviceIdType.MESH,
        )
    pl.semaphore_wait(barrier, head_n - 1 + chips)
    own = lambda peer: x_ref
    sends = send_all("head", me_head, head_n, own, rows_buf, sems.at[0], sems.at[1])
    receive_all("head", me_head, head_n, own, rows_buf, sems.at[0], sems.at[1], sends)
    rows_buf[me_head] = x_ref[...]
    block_rows = x_ref.shape[0]
    states = rows_buf[...].reshape(head_n * block_rows, x_ref.shape[1]).astype(jnp.float32)
    scaled = (states * gain_ref[...].astype(jnp.float32)[None, :]).astype(jnp.bfloat16)
    columns = w_ref.shape[1]
    square = jnp.sum(states * states, axis=1, keepdims=True)
    w_copy.wait()
    packed = jnp.concatenate(
        [jnp.dot(scaled, w_ref[...], preferred_element_type=jnp.float32),
         jnp.broadcast_to(square, (square.shape[0], part.shape[-1] - columns))],
        axis=1,
    )
    count = k_ref.shape[0]
    packed = packed.reshape(chips, 2, count, part.shape[-1])
    part[0] = packed[:, 0]
    part[1] = packed[:, 1]
    pair = pltpu.make_async_remote_copy(
        src_ref=part.at[1 - me_core],
        dst_ref=pair_buf,
        send_sem=sems.at[2, 0],
        recv_sem=sems.at[3, 0],
        device_id={"req": partner},
        device_id_type=pl.DeviceIdType.MESH,
    )
    pair.start()
    pair.wait()
    mixed[...] = part[me_core] + pair_buf[...]
    sends = []
    for k in range(1, chips):
        chip = lax.rem(me_chip + k, chips)
        copy = pltpu.make_async_remote_copy(
            src_ref=mixed.at[chip],
            dst_ref=sums_buf.at[me_chip],
            send_sem=sems.at[2, k],
            recv_sem=sems.at[3, k],
            device_id={"req": chip * 2 + me_core},
            device_id_type=pl.DeviceIdType.MESH,
        )
        copy.start()
        sends.append(copy)
    for k in range(1, chips):
        chip = lax.rem(me_chip + chips - k, chips)
        arrival = pltpu.make_async_remote_copy(
            src_ref=mixed.at[chip],
            dst_ref=sums_buf.at[chip],
            send_sem=sems.at[2, k],
            recv_sem=sems.at[3, k],
            device_id={"req": chip * 2 + me_core},
            device_id_type=pl.DeviceIdType.MESH,
        )
        arrival.wait_recv()
    for copy in sends:
        copy.wait_send()
    total = mixed[me_chip]
    for k in range(1, chips):
        total = total + sums_buf[lax.rem(me_chip + chips - k, chips)]
    mean_square = total[:, columns:columns + 1] / D
    projected = total[:, :columns] * lax.rsqrt(mean_square + epsilon)
    cosine, sine = cos_ref[...], sin_ref[...]
    rotated = lambda block: block * cosine + pltpu.roll(block, HD // 2, 1) * sine
    for g in range(GROUP):
        q_ref[g] = rotated(projected[:, g * HD:(g + 1) * HD]).astype(jnp.bfloat16).astype(jnp.float32)
    k_ref[...] = rotated(projected[:, GROUP * HD:(GROUP + 1) * HD]).astype(k_ref.dtype)
    v_ref[...] = projected[:, (GROUP + 1) * HD:].astype(v_ref.dtype)
    key_copy.wait()
    value_copy.wait()


def project(hidden_in, gain, w_qkv, lengths, k_cache, v_cache, req_n, head_n, count):
    rows, width = hidden_in.shape
    columns = w_qkv.shape[1] + 128
    halfway = HD // 2
    frequency = jnp.exp(
        -jnp.log(rope_base) * 2.0 * jnp.arange(halfway, dtype=jnp.float32) / HD
    )
    angles = lengths.astype(jnp.float32)[:, None] * frequency[None, :]
    cosine = jnp.concatenate([jnp.cos(angles), jnp.cos(angles)], axis=1)
    sine = jnp.concatenate([-jnp.sin(angles), jnp.sin(angles)], axis=1)
    return pl.pallas_call(
        functools.partial(project_kernel, req_n, head_n),
        out_shape=(
            jax.ShapeDtypeStruct((GROUP, count, HD), jnp.float32),
            jax.ShapeDtypeStruct((count, HD), jnp.bfloat16),
            jax.ShapeDtypeStruct((count, HD), jnp.bfloat16),
            jax.ShapeDtypeStruct(k_cache.shape, k_cache.dtype),
            jax.ShapeDtypeStruct(v_cache.shape, v_cache.dtype),
        ),
        in_specs=[pl.BlockSpec(memory_space=pltpu.VMEM)] * 2
        + [pl.BlockSpec(memory_space=pl.ANY)]
        + [pl.BlockSpec(memory_space=pltpu.VMEM)] * 2
        + [pl.BlockSpec(memory_space=pl.ANY)] * 2,
        out_specs=(pl.BlockSpec(memory_space=pltpu.VMEM),) * 5,
        scratch_shapes=[
            pltpu.VMEM(w_qkv.shape, w_qkv.dtype),
            pltpu.VMEM((head_n, rows, width), hidden_in.dtype),
            pltpu.VMEM((2, req_n // 2, count, columns), jnp.float32),
            pltpu.VMEM((req_n // 2, count, columns), jnp.float32),
            pltpu.VMEM((req_n // 2, count, columns), jnp.float32),
            pltpu.VMEM((req_n // 2, count, columns), jnp.float32),
            pltpu.SemaphoreType.DMA((4, max(req_n, head_n))),
            pltpu.SemaphoreType.DMA(()),
            pltpu.SemaphoreType.DMA((2,)),
        ],
        compiler_params=pltpu.CompilerParams(
            collective_id=0, has_side_effects=True, vmem_limit_bytes=30 * 1024 * 1024
        ),
    )(hidden_in, gain, w_qkv, cosine, sine, k_cache, v_cache)


def output_kernel(req_n, head_n, a_ref, w_hbm, s_ref, o_ref, w_ref, att_buf, part, sums_buf,
                  sems, w_sem):
    me_head = lax.axis_index("head")
    me_req = lax.axis_index("req")
    w_copy = pltpu.make_async_copy(w_hbm, w_ref, w_sem)
    w_copy.start()
    greet((("req", me_req, req_n), ("head", me_head, head_n)))
    own = lambda peer: a_ref
    sends = send_all("req", me_req, req_n, own, att_buf, sems.at[0], sems.at[1])
    receive_all("req", me_req, req_n, own, att_buf, sems.at[0], sems.at[1], sends)
    att_buf[me_req] = a_ref[...]
    every = jnp.concatenate(
        [att_buf[s].astype(jnp.float32) for s in range(req_n)], axis=0
    ).astype(jnp.bfloat16)
    w_copy.wait()
    part[...] = jnp.dot(every, w_ref[...], preferred_element_type=jnp.float32)
    rows = o_ref.shape[0]
    chunk = lambda peer: part.at[pl.ds(pl.multiple_of(peer * rows, rows), rows)]
    sends = send_all("head", me_head, head_n, chunk, sums_buf, sems.at[2], sems.at[3])
    receive_all("head", me_head, head_n, chunk, sums_buf, sems.at[2], sems.at[3], sends)
    total = part[pl.ds(pl.multiple_of(me_head * rows, rows), rows), :]
    for k in range(1, head_n):
        total = total + sums_buf[lax.rem(me_head + head_n - k, head_n)]
    o_ref[...] = (s_ref[...].astype(jnp.float32) + total).astype(o_ref.dtype)


def output_block(attended, w_out, hidden_in, req_n, head_n):
    count, width = attended.shape
    rows, columns = hidden_in.shape
    return pl.pallas_call(
        functools.partial(output_kernel, req_n, head_n),
        out_shape=jax.ShapeDtypeStruct((rows, columns), hidden_in.dtype),
        in_specs=[
            pl.BlockSpec(memory_space=pltpu.VMEM),
            pl.BlockSpec(memory_space=pl.ANY),
            pl.BlockSpec(memory_space=pltpu.VMEM),
        ],
        out_specs=pl.BlockSpec(memory_space=pltpu.VMEM),
        scratch_shapes=[
            pltpu.VMEM(w_out.shape, w_out.dtype),
            pltpu.VMEM((req_n, count, width), attended.dtype),
            pltpu.VMEM((head_n * rows, columns), jnp.float32),
            pltpu.VMEM((head_n, rows, columns), jnp.float32),
            pltpu.SemaphoreType.DMA((4, max(req_n, head_n))),
            pltpu.SemaphoreType.DMA(()),
        ],
        compiler_params=pltpu.CompilerParams(
            collective_id=1, has_side_effects=True, vmem_limit_bytes=12 * 1024 * 1024
        ),
    )(attended, w_out, hidden_in)


def local(req_n, head_n, hidden_in, attn_gain, w_qkv, w_out, k_cache, v_cache, lengths):
    own_count = k_cache.shape[0]
    queries, new_keys, new_values, k_cache, v_cache = project(
        hidden_in, attn_gain, w_qkv, lengths, k_cache, v_cache, req_n, head_n, own_count
    )
    slots = k_cache.shape[1]
    local_heads = k_cache.shape[2] // HD
    queries = jnp.transpose(queries.astype(jnp.bfloat16), (1, 0, 2))[:, None]
    new_keys = new_keys[:, None]
    new_values = new_values[:, None]
    cached_keys = k_cache.reshape(own_count, slots, local_heads, HD)
    cached_values = v_cache.reshape(own_count, slots, local_heads, HD)
    factor = HD ** (-0.5)
    attended = attend_padded(
        queries, new_keys, new_values, cached_keys, cached_values, lengths, factor
    )
    flat_rows = attended.reshape(own_count, local_heads * GROUP * HD)
    return output_block(flat_rows, w_out, hidden_in, req_n, head_n)


def solution(mesh):
    return jax.shard_map(
        functools.partial(local, mesh.shape["req"], mesh.shape["head"]),
        mesh=mesh,
        in_specs=(
            P("head", "req"),
            P("req"),
            P("req", "head"),
            P("head", "req"),
            P("req", None, "head"),
            P("req", None, "head"),
            P("req"),
        ),
        out_specs=P("head", "req"),
        check_vma=False,
    )
```

```python
import functools

import jax
import jax.numpy as jnp
from jax import lax
from jax.experimental import pallas as pl
from jax.experimental.pallas import tpu as pltpu
from jax.sharding import PartitionSpec as P

D = 8192
GROUP = 8
HD = 128


epsilon = 1e-05
rope_base = 500000.0


def rotate(vectors, positions):
    halfway = vectors.shape[-1] // 2
    frequency = jnp.exp(
        -jnp.log(rope_base) * 2.0 * jnp.arange(halfway, dtype=jnp.float32) / vectors.shape[-1]
    )
    angles = positions.astype(jnp.float32)[:, None] * frequency[None, :]
    target_shape = (angles.shape[0],) + (1,) * (vectors.ndim - 2) + (halfway,)
    cosine = jnp.cos(angles).reshape(target_shape)
    sine_part = jnp.sin(angles).reshape(target_shape)
    first = vectors[..., :halfway]
    second = vectors[..., halfway:]
    return jnp.concatenate(
        [first * cosine - second * sine_part, second * cosine + first * sine_part], axis=-1
    )


def own_part(own_score, running, totals, new_values):
    own_prob = lax.optimization_barrier(
        (jnp.exp(own_score - running) / totals).astype(jnp.bfloat16)
    )
    return own_prob.astype(jnp.float32)[..., None] * new_values.astype(jnp.float32)[:, :, None, :]


def attend_padded(queries, new_keys, new_values, cached_keys, cached_values, lengths, factor):
    slots = cached_keys.shape[1]
    inside = jnp.arange(slots, dtype=jnp.int32)[None, :] < lengths[:, None]
    scores = (
        jnp.einsum("rkgd,rpkd->rkgp", queries, cached_keys, preferred_element_type=jnp.float32)
        * factor
    )
    scores = jnp.where(inside[:, None, None, :], scores, -1e30)
    own_score = (
        jnp.einsum("rkgd,rkd->rkg", queries, new_keys, preferred_element_type=jnp.float32) * factor
    )
    running = jnp.maximum(jnp.max(scores, axis=3), own_score)
    weights = jnp.where(inside[:, None, None, :], jnp.exp(scores - running[..., None]), 0.0)
    totals = jnp.sum(weights, axis=3) + jnp.exp(own_score - running)
    probs = (weights / totals[..., None]).astype(jnp.bfloat16)
    mixed = jnp.einsum("rkgp,rpkd->rkgd", probs, cached_values, preferred_element_type=jnp.float32)
    mixed = mixed + own_part(own_score, running, totals, new_values)
    return mixed.astype(jnp.bfloat16)


def greet(peers):
    barrier = pltpu.get_barrier_semaphore()
    for axis, me, n in peers:
        for k in range(1, n):
            pl.semaphore_signal(
                barrier, inc=1, device_id={axis: lax.rem(me + k, n)},
                device_id_type=pl.DeviceIdType.MESH,
            )
    pl.semaphore_wait(barrier, sum(n - 1 for _, _, n in peers))


def send_all(axis, me, n, block_of, dst, send_sems, recv_sems):
    sends = []
    for k in range(1, n):
        peer = lax.rem(me + k, n)
        copy = pltpu.make_async_remote_copy(
            src_ref=block_of(peer),
            dst_ref=dst.at[me],
            send_sem=send_sems.at[k],
            recv_sem=recv_sems.at[k],
            device_id={axis: peer},
            device_id_type=pl.DeviceIdType.MESH,
        )
        copy.start()
        sends.append(copy)
    return sends


def receive_all(axis, me, n, block_of, dst, send_sems, recv_sems, sends):
    for k in range(1, n):
        source = lax.rem(me + n - k, n)
        arrival = pltpu.make_async_remote_copy(
            src_ref=block_of(source),
            dst_ref=dst.at[source],
            send_sem=send_sems.at[k],
            recv_sem=recv_sems.at[k],
            device_id={axis: source},
            device_id_type=pl.DeviceIdType.MESH,
        )
        arrival.wait_recv()
    for copy in sends:
        copy.wait_send()


def project_kernel(req_n, head_n, x_hbm, gain_hbm, w_hbm, cos_ref, sin_ref, keys_hbm, values_hbm,
                   q_ref, k_ref, v_ref, keys_ref, values_ref,
                   w_ref, gain_ref, rows_buf, part, pair_buf, mixed, sums_buf, sems, w_sem, key_sem):
    me_head = lax.axis_index("head")
    me_req = lax.axis_index("req")
    chips = req_n // 2
    me_core = lax.rem(me_req, 2)
    me_chip = me_req // 2
    partner = me_req + 1 - 2 * me_core
    w_copy = pltpu.make_async_copy(w_hbm, w_ref, w_sem.at[0])
    w_copy.start()
    x_copy = pltpu.make_async_copy(x_hbm, rows_buf.at[me_head], w_sem.at[1])
    x_copy.start()
    gain_copy = pltpu.make_async_copy(gain_hbm, gain_ref, w_sem.at[2])
    gain_copy.start()
    key_copy = pltpu.make_async_copy(keys_hbm, keys_ref, key_sem.at[0])
    key_copy.start()
    value_copy = pltpu.make_async_copy(values_hbm, values_ref, key_sem.at[1])
    value_copy.start()
    barrier = pltpu.get_barrier_semaphore()
    for k in range(1, head_n):
        pl.semaphore_signal(
            barrier, inc=1, device_id={"head": lax.rem(me_head + k, head_n)},
            device_id_type=pl.DeviceIdType.MESH,
        )
    pl.semaphore_signal(
        barrier, inc=1, device_id={"req": partner}, device_id_type=pl.DeviceIdType.MESH
    )
    for k in range(1, chips):
        pl.semaphore_signal(
            barrier, inc=1, device_id={"req": lax.rem(me_chip + k, chips) * 2 + me_core},
            device_id_type=pl.DeviceIdType.MESH,
        )
    pl.semaphore_wait(barrier, head_n - 1 + chips)
    own = lambda peer: x_hbm
    sends = send_all("head", me_head, head_n, own, rows_buf, sems.at[0], sems.at[1])
    receive_all("head", me_head, head_n, own, rows_buf, sems.at[0], sems.at[1], sends)
    x_copy.wait()
    gain_copy.wait()
    block_rows = x_hbm.shape[0]
    states = rows_buf[...].reshape(head_n * block_rows, x_hbm.shape[1]).astype(jnp.float32)
    scaled = (states * gain_ref[...].astype(jnp.float32)[None, :]).astype(jnp.bfloat16)
    columns = w_ref.shape[1]
    square = jnp.sum(states * states, axis=1, keepdims=True)
    w_copy.wait()
    packed = jnp.concatenate(
        [jnp.dot(scaled, w_ref[...], preferred_element_type=jnp.float32),
         jnp.broadcast_to(square, (square.shape[0], part.shape[-1] - columns))],
        axis=1,
    )
    count = k_ref.shape[0]
    packed = packed.reshape(chips, 2, count, part.shape[-1])
    part[0] = packed[:, 0]
    part[1] = packed[:, 1]
    pair = pltpu.make_async_remote_copy(
        src_ref=part.at[1 - me_core],
        dst_ref=pair_buf,
        send_sem=sems.at[2, 0],
        recv_sem=sems.at[3, 0],
        device_id={"req": partner},
        device_id_type=pl.DeviceIdType.MESH,
    )
    pair.start()
    pair.wait()
    mixed[...] = part[me_core] + pair_buf[...]
    sends = []
    for k in range(1, chips):
        chip = lax.rem(me_chip + k, chips)
        copy = pltpu.make_async_remote_copy(
            src_ref=mixed.at[chip],
            dst_ref=sums_buf.at[me_chip],
            send_sem=sems.at[2, k],
            recv_sem=sems.at[3, k],
            device_id={"req": chip * 2 + me_core},
            device_id_type=pl.DeviceIdType.MESH,
        )
        copy.start()
        sends.append(copy)
    for k in range(1, chips):
        chip = lax.rem(me_chip + chips - k, chips)
        arrival = pltpu.make_async_remote_copy(
            src_ref=mixed.at[chip],
            dst_ref=sums_buf.at[chip],
            send_sem=sems.at[2, k],
            recv_sem=sems.at[3, k],
            device_id={"req": chip * 2 + me_core},
            device_id_type=pl.DeviceIdType.MESH,
        )
        arrival.wait_recv()
    for copy in sends:
        copy.wait_send()
    total = mixed[me_chip]
    for k in range(1, chips):
        total = total + sums_buf[lax.rem(me_chip + chips - k, chips)]
    mean_square = total[:, columns:columns + 1] / D
    projected = total[:, :columns] * lax.rsqrt(mean_square + epsilon)
    cosine, sine = cos_ref[...], sin_ref[...]
    rotated = lambda block: block * cosine + pltpu.roll(block, HD // 2, 1) * sine
    for g in range(GROUP):
        q_ref[g] = rotated(projected[:, g * HD:(g + 1) * HD]).astype(jnp.bfloat16).astype(jnp.float32)
    k_ref[...] = rotated(projected[:, GROUP * HD:(GROUP + 1) * HD]).astype(k_ref.dtype)
    v_ref[...] = projected[:, (GROUP + 1) * HD:].astype(v_ref.dtype)
    key_copy.wait()
    value_copy.wait()


def project(hidden_in, gain, w_qkv, lengths, k_cache, v_cache, req_n, head_n, count):
    rows, width = hidden_in.shape
    columns = w_qkv.shape[1] + 128
    halfway = HD // 2
    frequency = jnp.exp(
        -jnp.log(rope_base) * 2.0 * jnp.arange(halfway, dtype=jnp.float32) / HD
    )
    angles = lengths.astype(jnp.float32)[:, None] * frequency[None, :]
    cosine = jnp.concatenate([jnp.cos(angles), jnp.cos(angles)], axis=1)
    sine = jnp.concatenate([-jnp.sin(angles), jnp.sin(angles)], axis=1)
    return pl.pallas_call(
        functools.partial(project_kernel, req_n, head_n),
        out_shape=(
            jax.ShapeDtypeStruct((GROUP, count, HD), jnp.float32),
            jax.ShapeDtypeStruct((count, HD), jnp.bfloat16),
            jax.ShapeDtypeStruct((count, HD), jnp.bfloat16),
            jax.ShapeDtypeStruct(k_cache.shape, k_cache.dtype),
            jax.ShapeDtypeStruct(v_cache.shape, v_cache.dtype),
        ),
        in_specs=[pl.BlockSpec(memory_space=pltpu.HBM)] * 3
        + [pl.BlockSpec(memory_space=pltpu.VMEM)] * 2
        + [pl.BlockSpec(memory_space=pl.ANY)] * 2,
        out_specs=(pl.BlockSpec(memory_space=pltpu.VMEM),) * 5,
        scratch_shapes=[
            pltpu.VMEM(w_qkv.shape, w_qkv.dtype),
            pltpu.VMEM(gain.shape, gain.dtype),
            pltpu.VMEM((head_n, rows, width), hidden_in.dtype),
            pltpu.VMEM((2, req_n // 2, count, columns), jnp.float32),
            pltpu.VMEM((req_n // 2, count, columns), jnp.float32),
            pltpu.VMEM((req_n // 2, count, columns), jnp.float32),
            pltpu.VMEM((req_n // 2, count, columns), jnp.float32),
            pltpu.SemaphoreType.DMA((4, max(req_n, head_n))),
            pltpu.SemaphoreType.DMA((3,)),
            pltpu.SemaphoreType.DMA((2,)),
        ],
        compiler_params=pltpu.CompilerParams(
            collective_id=0, has_side_effects=True, vmem_limit_bytes=30 * 1024 * 1024
        ),
    )(
        pltpu.with_memory_space_constraint(hidden_in, pltpu.HBM),
        pltpu.with_memory_space_constraint(gain, pltpu.HBM),
        pltpu.with_memory_space_constraint(w_qkv, pltpu.HBM),
        cosine, sine, k_cache, v_cache,
    )


def output_kernel(req_n, head_n, a_ref, w_hbm, s_ref, o_ref, w_ref, att_buf, part, sums_buf,
                  sems, w_sem):
    me_head = lax.axis_index("head")
    me_req = lax.axis_index("req")
    w_copy = pltpu.make_async_copy(w_hbm, w_ref, w_sem)
    w_copy.start()
    greet((("req", me_req, req_n), ("head", me_head, head_n)))
    own = lambda peer: a_ref
    sends = send_all("req", me_req, req_n, own, att_buf, sems.at[0], sems.at[1])
    receive_all("req", me_req, req_n, own, att_buf, sems.at[0], sems.at[1], sends)
    att_buf[me_req] = a_ref[...]
    every = jnp.concatenate(
        [att_buf[s].astype(jnp.float32) for s in range(req_n)], axis=0
    ).astype(jnp.bfloat16)
    w_copy.wait()
    part[...] = jnp.dot(every, w_ref[...], preferred_element_type=jnp.float32)
    rows = o_ref.shape[0]
    chunk = lambda peer: part.at[pl.ds(pl.multiple_of(peer * rows, rows), rows)]
    sends = send_all("head", me_head, head_n, chunk, sums_buf, sems.at[2], sems.at[3])
    receive_all("head", me_head, head_n, chunk, sums_buf, sems.at[2], sems.at[3], sends)
    total = part[pl.ds(pl.multiple_of(me_head * rows, rows), rows), :]
    for k in range(1, head_n):
        total = total + sums_buf[lax.rem(me_head + head_n - k, head_n)]
    o_ref[...] = (s_ref[...].astype(jnp.float32) + total).astype(o_ref.dtype)


def output_block(attended, w_out, hidden_in, req_n, head_n):
    count, width = attended.shape
    rows, columns = hidden_in.shape
    return pl.pallas_call(
        functools.partial(output_kernel, req_n, head_n),
        out_shape=jax.ShapeDtypeStruct((rows, columns), hidden_in.dtype),
        in_specs=[
            pl.BlockSpec(memory_space=pltpu.VMEM),
            pl.BlockSpec(memory_space=pl.ANY),
            pl.BlockSpec(memory_space=pltpu.VMEM),
        ],
        out_specs=pl.BlockSpec(memory_space=pltpu.VMEM),
        scratch_shapes=[
            pltpu.VMEM(w_out.shape, w_out.dtype),
            pltpu.VMEM((req_n, count, width), attended.dtype),
            pltpu.VMEM((head_n * rows, columns), jnp.float32),
            pltpu.VMEM((head_n, rows, columns), jnp.float32),
            pltpu.SemaphoreType.DMA((4, max(req_n, head_n))),
            pltpu.SemaphoreType.DMA(()),
        ],
        compiler_params=pltpu.CompilerParams(
            collective_id=1, has_side_effects=True, vmem_limit_bytes=12 * 1024 * 1024
        ),
    )(attended, w_out, hidden_in)


def local(req_n, head_n, hidden_in, attn_gain, w_qkv, w_out, k_cache, v_cache, lengths):
    own_count = k_cache.shape[0]
    queries, new_keys, new_values, k_cache, v_cache = project(
        hidden_in, attn_gain, w_qkv, lengths, k_cache, v_cache, req_n, head_n, own_count
    )
    slots = k_cache.shape[1]
    local_heads = k_cache.shape[2] // HD
    queries = jnp.transpose(queries.astype(jnp.bfloat16), (1, 0, 2))[:, None]
    new_keys = new_keys[:, None]
    new_values = new_values[:, None]
    cached_keys = k_cache.reshape(own_count, slots, local_heads, HD)
    cached_values = v_cache.reshape(own_count, slots, local_heads, HD)
    factor = HD ** (-0.5)
    attended = attend_padded(
        queries, new_keys, new_values, cached_keys, cached_values, lengths, factor
    )
    flat_rows = attended.reshape(own_count, local_heads * GROUP * HD)
    return output_block(flat_rows, w_out, hidden_in, req_n, head_n)


def solution(mesh):
    return jax.shard_map(
        functools.partial(local, mesh.shape["req"], mesh.shape["head"]),
        mesh=mesh,
        in_specs=(
            P("head", "req"),
            P("req"),
            P("req", "head"),
            P("head", "req"),
            P("req", None, "head"),
            P("req", None, "head"),
            P("req"),
        ),
        out_specs=P("head", "req"),
        check_vma=False,
    )
```

```python
import functools

import jax
import jax.numpy as jnp
from jax import lax
from jax.experimental import pallas as pl
from jax.experimental.pallas import tpu as pltpu
from jax.sharding import PartitionSpec as P

D = 8192
GROUP = 8
HD = 128


epsilon = 1e-05
rope_base = 500000.0


def rotate(vectors, positions):
    halfway = vectors.shape[-1] // 2
    frequency = jnp.exp(
        -jnp.log(rope_base) * 2.0 * jnp.arange(halfway, dtype=jnp.float32) / vectors.shape[-1]
    )
    angles = positions.astype(jnp.float32)[:, None] * frequency[None, :]
    target_shape = (angles.shape[0],) + (1,) * (vectors.ndim - 2) + (halfway,)
    cosine = jnp.cos(angles).reshape(target_shape)
    sine_part = jnp.sin(angles).reshape(target_shape)
    first = vectors[..., :halfway]
    second = vectors[..., halfway:]
    return jnp.concatenate(
        [first * cosine - second * sine_part, second * cosine + first * sine_part], axis=-1
    )


def own_part(own_score, running, totals, new_values):
    own_prob = lax.optimization_barrier(
        (jnp.exp(own_score - running) / totals).astype(jnp.bfloat16)
    )
    return own_prob.astype(jnp.float32)[..., None] * new_values.astype(jnp.float32)[:, :, None, :]


def attend_padded(queries, new_keys, new_values, cached_keys, cached_values, inside, factor):
    scores = (
        jnp.einsum("rkgd,rpkd->rkgp", queries, cached_keys, preferred_element_type=jnp.float32)
        * factor
    )
    scores = jnp.where(inside[:, None, None, :], scores, -1e30)
    own_score = (
        jnp.einsum("rkgd,rkd->rkg", queries, new_keys, preferred_element_type=jnp.float32) * factor
    )
    running = jnp.maximum(jnp.max(scores, axis=3), own_score)
    weights = jnp.where(inside[:, None, None, :], jnp.exp(scores - running[..., None]), 0.0)
    totals = jnp.sum(weights, axis=3) + jnp.exp(own_score - running)
    probs = (weights / totals[..., None]).astype(jnp.bfloat16)
    mixed = jnp.einsum("rkgp,rpkd->rkgd", probs, cached_values, preferred_element_type=jnp.float32)
    mixed = mixed + own_part(own_score, running, totals, new_values)
    return mixed.astype(jnp.bfloat16)


def greet(peers):
    barrier = pltpu.get_barrier_semaphore()
    for axis, me, n in peers:
        for k in range(1, n):
            pl.semaphore_signal(
                barrier, inc=1, device_id={axis: lax.rem(me + k, n)},
                device_id_type=pl.DeviceIdType.MESH,
            )
    pl.semaphore_wait(barrier, sum(n - 1 for _, _, n in peers))


def send_all(axis, me, n, block_of, dst, send_sems, recv_sems):
    sends = []
    for k in range(1, n):
        peer = lax.rem(me + k, n)
        copy = pltpu.make_async_remote_copy(
            src_ref=block_of(peer),
            dst_ref=dst.at[me],
            send_sem=send_sems.at[k],
            recv_sem=recv_sems.at[k],
            device_id={axis: peer},
            device_id_type=pl.DeviceIdType.MESH,
        )
        copy.start()
        sends.append(copy)
    return sends


def receive_all(axis, me, n, block_of, dst, send_sems, recv_sems, sends):
    for k in range(1, n):
        source = lax.rem(me + n - k, n)
        arrival = pltpu.make_async_remote_copy(
            src_ref=block_of(source),
            dst_ref=dst.at[source],
            send_sem=send_sems.at[k],
            recv_sem=recv_sems.at[k],
            device_id={axis: source},
            device_id_type=pl.DeviceIdType.MESH,
        )
        arrival.wait_recv()
    for copy in sends:
        copy.wait_send()


def project_kernel(req_n, head_n, x_hbm, gain_hbm, w_hbm, cos_ref, sin_ref, len_ref, keys_hbm,
                   values_hbm, q_ref, k_ref, v_ref, inside_ref, keys_ref, values_ref,
                   w_ref, gain_ref, rows_buf, part, pair_buf, mixed, sums_buf, sems, w_sem, key_sem):
    me_head = lax.axis_index("head")
    me_req = lax.axis_index("req")
    chips = req_n // 2
    me_core = lax.rem(me_req, 2)
    me_chip = me_req // 2
    partner = me_req + 1 - 2 * me_core
    w_copy = pltpu.make_async_copy(w_hbm, w_ref, w_sem.at[0])
    w_copy.start()
    x_copy = pltpu.make_async_copy(x_hbm, rows_buf.at[me_head], w_sem.at[1])
    x_copy.start()
    gain_copy = pltpu.make_async_copy(gain_hbm, gain_ref, w_sem.at[2])
    gain_copy.start()
    key_copy = pltpu.make_async_copy(keys_hbm, keys_ref, key_sem.at[0])
    key_copy.start()
    value_copy = pltpu.make_async_copy(values_hbm, values_ref, key_sem.at[1])
    value_copy.start()
    barrier = pltpu.get_barrier_semaphore()
    for k in range(1, head_n):
        pl.semaphore_signal(
            barrier, inc=1, device_id={"head": lax.rem(me_head + k, head_n)},
            device_id_type=pl.DeviceIdType.MESH,
        )
    pl.semaphore_signal(
        barrier, inc=1, device_id={"req": partner}, device_id_type=pl.DeviceIdType.MESH
    )
    for k in range(1, chips):
        pl.semaphore_signal(
            barrier, inc=1, device_id={"req": lax.rem(me_chip + k, chips) * 2 + me_core},
            device_id_type=pl.DeviceIdType.MESH,
        )
    pl.semaphore_wait(barrier, head_n - 1 + chips)
    own = lambda peer: x_hbm
    sends = send_all("head", me_head, head_n, own, rows_buf, sems.at[0], sems.at[1])
    receive_all("head", me_head, head_n, own, rows_buf, sems.at[0], sems.at[1], sends)
    x_copy.wait()
    gain_copy.wait()
    block_rows = x_hbm.shape[0]
    states = rows_buf[...].reshape(head_n * block_rows, x_hbm.shape[1]).astype(jnp.float32)
    scaled = (states * gain_ref[...].astype(jnp.float32)[None, :]).astype(jnp.bfloat16)
    columns = w_ref.shape[1]
    square = jnp.sum(states * states, axis=1, keepdims=True)
    w_copy.wait()
    packed = jnp.concatenate(
        [jnp.dot(scaled, w_ref[...], preferred_element_type=jnp.float32),
         jnp.broadcast_to(square, (square.shape[0], part.shape[-1] - columns))],
        axis=1,
    )
    count = k_ref.shape[0]
    packed = packed.reshape(chips, 2, count, part.shape[-1])
    part[0] = packed[:, 0]
    part[1] = packed[:, 1]
    pair = pltpu.make_async_remote_copy(
        src_ref=part.at[1 - me_core],
        dst_ref=pair_buf,
        send_sem=sems.at[2, 0],
        recv_sem=sems.at[3, 0],
        device_id={"req": partner},
        device_id_type=pl.DeviceIdType.MESH,
    )
    pair.start()
    pair.wait()
    mixed[...] = part[me_core] + pair_buf[...]
    sends = []
    for k in range(1, chips):
        chip = lax.rem(me_chip + k, chips)
        copy = pltpu.make_async_remote_copy(
            src_ref=mixed.at[chip],
            dst_ref=sums_buf.at[me_chip],
            send_sem=sems.at[2, k],
            recv_sem=sems.at[3, k],
            device_id={"req": chip * 2 + me_core},
            device_id_type=pl.DeviceIdType.MESH,
        )
        copy.start()
        sends.append(copy)
    for k in range(1, chips):
        chip = lax.rem(me_chip + chips - k, chips)
        arrival = pltpu.make_async_remote_copy(
            src_ref=mixed.at[chip],
            dst_ref=sums_buf.at[chip],
            send_sem=sems.at[2, k],
            recv_sem=sems.at[3, k],
            device_id={"req": chip * 2 + me_core},
            device_id_type=pl.DeviceIdType.MESH,
        )
        arrival.wait_recv()
    for copy in sends:
        copy.wait_send()
    total = mixed[me_chip]
    for k in range(1, chips):
        total = total + sums_buf[lax.rem(me_chip + chips - k, chips)]
    mean_square = total[:, columns:columns + 1] / D
    projected = total[:, :columns] * lax.rsqrt(mean_square + epsilon)
    cosine, sine = cos_ref[...], sin_ref[...]
    rotated = lambda block: block * cosine + pltpu.roll(block, HD // 2, 1) * sine
    for g in range(GROUP):
        q_ref[g] = rotated(projected[:, g * HD:(g + 1) * HD]).astype(jnp.bfloat16).astype(jnp.float32)
    k_ref[...] = rotated(projected[:, GROUP * HD:(GROUP + 1) * HD]).astype(k_ref.dtype)
    v_ref[...] = projected[:, (GROUP + 1) * HD:].astype(v_ref.dtype)
    slot = lax.broadcasted_iota(jnp.int32, (1, inside_ref.shape[1]), 1)
    for b in range(inside_ref.shape[0]):
        inside_ref[pl.ds(b, 1), :] = (slot < len_ref[b]).astype(inside_ref.dtype)
    key_copy.wait()
    value_copy.wait()


def project(hidden_in, gain, w_qkv, lengths, k_cache, v_cache, req_n, head_n, count):
    rows, width = hidden_in.shape
    columns = w_qkv.shape[1] + 128
    halfway = HD // 2
    frequency = jnp.exp(
        -jnp.log(rope_base) * 2.0 * jnp.arange(halfway, dtype=jnp.float32) / HD
    )
    angles = lengths.astype(jnp.float32)[:, None] * frequency[None, :]
    cosine = jnp.concatenate([jnp.cos(angles), jnp.cos(angles)], axis=1)
    sine = jnp.concatenate([-jnp.sin(angles), jnp.sin(angles)], axis=1)
    return pl.pallas_call(
        functools.partial(project_kernel, req_n, head_n),
        out_shape=(
            jax.ShapeDtypeStruct((GROUP, count, HD), jnp.float32),
            jax.ShapeDtypeStruct((count, HD), jnp.bfloat16),
            jax.ShapeDtypeStruct((count, HD), jnp.bfloat16),
            jax.ShapeDtypeStruct((count, k_cache.shape[1]), jnp.int32),
            jax.ShapeDtypeStruct(k_cache.shape, k_cache.dtype),
            jax.ShapeDtypeStruct(v_cache.shape, v_cache.dtype),
        ),
        in_specs=[pl.BlockSpec(memory_space=pltpu.HBM)] * 3
        + [pl.BlockSpec(memory_space=pltpu.VMEM)] * 2
        + [pl.BlockSpec(memory_space=pltpu.SMEM)]
        + [pl.BlockSpec(memory_space=pl.ANY)] * 2,
        out_specs=(pl.BlockSpec(memory_space=pltpu.VMEM),) * 6,
        scratch_shapes=[
            pltpu.VMEM(w_qkv.shape, w_qkv.dtype),
            pltpu.VMEM(gain.shape, gain.dtype),
            pltpu.VMEM((head_n, rows, width), hidden_in.dtype),
            pltpu.VMEM((2, req_n // 2, count, columns), jnp.float32),
            pltpu.VMEM((req_n // 2, count, columns), jnp.float32),
            pltpu.VMEM((req_n // 2, count, columns), jnp.float32),
            pltpu.VMEM((req_n // 2, count, columns), jnp.float32),
            pltpu.SemaphoreType.DMA((4, max(req_n, head_n))),
            pltpu.SemaphoreType.DMA((3,)),
            pltpu.SemaphoreType.DMA((2,)),
        ],
        compiler_params=pltpu.CompilerParams(
            collective_id=0, has_side_effects=True, vmem_limit_bytes=30 * 1024 * 1024
        ),
    )(
        pltpu.with_memory_space_constraint(hidden_in, pltpu.HBM),
        pltpu.with_memory_space_constraint(gain, pltpu.HBM),
        pltpu.with_memory_space_constraint(w_qkv, pltpu.HBM),
        cosine, sine, pltpu.with_memory_space_constraint(lengths, pltpu.HBM), k_cache, v_cache,
    )


def output_kernel(req_n, head_n, a_ref, w_hbm, s_ref, o_ref, w_ref, att_buf, part, sums_buf,
                  sems, w_sem):
    me_head = lax.axis_index("head")
    me_req = lax.axis_index("req")
    w_copy = pltpu.make_async_copy(w_hbm, w_ref, w_sem)
    w_copy.start()
    greet((("req", me_req, req_n), ("head", me_head, head_n)))
    own = lambda peer: a_ref
    sends = send_all("req", me_req, req_n, own, att_buf, sems.at[0], sems.at[1])
    receive_all("req", me_req, req_n, own, att_buf, sems.at[0], sems.at[1], sends)
    att_buf[me_req] = a_ref[...]
    every = jnp.concatenate(
        [att_buf[s].astype(jnp.float32) for s in range(req_n)], axis=0
    ).astype(jnp.bfloat16)
    w_copy.wait()
    part[...] = jnp.dot(every, w_ref[...], preferred_element_type=jnp.float32)
    rows = o_ref.shape[0]
    chunk = lambda peer: part.at[pl.ds(pl.multiple_of(peer * rows, rows), rows)]
    sends = send_all("head", me_head, head_n, chunk, sums_buf, sems.at[2], sems.at[3])
    receive_all("head", me_head, head_n, chunk, sums_buf, sems.at[2], sems.at[3], sends)
    total = part[pl.ds(pl.multiple_of(me_head * rows, rows), rows), :]
    for k in range(1, head_n):
        total = total + sums_buf[lax.rem(me_head + head_n - k, head_n)]
    o_ref[...] = (s_ref[...].astype(jnp.float32) + total).astype(o_ref.dtype)


def output_block(attended, w_out, hidden_in, req_n, head_n):
    count, width = attended.shape
    rows, columns = hidden_in.shape
    return pl.pallas_call(
        functools.partial(output_kernel, req_n, head_n),
        out_shape=jax.ShapeDtypeStruct((rows, columns), hidden_in.dtype),
        in_specs=[
            pl.BlockSpec(memory_space=pltpu.VMEM),
            pl.BlockSpec(memory_space=pl.ANY),
            pl.BlockSpec(memory_space=pltpu.VMEM),
        ],
        out_specs=pl.BlockSpec(memory_space=pltpu.VMEM),
        scratch_shapes=[
            pltpu.VMEM(w_out.shape, w_out.dtype),
            pltpu.VMEM((req_n, count, width), attended.dtype),
            pltpu.VMEM((head_n * rows, columns), jnp.float32),
            pltpu.VMEM((head_n, rows, columns), jnp.float32),
            pltpu.SemaphoreType.DMA((4, max(req_n, head_n))),
            pltpu.SemaphoreType.DMA(()),
        ],
        compiler_params=pltpu.CompilerParams(
            collective_id=1, has_side_effects=True, vmem_limit_bytes=12 * 1024 * 1024
        ),
    )(attended, w_out, hidden_in)


def local(req_n, head_n, hidden_in, attn_gain, w_qkv, w_out, k_cache, v_cache, lengths):
    own_count = k_cache.shape[0]
    queries, new_keys, new_values, inside, k_cache, v_cache = project(
        hidden_in, attn_gain, w_qkv, lengths, k_cache, v_cache, req_n, head_n, own_count
    )
    slots = k_cache.shape[1]
    local_heads = k_cache.shape[2] // HD
    queries = jnp.transpose(queries.astype(jnp.bfloat16), (1, 0, 2))[:, None]
    new_keys = new_keys[:, None]
    new_values = new_values[:, None]
    cached_keys = k_cache.reshape(own_count, slots, local_heads, HD)
    cached_values = v_cache.reshape(own_count, slots, local_heads, HD)
    factor = HD ** (-0.5)
    attended = attend_padded(
        queries, new_keys, new_values, cached_keys, cached_values, inside != 0, factor
    )
    flat_rows = attended.reshape(own_count, local_heads * GROUP * HD)
    return output_block(flat_rows, w_out, hidden_in, req_n, head_n)


def solution(mesh):
    return jax.shard_map(
        functools.partial(local, mesh.shape["req"], mesh.shape["head"]),
        mesh=mesh,
        in_specs=(
            P("head", "req"),
            P("req"),
            P("req", "head"),
            P("head", "req"),
            P("req", None, "head"),
            P("req", None, "head"),
            P("req"),
        ),
        out_specs=P("head", "req"),
        check_vma=False,
    )
```

```python
import functools

import jax
import jax.numpy as jnp
from jax import lax
from jax.experimental import pallas as pl
from jax.experimental.pallas import tpu as pltpu
from jax.sharding import PartitionSpec as P

D = 8192
GROUP = 8
HD = 128


epsilon = 1e-05
rope_base = 500000.0


def rotate(vectors, positions):
    halfway = vectors.shape[-1] // 2
    frequency = jnp.exp(
        -jnp.log(rope_base) * 2.0 * jnp.arange(halfway, dtype=jnp.float32) / vectors.shape[-1]
    )
    angles = positions.astype(jnp.float32)[:, None] * frequency[None, :]
    target_shape = (angles.shape[0],) + (1,) * (vectors.ndim - 2) + (halfway,)
    cosine = jnp.cos(angles).reshape(target_shape)
    sine_part = jnp.sin(angles).reshape(target_shape)
    first = vectors[..., :halfway]
    second = vectors[..., halfway:]
    return jnp.concatenate(
        [first * cosine - second * sine_part, second * cosine + first * sine_part], axis=-1
    )


def own_part(own_score, running, totals, new_values):
    own_prob = lax.optimization_barrier(
        (jnp.exp(own_score - running) / totals).astype(jnp.bfloat16)
    )
    return own_prob.astype(jnp.float32)[..., None] * new_values.astype(jnp.float32)[:, :, None, :]


def attend_padded(queries, new_keys, new_values, cached_keys, cached_values, inside, factor):
    scores = (
        jnp.einsum("rkgd,rpkd->rkgp", queries, cached_keys, preferred_element_type=jnp.float32)
        * factor
    )
    scores = jnp.where(inside[:, None, None, :], scores, -1e30)
    own_score = (
        jnp.einsum("rkgd,rkd->rkg", queries, new_keys, preferred_element_type=jnp.float32) * factor
    )
    running = jnp.maximum(jnp.max(scores, axis=3), own_score)
    weights = jnp.where(inside[:, None, None, :], jnp.exp(scores - running[..., None]), 0.0)
    totals = jnp.sum(weights, axis=3) + jnp.exp(own_score - running)
    probs = (weights / totals[..., None]).astype(jnp.bfloat16)
    mixed = jnp.einsum("rkgp,rpkd->rkgd", probs, cached_values, preferred_element_type=jnp.float32)
    mixed = mixed + own_part(own_score, running, totals, new_values)
    return mixed.astype(jnp.bfloat16)


def greet(peers):
    barrier = pltpu.get_barrier_semaphore()
    for axis, me, n in peers:
        for k in range(1, n):
            pl.semaphore_signal(
                barrier, inc=1, device_id={axis: lax.rem(me + k, n)},
                device_id_type=pl.DeviceIdType.MESH,
            )
    pl.semaphore_wait(barrier, sum(n - 1 for _, _, n in peers))


def send_all(axis, me, n, block_of, dst, send_sems, recv_sems):
    sends = []
    for k in range(1, n):
        peer = lax.rem(me + k, n)
        copy = pltpu.make_async_remote_copy(
            src_ref=block_of(peer),
            dst_ref=dst.at[me],
            send_sem=send_sems.at[k],
            recv_sem=recv_sems.at[k],
            device_id={axis: peer},
            device_id_type=pl.DeviceIdType.MESH,
        )
        copy.start()
        sends.append(copy)
    return sends


def receive_all(axis, me, n, block_of, dst, send_sems, recv_sems, sends):
    for k in range(1, n):
        source = lax.rem(me + n - k, n)
        arrival = pltpu.make_async_remote_copy(
            src_ref=block_of(source),
            dst_ref=dst.at[source],
            send_sem=send_sems.at[k],
            recv_sem=recv_sems.at[k],
            device_id={axis: source},
            device_id_type=pl.DeviceIdType.MESH,
        )
        arrival.wait_recv()
    for copy in sends:
        copy.wait_send()


def project_kernel(req_n, head_n, x_hbm, gain_hbm, w_hbm, cos_ref, sin_ref, len_ref, keys_hbm,
                   values_hbm, q_ref, k_ref, v_ref, inside_ref, keys_ref, values_ref,
                   w_ref, gain_ref, rows_buf, part, pair_buf, mixed, sums_buf, sems, w_sem, key_sem):
    me_head = lax.axis_index("head")
    me_req = lax.axis_index("req")
    chips = req_n // 2
    me_core = lax.rem(me_req, 2)
    me_chip = me_req // 2
    partner = me_req + 1 - 2 * me_core
    w_copy = pltpu.make_async_copy(w_hbm, w_ref, w_sem.at[0])
    w_copy.start()
    x_copy = pltpu.make_async_copy(x_hbm, rows_buf.at[me_head], w_sem.at[1])
    x_copy.start()
    gain_copy = pltpu.make_async_copy(gain_hbm, gain_ref, w_sem.at[2])
    gain_copy.start()
    key_copy = pltpu.make_async_copy(keys_hbm, keys_ref, key_sem.at[0])
    key_copy.start()
    value_copy = pltpu.make_async_copy(values_hbm, values_ref, key_sem.at[1])
    value_copy.start()
    barrier = pltpu.get_barrier_semaphore()
    for k in range(1, head_n):
        pl.semaphore_signal(
            barrier, inc=1, device_id={"head": lax.rem(me_head + k, head_n)},
            device_id_type=pl.DeviceIdType.MESH,
        )
    pl.semaphore_signal(
        barrier, inc=1, device_id={"req": partner}, device_id_type=pl.DeviceIdType.MESH
    )
    for k in range(1, chips):
        pl.semaphore_signal(
            barrier, inc=1, device_id={"req": lax.rem(me_chip + k, chips) * 2 + me_core},
            device_id_type=pl.DeviceIdType.MESH,
        )
    pl.semaphore_wait(barrier, head_n - 1 + chips)
    x_copy.wait()
    own = lambda peer: rows_buf.at[me_head]
    sends = send_all("head", me_head, head_n, own, rows_buf, sems.at[0], sems.at[1])
    receive_all("head", me_head, head_n, own, rows_buf, sems.at[0], sems.at[1], sends)
    gain_copy.wait()
    block_rows = x_hbm.shape[0]
    states = rows_buf[...].reshape(head_n * block_rows, x_hbm.shape[1]).astype(jnp.float32)
    scaled = (states * gain_ref[...].astype(jnp.float32)[None, :]).astype(jnp.bfloat16)
    columns = w_ref.shape[1]
    square = jnp.sum(states * states, axis=1, keepdims=True)
    w_copy.wait()
    packed = jnp.concatenate(
        [jnp.dot(scaled, w_ref[...], preferred_element_type=jnp.float32),
         jnp.broadcast_to(square, (square.shape[0], part.shape[-1] - columns))],
        axis=1,
    )
    count = k_ref.shape[0]
    packed = packed.reshape(chips, 2, count, part.shape[-1])
    part[0] = packed[:, 0]
    part[1] = packed[:, 1]
    pair = pltpu.make_async_remote_copy(
        src_ref=part.at[1 - me_core],
        dst_ref=pair_buf,
        send_sem=sems.at[2, 0],
        recv_sem=sems.at[3, 0],
        device_id={"req": partner},
        device_id_type=pl.DeviceIdType.MESH,
    )
    pair.start()
    pair.wait()
    mixed[...] = part[me_core] + pair_buf[...]
    sends = []
    for k in range(1, chips):
        chip = lax.rem(me_chip + k, chips)
        copy = pltpu.make_async_remote_copy(
            src_ref=mixed.at[chip],
            dst_ref=sums_buf.at[me_chip],
            send_sem=sems.at[2, k],
            recv_sem=sems.at[3, k],
            device_id={"req": chip * 2 + me_core},
            device_id_type=pl.DeviceIdType.MESH,
        )
        copy.start()
        sends.append(copy)
    for k in range(1, chips):
        chip = lax.rem(me_chip + chips - k, chips)
        arrival = pltpu.make_async_remote_copy(
            src_ref=mixed.at[chip],
            dst_ref=sums_buf.at[chip],
            send_sem=sems.at[2, k],
            recv_sem=sems.at[3, k],
            device_id={"req": chip * 2 + me_core},
            device_id_type=pl.DeviceIdType.MESH,
        )
        arrival.wait_recv()
    for copy in sends:
        copy.wait_send()
    total = mixed[me_chip]
    for k in range(1, chips):
        total = total + sums_buf[lax.rem(me_chip + chips - k, chips)]
    mean_square = total[:, columns:columns + 1] / D
    projected = total[:, :columns] * lax.rsqrt(mean_square + epsilon)
    cosine, sine = cos_ref[...], sin_ref[...]
    rotated = lambda block: block * cosine + pltpu.roll(block, HD // 2, 1) * sine
    for g in range(GROUP):
        q_ref[g] = rotated(projected[:, g * HD:(g + 1) * HD]).astype(jnp.bfloat16).astype(jnp.float32)
    k_ref[...] = rotated(projected[:, GROUP * HD:(GROUP + 1) * HD]).astype(k_ref.dtype)
    v_ref[...] = projected[:, (GROUP + 1) * HD:].astype(v_ref.dtype)
    slot = lax.broadcasted_iota(jnp.int32, (1, inside_ref.shape[1]), 1)
    for b in range(inside_ref.shape[0]):
        inside_ref[pl.ds(b, 1), :] = (slot < len_ref[b]).astype(inside_ref.dtype)
    key_copy.wait()
    value_copy.wait()


def project(hidden_in, gain, w_qkv, lengths, k_cache, v_cache, req_n, head_n, count):
    rows, width = hidden_in.shape
    columns = w_qkv.shape[1] + 128
    halfway = HD // 2
    frequency = jnp.exp(
        -jnp.log(rope_base) * 2.0 * jnp.arange(halfway, dtype=jnp.float32) / HD
    )
    angles = lengths.astype(jnp.float32)[:, None] * frequency[None, :]
    cosine = jnp.concatenate([jnp.cos(angles), jnp.cos(angles)], axis=1)
    sine = jnp.concatenate([-jnp.sin(angles), jnp.sin(angles)], axis=1)
    return pl.pallas_call(
        functools.partial(project_kernel, req_n, head_n),
        out_shape=(
            jax.ShapeDtypeStruct((GROUP, count, HD), jnp.float32),
            jax.ShapeDtypeStruct((count, HD), jnp.bfloat16),
            jax.ShapeDtypeStruct((count, HD), jnp.bfloat16),
            jax.ShapeDtypeStruct((count, k_cache.shape[1]), jnp.int32),
            jax.ShapeDtypeStruct(k_cache.shape, k_cache.dtype),
            jax.ShapeDtypeStruct(v_cache.shape, v_cache.dtype),
        ),
        in_specs=[pl.BlockSpec(memory_space=pltpu.HBM)] * 3
        + [pl.BlockSpec(memory_space=pltpu.VMEM)] * 2
        + [pl.BlockSpec(memory_space=pltpu.SMEM)]
        + [pl.BlockSpec(memory_space=pl.ANY)] * 2,
        out_specs=(pl.BlockSpec(memory_space=pltpu.VMEM),) * 6,
        scratch_shapes=[
            pltpu.VMEM(w_qkv.shape, w_qkv.dtype),
            pltpu.VMEM(gain.shape, gain.dtype),
            pltpu.VMEM((head_n, rows, width), hidden_in.dtype),
            pltpu.VMEM((2, req_n // 2, count, columns), jnp.float32),
            pltpu.VMEM((req_n // 2, count, columns), jnp.float32),
            pltpu.VMEM((req_n // 2, count, columns), jnp.float32),
            pltpu.VMEM((req_n // 2, count, columns), jnp.float32),
            pltpu.SemaphoreType.DMA((4, max(req_n, head_n))),
            pltpu.SemaphoreType.DMA((3,)),
            pltpu.SemaphoreType.DMA((2,)),
        ],
        compiler_params=pltpu.CompilerParams(
            collective_id=0, has_side_effects=True, vmem_limit_bytes=30 * 1024 * 1024
        ),
    )(
        pltpu.with_memory_space_constraint(hidden_in, pltpu.HBM),
        pltpu.with_memory_space_constraint(gain, pltpu.HBM),
        pltpu.with_memory_space_constraint(w_qkv, pltpu.HBM),
        cosine, sine, pltpu.with_memory_space_constraint(lengths, pltpu.HBM), k_cache, v_cache,
    )


def output_kernel(req_n, head_n, a_ref, w_hbm, s_ref, o_ref, w_ref, att_buf, part, sums_buf,
                  sems, w_sem):
    me_head = lax.axis_index("head")
    me_req = lax.axis_index("req")
    w_copy = pltpu.make_async_copy(w_hbm, w_ref, w_sem)
    w_copy.start()
    greet((("req", me_req, req_n), ("head", me_head, head_n)))
    own = lambda peer: a_ref
    sends = send_all("req", me_req, req_n, own, att_buf, sems.at[0], sems.at[1])
    receive_all("req", me_req, req_n, own, att_buf, sems.at[0], sems.at[1], sends)
    att_buf[me_req] = a_ref[...]
    every = jnp.concatenate(
        [att_buf[s].astype(jnp.float32) for s in range(req_n)], axis=0
    ).astype(jnp.bfloat16)
    w_copy.wait()
    part[...] = jnp.dot(every, w_ref[...], preferred_element_type=jnp.float32)
    rows = o_ref.shape[0]
    chunk = lambda peer: part.at[pl.ds(pl.multiple_of(peer * rows, rows), rows)]
    sends = send_all("head", me_head, head_n, chunk, sums_buf, sems.at[2], sems.at[3])
    receive_all("head", me_head, head_n, chunk, sums_buf, sems.at[2], sems.at[3], sends)
    total = part[pl.ds(pl.multiple_of(me_head * rows, rows), rows), :]
    for k in range(1, head_n):
        total = total + sums_buf[lax.rem(me_head + head_n - k, head_n)]
    o_ref[...] = (s_ref[...].astype(jnp.float32) + total).astype(o_ref.dtype)


def output_block(attended, w_out, hidden_in, req_n, head_n):
    count, width = attended.shape
    rows, columns = hidden_in.shape
    return pl.pallas_call(
        functools.partial(output_kernel, req_n, head_n),
        out_shape=jax.ShapeDtypeStruct((rows, columns), hidden_in.dtype),
        in_specs=[
            pl.BlockSpec(memory_space=pltpu.VMEM),
            pl.BlockSpec(memory_space=pl.ANY),
            pl.BlockSpec(memory_space=pltpu.VMEM),
        ],
        out_specs=pl.BlockSpec(memory_space=pltpu.VMEM),
        scratch_shapes=[
            pltpu.VMEM(w_out.shape, w_out.dtype),
            pltpu.VMEM((req_n, count, width), attended.dtype),
            pltpu.VMEM((head_n * rows, columns), jnp.float32),
            pltpu.VMEM((head_n, rows, columns), jnp.float32),
            pltpu.SemaphoreType.DMA((4, max(req_n, head_n))),
            pltpu.SemaphoreType.DMA(()),
        ],
        compiler_params=pltpu.CompilerParams(
            collective_id=1, has_side_effects=True, vmem_limit_bytes=12 * 1024 * 1024
        ),
    )(attended, w_out, hidden_in)


def local(req_n, head_n, hidden_in, attn_gain, w_qkv, w_out, k_cache, v_cache, lengths):
    own_count = k_cache.shape[0]
    queries, new_keys, new_values, inside, k_cache, v_cache = project(
        hidden_in, attn_gain, w_qkv, lengths, k_cache, v_cache, req_n, head_n, own_count
    )
    slots = k_cache.shape[1]
    local_heads = k_cache.shape[2] // HD
    queries = jnp.transpose(queries.astype(jnp.bfloat16), (1, 0, 2))[:, None]
    new_keys = new_keys[:, None]
    new_values = new_values[:, None]
    cached_keys = k_cache.reshape(own_count, slots, local_heads, HD)
    cached_values = v_cache.reshape(own_count, slots, local_heads, HD)
    factor = HD ** (-0.5)
    attended = attend_padded(
        queries, new_keys, new_values, cached_keys, cached_values, inside != 0, factor
    )
    flat_rows = attended.reshape(own_count, local_heads * GROUP * HD)
    return output_block(flat_rows, w_out, hidden_in, req_n, head_n)


def solution(mesh):
    return jax.shard_map(
        functools.partial(local, mesh.shape["req"], mesh.shape["head"]),
        mesh=mesh,
        in_specs=(
            P("head", "req"),
            P("req"),
            P("req", "head"),
            P("head", "req"),
            P("req", None, "head"),
            P("req", None, "head"),
            P("req"),
        ),
        out_specs=P("head", "req"),
        check_vma=False,
    )
```

```python
import functools

import jax
import jax.numpy as jnp
from jax import lax
from jax.experimental import pallas as pl
from jax.experimental.pallas import tpu as pltpu
from jax.sharding import PartitionSpec as P

D = 8192
GROUP = 8
HD = 128


epsilon = 1e-05
rope_base = 500000.0


def rotate(vectors, positions):
    halfway = vectors.shape[-1] // 2
    frequency = jnp.exp(
        -jnp.log(rope_base) * 2.0 * jnp.arange(halfway, dtype=jnp.float32) / vectors.shape[-1]
    )
    angles = positions.astype(jnp.float32)[:, None] * frequency[None, :]
    target_shape = (angles.shape[0],) + (1,) * (vectors.ndim - 2) + (halfway,)
    cosine = jnp.cos(angles).reshape(target_shape)
    sine_part = jnp.sin(angles).reshape(target_shape)
    first = vectors[..., :halfway]
    second = vectors[..., halfway:]
    return jnp.concatenate(
        [first * cosine - second * sine_part, second * cosine + first * sine_part], axis=-1
    )


def own_part(own_score, running, totals, new_values):
    own_prob = lax.optimization_barrier(
        (jnp.exp(own_score - running) / totals).astype(jnp.bfloat16)
    )
    return own_prob.astype(jnp.float32)[..., None] * new_values.astype(jnp.float32)[:, :, None, :]


def attend_padded(queries, new_keys, new_values, cached_keys, cached_values, inside, factor):
    scores = (
        jnp.einsum("rkgd,rpkd->rkgp", queries, cached_keys, preferred_element_type=jnp.float32)
        * factor
    )
    scores = jnp.where(inside[:, None, None, :], scores, -1e30)
    own_score = (
        jnp.einsum("rkgd,rkd->rkg", queries, new_keys, preferred_element_type=jnp.float32) * factor
    )
    running = jnp.maximum(jnp.max(scores, axis=3), own_score)
    weights = jnp.where(inside[:, None, None, :], jnp.exp(scores - running[..., None]), 0.0)
    totals = jnp.sum(weights, axis=3) + jnp.exp(own_score - running)
    probs = (weights / totals[..., None]).astype(jnp.bfloat16)
    mixed = jnp.einsum("rkgp,rpkd->rkgd", probs, cached_values, preferred_element_type=jnp.float32)
    mixed = mixed + own_part(own_score, running, totals, new_values)
    return mixed.astype(jnp.bfloat16)


def greet(peers):
    barrier = pltpu.get_barrier_semaphore()
    for axis, me, n in peers:
        for k in range(1, n):
            pl.semaphore_signal(
                barrier, inc=1, device_id={axis: lax.rem(me + k, n)},
                device_id_type=pl.DeviceIdType.MESH,
            )
    pl.semaphore_wait(barrier, sum(n - 1 for _, _, n in peers))


def send_all(axis, me, n, block_of, dst, send_sems, recv_sems):
    sends = []
    for k in range(1, n):
        peer = lax.rem(me + k, n)
        copy = pltpu.make_async_remote_copy(
            src_ref=block_of(peer),
            dst_ref=dst.at[me],
            send_sem=send_sems.at[k],
            recv_sem=recv_sems.at[k],
            device_id={axis: peer},
            device_id_type=pl.DeviceIdType.MESH,
        )
        copy.start()
        sends.append(copy)
    return sends


def receive_all(axis, me, n, block_of, dst, send_sems, recv_sems, sends):
    for k in range(1, n):
        source = lax.rem(me + n - k, n)
        arrival = pltpu.make_async_remote_copy(
            src_ref=block_of(source),
            dst_ref=dst.at[source],
            send_sem=send_sems.at[k],
            recv_sem=recv_sems.at[k],
            device_id={axis: source},
            device_id_type=pl.DeviceIdType.MESH,
        )
        arrival.wait_recv()
    for copy in sends:
        copy.wait_send()


def project_kernel(req_n, head_n, x_hbm, gain_hbm, w_hbm, cos_ref, sin_ref, len_ref, keys_hbm,
                   values_hbm, q_ref, k_ref, v_ref, inside_ref, keys_ref, values_ref,
                   w_ref, gain_ref, rows_buf, part, pair_buf, mixed, sums_buf, sems, w_sem, key_sem):
    me_head = lax.axis_index("head")
    me_req = lax.axis_index("req")
    chips = req_n // 2
    me_core = lax.rem(me_req, 2)
    me_chip = me_req // 2
    partner = me_req + 1 - 2 * me_core
    w_copy = pltpu.make_async_copy(w_hbm, w_ref, w_sem.at[0])
    w_copy.start()
    x_copy = pltpu.make_async_copy(x_hbm, rows_buf.at[me_head], w_sem.at[1])
    x_copy.start()
    gain_copy = pltpu.make_async_copy(gain_hbm, gain_ref, w_sem.at[2])
    gain_copy.start()
    key_copy = pltpu.make_async_copy(keys_hbm, keys_ref, key_sem.at[0])
    key_copy.start()
    value_copy = pltpu.make_async_copy(values_hbm, values_ref, key_sem.at[1])
    value_copy.start()
    barrier = pltpu.get_barrier_semaphore()
    for k in range(1, head_n):
        pl.semaphore_signal(
            barrier, inc=1, device_id={"head": lax.rem(me_head + k, head_n)},
            device_id_type=pl.DeviceIdType.MESH,
        )
    pl.semaphore_signal(
        barrier, inc=1, device_id={"req": partner}, device_id_type=pl.DeviceIdType.MESH
    )
    for k in range(1, chips):
        pl.semaphore_signal(
            barrier, inc=1, device_id={"req": lax.rem(me_chip + k, chips) * 2 + me_core},
            device_id_type=pl.DeviceIdType.MESH,
        )
    pl.semaphore_wait(barrier, head_n - 1 + chips)
    own = lambda peer: x_hbm
    sends = send_all("head", me_head, head_n, own, rows_buf, sems.at[0], sems.at[1])
    receive_all("head", me_head, head_n, own, rows_buf, sems.at[0], sems.at[1], sends)
    x_copy.wait()
    gain_copy.wait()
    block_rows = x_hbm.shape[0]
    states = rows_buf[...].reshape(head_n * block_rows, x_hbm.shape[1]).astype(jnp.float32)
    scaled = (states * gain_ref[...].astype(jnp.float32)[None, :]).astype(jnp.bfloat16)
    columns = w_ref.shape[1]
    square = jnp.sum(states * states, axis=1, keepdims=True)
    w_copy.wait()
    packed = jnp.concatenate(
        [jnp.dot(scaled, w_ref[...], preferred_element_type=jnp.float32),
         jnp.broadcast_to(square, (square.shape[0], part.shape[-1] - columns))],
        axis=1,
    )
    count = k_ref.shape[0]
    packed = packed.reshape(chips, 2, count, part.shape[-1])
    part[0] = packed[:, 0]
    part[1] = packed[:, 1]
    pair = pltpu.make_async_remote_copy(
        src_ref=part.at[1 - me_core],
        dst_ref=pair_buf,
        send_sem=sems.at[2, 0],
        recv_sem=sems.at[3, 0],
        device_id={"req": partner},
        device_id_type=pl.DeviceIdType.MESH,
    )
    pair.start()
    pair.wait()
    mixed[...] = part[me_core] + pair_buf[...]
    z_n = chips // 2
    me_z, me_x = me_chip // 2, lax.rem(me_chip, 2)
    offsets = sorted(
        [(dz, dx) for dz in range(z_n) for dx in range(2) if dz or dx],
        key=lambda o: -(min(o[0], z_n - o[0]) + 2 * o[1]),
    )
    sends = []
    for k, (dz, dx) in enumerate(offsets, start=1):
        chip = lax.rem(me_z + dz, z_n) * 2 + lax.rem(me_x + dx, 2)
        copy = pltpu.make_async_remote_copy(
            src_ref=mixed.at[chip],
            dst_ref=sums_buf.at[me_chip],
            send_sem=sems.at[2, k],
            recv_sem=sems.at[3, k],
            device_id={"req": chip * 2 + me_core},
            device_id_type=pl.DeviceIdType.MESH,
        )
        copy.start()
        sends.append(copy)
    for k, (dz, dx) in enumerate(offsets, start=1):
        chip = lax.rem(me_z + z_n - dz, z_n) * 2 + lax.rem(me_x + 2 - dx, 2)
        arrival = pltpu.make_async_remote_copy(
            src_ref=mixed.at[chip],
            dst_ref=sums_buf.at[chip],
            send_sem=sems.at[2, k],
            recv_sem=sems.at[3, k],
            device_id={"req": chip * 2 + me_core},
            device_id_type=pl.DeviceIdType.MESH,
        )
        arrival.wait_recv()
    for copy in sends:
        copy.wait_send()
    total = mixed[me_chip]
    for k in range(1, chips):
        total = total + sums_buf[lax.rem(me_chip + chips - k, chips)]
    mean_square = total[:, columns:columns + 1] / D
    projected = total[:, :columns] * lax.rsqrt(mean_square + epsilon)
    cosine, sine = cos_ref[...], sin_ref[...]
    rotated = lambda block: block * cosine + pltpu.roll(block, HD // 2, 1) * sine
    for g in range(GROUP):
        q_ref[g] = rotated(projected[:, g * HD:(g + 1) * HD]).astype(jnp.bfloat16).astype(jnp.float32)
    k_ref[...] = rotated(projected[:, GROUP * HD:(GROUP + 1) * HD]).astype(k_ref.dtype)
    v_ref[...] = projected[:, (GROUP + 1) * HD:].astype(v_ref.dtype)
    slot = lax.broadcasted_iota(jnp.int32, (1, inside_ref.shape[1]), 1)
    for b in range(inside_ref.shape[0]):
        inside_ref[pl.ds(b, 1), :] = (slot < len_ref[b]).astype(inside_ref.dtype)
    key_copy.wait()
    value_copy.wait()


def project(hidden_in, gain, w_qkv, lengths, k_cache, v_cache, req_n, head_n, count):
    rows, width = hidden_in.shape
    columns = w_qkv.shape[1] + 128
    halfway = HD // 2
    frequency = jnp.exp(
        -jnp.log(rope_base) * 2.0 * jnp.arange(halfway, dtype=jnp.float32) / HD
    )
    angles = lengths.astype(jnp.float32)[:, None] * frequency[None, :]
    cosine = jnp.concatenate([jnp.cos(angles), jnp.cos(angles)], axis=1)
    sine = jnp.concatenate([-jnp.sin(angles), jnp.sin(angles)], axis=1)
    return pl.pallas_call(
        functools.partial(project_kernel, req_n, head_n),
        out_shape=(
            jax.ShapeDtypeStruct((GROUP, count, HD), jnp.float32),
            jax.ShapeDtypeStruct((count, HD), jnp.bfloat16),
            jax.ShapeDtypeStruct((count, HD), jnp.bfloat16),
            jax.ShapeDtypeStruct((count, k_cache.shape[1]), jnp.int32),
            jax.ShapeDtypeStruct(k_cache.shape, k_cache.dtype),
            jax.ShapeDtypeStruct(v_cache.shape, v_cache.dtype),
        ),
        in_specs=[pl.BlockSpec(memory_space=pltpu.HBM)] * 3
        + [pl.BlockSpec(memory_space=pltpu.VMEM)] * 2
        + [pl.BlockSpec(memory_space=pltpu.SMEM)]
        + [pl.BlockSpec(memory_space=pl.ANY)] * 2,
        out_specs=(pl.BlockSpec(memory_space=pltpu.VMEM),) * 6,
        scratch_shapes=[
            pltpu.VMEM(w_qkv.shape, w_qkv.dtype),
            pltpu.VMEM(gain.shape, gain.dtype),
            pltpu.VMEM((head_n, rows, width), hidden_in.dtype),
            pltpu.VMEM((2, req_n // 2, count, columns), jnp.float32),
            pltpu.VMEM((req_n // 2, count, columns), jnp.float32),
            pltpu.VMEM((req_n // 2, count, columns), jnp.float32),
            pltpu.VMEM((req_n // 2, count, columns), jnp.float32),
            pltpu.SemaphoreType.DMA((4, max(req_n, head_n))),
            pltpu.SemaphoreType.DMA((3,)),
            pltpu.SemaphoreType.DMA((2,)),
        ],
        compiler_params=pltpu.CompilerParams(
            collective_id=0, has_side_effects=True, vmem_limit_bytes=30 * 1024 * 1024
        ),
    )(
        pltpu.with_memory_space_constraint(hidden_in, pltpu.HBM),
        pltpu.with_memory_space_constraint(gain, pltpu.HBM),
        pltpu.with_memory_space_constraint(w_qkv, pltpu.HBM),
        cosine, sine, pltpu.with_memory_space_constraint(lengths, pltpu.HBM), k_cache, v_cache,
    )


def output_kernel(req_n, head_n, a_ref, w_hbm, s_ref, o_ref, w_ref, att_buf, part, sums_buf,
                  sems, w_sem):
    me_head = lax.axis_index("head")
    me_req = lax.axis_index("req")
    w_copy = pltpu.make_async_copy(w_hbm, w_ref, w_sem)
    w_copy.start()
    greet((("req", me_req, req_n), ("head", me_head, head_n)))
    own = lambda peer: a_ref
    sends = send_all("req", me_req, req_n, own, att_buf, sems.at[0], sems.at[1])
    receive_all("req", me_req, req_n, own, att_buf, sems.at[0], sems.at[1], sends)
    att_buf[me_req] = a_ref[...]
    every = jnp.concatenate(
        [att_buf[s].astype(jnp.float32) for s in range(req_n)], axis=0
    ).astype(jnp.bfloat16)
    w_copy.wait()
    part[...] = jnp.dot(every, w_ref[...], preferred_element_type=jnp.float32)
    rows = o_ref.shape[0]
    chunk = lambda peer: part.at[pl.ds(pl.multiple_of(peer * rows, rows), rows)]
    sends = send_all("head", me_head, head_n, chunk, sums_buf, sems.at[2], sems.at[3])
    receive_all("head", me_head, head_n, chunk, sums_buf, sems.at[2], sems.at[3], sends)
    total = part[pl.ds(pl.multiple_of(me_head * rows, rows), rows), :]
    for k in range(1, head_n):
        total = total + sums_buf[lax.rem(me_head + head_n - k, head_n)]
    o_ref[...] = (s_ref[...].astype(jnp.float32) + total).astype(o_ref.dtype)


def output_block(attended, w_out, hidden_in, req_n, head_n):
    count, width = attended.shape
    rows, columns = hidden_in.shape
    return pl.pallas_call(
        functools.partial(output_kernel, req_n, head_n),
        out_shape=jax.ShapeDtypeStruct((rows, columns), hidden_in.dtype),
        in_specs=[
            pl.BlockSpec(memory_space=pltpu.VMEM),
            pl.BlockSpec(memory_space=pl.ANY),
            pl.BlockSpec(memory_space=pltpu.VMEM),
        ],
        out_specs=pl.BlockSpec(memory_space=pltpu.VMEM),
        scratch_shapes=[
            pltpu.VMEM(w_out.shape, w_out.dtype),
            pltpu.VMEM((req_n, count, width), attended.dtype),
            pltpu.VMEM((head_n * rows, columns), jnp.float32),
            pltpu.VMEM((head_n, rows, columns), jnp.float32),
            pltpu.SemaphoreType.DMA((4, max(req_n, head_n))),
            pltpu.SemaphoreType.DMA(()),
        ],
        compiler_params=pltpu.CompilerParams(
            collective_id=1, has_side_effects=True, vmem_limit_bytes=12 * 1024 * 1024
        ),
    )(attended, w_out, hidden_in)


def local(req_n, head_n, hidden_in, attn_gain, w_qkv, w_out, k_cache, v_cache, lengths):
    own_count = k_cache.shape[0]
    queries, new_keys, new_values, inside, k_cache, v_cache = project(
        hidden_in, attn_gain, w_qkv, lengths, k_cache, v_cache, req_n, head_n, own_count
    )
    slots = k_cache.shape[1]
    local_heads = k_cache.shape[2] // HD
    queries = jnp.transpose(queries.astype(jnp.bfloat16), (1, 0, 2))[:, None]
    new_keys = new_keys[:, None]
    new_values = new_values[:, None]
    cached_keys = k_cache.reshape(own_count, slots, local_heads, HD)
    cached_values = v_cache.reshape(own_count, slots, local_heads, HD)
    factor = HD ** (-0.5)
    attended = attend_padded(
        queries, new_keys, new_values, cached_keys, cached_values, inside != 0, factor
    )
    flat_rows = attended.reshape(own_count, local_heads * GROUP * HD)
    return output_block(flat_rows, w_out, hidden_in, req_n, head_n)


def solution(mesh):
    return jax.shard_map(
        functools.partial(local, mesh.shape["req"], mesh.shape["head"]),
        mesh=mesh,
        in_specs=(
            P("head", "req"),
            P("req"),
            P("req", "head"),
            P("head", "req"),
            P("req", None, "head"),
            P("req", None, "head"),
            P("req"),
        ),
        out_specs=P("head", "req"),
        check_vma=False,
    )
```

```python
import functools
import itertools

import jax
import jax.numpy as jnp
from jax import lax
from jax.experimental import pallas as pl
from jax.experimental.pallas import tpu as pltpu
from jax.sharding import PartitionSpec as P

D = 8192
GROUP = 8
HD = 128


epsilon = 1e-05
rope_base = 500000.0


def rotate(vectors, positions):
    halfway = vectors.shape[-1] // 2
    frequency = jnp.exp(
        -jnp.log(rope_base) * 2.0 * jnp.arange(halfway, dtype=jnp.float32) / vectors.shape[-1]
    )
    angles = positions.astype(jnp.float32)[:, None] * frequency[None, :]
    target_shape = (angles.shape[0],) + (1,) * (vectors.ndim - 2) + (halfway,)
    cosine = jnp.cos(angles).reshape(target_shape)
    sine_part = jnp.sin(angles).reshape(target_shape)
    first = vectors[..., :halfway]
    second = vectors[..., halfway:]
    return jnp.concatenate(
        [first * cosine - second * sine_part, second * cosine + first * sine_part], axis=-1
    )


def own_part(own_score, running, totals, new_values):
    own_prob = lax.optimization_barrier(
        (jnp.exp(own_score - running) / totals).astype(jnp.bfloat16)
    )
    return own_prob.astype(jnp.float32)[..., None] * new_values.astype(jnp.float32)[:, :, None, :]


def attend_padded(queries, new_keys, new_values, cached_keys, cached_values, inside, factor):
    scores = (
        jnp.einsum("rkgd,rpkd->rkgp", queries, cached_keys, preferred_element_type=jnp.float32)
        * factor
    )
    scores = jnp.where(inside[:, None, None, :], scores, -1e30)
    own_score = (
        jnp.einsum("rkgd,rkd->rkg", queries, new_keys, preferred_element_type=jnp.float32) * factor
    )
    running = jnp.maximum(jnp.max(scores, axis=3), own_score)
    weights = jnp.where(inside[:, None, None, :], jnp.exp(scores - running[..., None]), 0.0)
    totals = jnp.sum(weights, axis=3) + jnp.exp(own_score - running)
    probs = (weights / totals[..., None]).astype(jnp.bfloat16)
    mixed = jnp.einsum("rkgp,rpkd->rkgd", probs, cached_values, preferred_element_type=jnp.float32)
    mixed = mixed + own_part(own_score, running, totals, new_values)
    return mixed.astype(jnp.bfloat16)


def greet(peers):
    barrier = pltpu.get_barrier_semaphore()
    for axis, me, n in peers:
        for k in range(1, n):
            pl.semaphore_signal(
                barrier, inc=1, device_id={axis: lax.rem(me + k, n)},
                device_id_type=pl.DeviceIdType.MESH,
            )
    pl.semaphore_wait(barrier, sum(n - 1 for _, _, n in peers))


def ordered_peers(me, digits):
    sizes = [size for size, _ in digits]
    mine, rest = [], me
    for size in reversed(sizes):
        mine.append(lax.rem(rest, size))
        rest = rest // size
    mine = mine[::-1]
    offsets = [o for o in itertools.product(*[range(s) for s in sizes]) if any(o)]
    offsets.sort(key=lambda o: -sum(w * min(d, s - d) for d, (s, w) in zip(o, digits)))

    def compose(o, forward):
        index = 0
        for d, m, s in zip(o, mine, sizes):
            index = index * s + lax.rem(m + (d if forward else s - d), s)
        return index

    return [(compose(o, True), compose(o, False)) for o in offsets]


def send_all(axis, peers, block_of, dst, send_sems, recv_sems, me):
    sends = []
    for k, (peer, _) in enumerate(peers, start=1):
        copy = pltpu.make_async_remote_copy(
            src_ref=block_of(peer),
            dst_ref=dst.at[me],
            send_sem=send_sems.at[k],
            recv_sem=recv_sems.at[k],
            device_id={axis: peer},
            device_id_type=pl.DeviceIdType.MESH,
        )
        copy.start()
        sends.append(copy)
    return sends


def receive_all(axis, peers, block_of, dst, send_sems, recv_sems, sends):
    for k, (_, source) in enumerate(peers, start=1):
        arrival = pltpu.make_async_remote_copy(
            src_ref=block_of(source),
            dst_ref=dst.at[source],
            send_sem=send_sems.at[k],
            recv_sem=recv_sems.at[k],
            device_id={axis: source},
            device_id_type=pl.DeviceIdType.MESH,
        )
        arrival.wait_recv()
    for copy in sends:
        copy.wait_send()


def project_kernel(req_n, head_n, x_hbm, gain_hbm, w_hbm, cos_ref, sin_ref, len_ref, keys_hbm,
                   values_hbm, q_ref, k_ref, v_ref, inside_ref, keys_ref, values_ref,
                   w_ref, gain_ref, rows_buf, part, pair_buf, mixed, sums_buf, sems, w_sem, key_sem):
    me_head = lax.axis_index("head")
    me_req = lax.axis_index("req")
    chips = req_n // 2
    me_core = lax.rem(me_req, 2)
    me_chip = me_req // 2
    partner = me_req + 1 - 2 * me_core
    w_copy = pltpu.make_async_copy(w_hbm, w_ref, w_sem.at[0])
    w_copy.start()
    x_copy = pltpu.make_async_copy(x_hbm, rows_buf.at[me_head], w_sem.at[1])
    x_copy.start()
    gain_copy = pltpu.make_async_copy(gain_hbm, gain_ref, w_sem.at[2])
    gain_copy.start()
    key_copy = pltpu.make_async_copy(keys_hbm, keys_ref, key_sem.at[0])
    key_copy.start()
    value_copy = pltpu.make_async_copy(values_hbm, values_ref, key_sem.at[1])
    value_copy.start()
    barrier = pltpu.get_barrier_semaphore()
    for k in range(1, head_n):
        pl.semaphore_signal(
            barrier, inc=1, device_id={"head": lax.rem(me_head + k, head_n)},
            device_id_type=pl.DeviceIdType.MESH,
        )
    pl.semaphore_signal(
        barrier, inc=1, device_id={"req": partner}, device_id_type=pl.DeviceIdType.MESH
    )
    for k in range(1, chips):
        pl.semaphore_signal(
            barrier, inc=1, device_id={"req": lax.rem(me_chip + k, chips) * 2 + me_core},
            device_id_type=pl.DeviceIdType.MESH,
        )
    pl.semaphore_wait(barrier, head_n - 1 + chips)
    own = lambda peer: x_hbm
    head_peers = ordered_peers(me_head, ((head_n // 2, 1), (2, 1)))
    sends = send_all("head", head_peers, own, rows_buf, sems.at[0], sems.at[1], me_head)
    receive_all("head", head_peers, own, rows_buf, sems.at[0], sems.at[1], sends)
    x_copy.wait()
    gain_copy.wait()
    block_rows = x_hbm.shape[0]
    states = rows_buf[...].reshape(head_n * block_rows, x_hbm.shape[1]).astype(jnp.float32)
    scaled = (states * gain_ref[...].astype(jnp.float32)[None, :]).astype(jnp.bfloat16)
    columns = w_ref.shape[1]
    square = jnp.sum(states * states, axis=1, keepdims=True)
    w_copy.wait()
    packed = jnp.concatenate(
        [jnp.dot(scaled, w_ref[...], preferred_element_type=jnp.float32),
         jnp.broadcast_to(square, (square.shape[0], part.shape[-1] - columns))],
        axis=1,
    )
    count = k_ref.shape[0]
    packed = packed.reshape(chips, 2, count, part.shape[-1])
    part[0] = packed[:, 0]
    part[1] = packed[:, 1]
    pair = pltpu.make_async_remote_copy(
        src_ref=part.at[1 - me_core],
        dst_ref=pair_buf,
        send_sem=sems.at[2, 0],
        recv_sem=sems.at[3, 0],
        device_id={"req": partner},
        device_id_type=pl.DeviceIdType.MESH,
    )
    pair.start()
    pair.wait()
    mixed[...] = part[me_core] + pair_buf[...]
    z_n = chips // 2
    me_z, me_x = me_chip // 2, lax.rem(me_chip, 2)
    offsets = sorted(
        [(dz, dx) for dz in range(z_n) for dx in range(2) if dz or dx],
        key=lambda o: -(min(o[0], z_n - o[0]) + 2 * o[1]),
    )
    sends = []
    for k, (dz, dx) in enumerate(offsets, start=1):
        chip = lax.rem(me_z + dz, z_n) * 2 + lax.rem(me_x + dx, 2)
        copy = pltpu.make_async_remote_copy(
            src_ref=mixed.at[chip],
            dst_ref=sums_buf.at[me_chip],
            send_sem=sems.at[2, k],
            recv_sem=sems.at[3, k],
            device_id={"req": chip * 2 + me_core},
            device_id_type=pl.DeviceIdType.MESH,
        )
        copy.start()
        sends.append(copy)
    for k, (dz, dx) in enumerate(offsets, start=1):
        chip = lax.rem(me_z + z_n - dz, z_n) * 2 + lax.rem(me_x + 2 - dx, 2)
        arrival = pltpu.make_async_remote_copy(
            src_ref=mixed.at[chip],
            dst_ref=sums_buf.at[chip],
            send_sem=sems.at[2, k],
            recv_sem=sems.at[3, k],
            device_id={"req": chip * 2 + me_core},
            device_id_type=pl.DeviceIdType.MESH,
        )
        arrival.wait_recv()
    for copy in sends:
        copy.wait_send()
    total = mixed[me_chip]
    for k in range(1, chips):
        total = total + sums_buf[lax.rem(me_chip + chips - k, chips)]
    mean_square = total[:, columns:columns + 1] / D
    projected = total[:, :columns] * lax.rsqrt(mean_square + epsilon)
    cosine, sine = cos_ref[...], sin_ref[...]
    rotated = lambda block: block * cosine + pltpu.roll(block, HD // 2, 1) * sine
    for g in range(GROUP):
        q_ref[g] = rotated(projected[:, g * HD:(g + 1) * HD]).astype(jnp.bfloat16).astype(jnp.float32)
    k_ref[...] = rotated(projected[:, GROUP * HD:(GROUP + 1) * HD]).astype(k_ref.dtype)
    v_ref[...] = projected[:, (GROUP + 1) * HD:].astype(v_ref.dtype)
    slot = lax.broadcasted_iota(jnp.int32, (1, inside_ref.shape[1]), 1)
    for b in range(inside_ref.shape[0]):
        inside_ref[pl.ds(b, 1), :] = (slot < len_ref[b]).astype(inside_ref.dtype)
    key_copy.wait()
    value_copy.wait()


def project(hidden_in, gain, w_qkv, lengths, k_cache, v_cache, req_n, head_n, count):
    rows, width = hidden_in.shape
    columns = w_qkv.shape[1] + 128
    halfway = HD // 2
    frequency = jnp.exp(
        -jnp.log(rope_base) * 2.0 * jnp.arange(halfway, dtype=jnp.float32) / HD
    )
    angles = lengths.astype(jnp.float32)[:, None] * frequency[None, :]
    cosine = jnp.concatenate([jnp.cos(angles), jnp.cos(angles)], axis=1)
    sine = jnp.concatenate([-jnp.sin(angles), jnp.sin(angles)], axis=1)
    return pl.pallas_call(
        functools.partial(project_kernel, req_n, head_n),
        out_shape=(
            jax.ShapeDtypeStruct((GROUP, count, HD), jnp.float32),
            jax.ShapeDtypeStruct((count, HD), jnp.bfloat16),
            jax.ShapeDtypeStruct((count, HD), jnp.bfloat16),
            jax.ShapeDtypeStruct((count, k_cache.shape[1]), jnp.int32),
            jax.ShapeDtypeStruct(k_cache.shape, k_cache.dtype),
            jax.ShapeDtypeStruct(v_cache.shape, v_cache.dtype),
        ),
        in_specs=[pl.BlockSpec(memory_space=pltpu.HBM)] * 3
        + [pl.BlockSpec(memory_space=pltpu.VMEM)] * 2
        + [pl.BlockSpec(memory_space=pltpu.SMEM)]
        + [pl.BlockSpec(memory_space=pl.ANY)] * 2,
        out_specs=(pl.BlockSpec(memory_space=pltpu.VMEM),) * 6,
        scratch_shapes=[
            pltpu.VMEM(w_qkv.shape, w_qkv.dtype),
            pltpu.VMEM(gain.shape, gain.dtype),
            pltpu.VMEM((head_n, rows, width), hidden_in.dtype),
            pltpu.VMEM((2, req_n // 2, count, columns), jnp.float32),
            pltpu.VMEM((req_n // 2, count, columns), jnp.float32),
            pltpu.VMEM((req_n // 2, count, columns), jnp.float32),
            pltpu.VMEM((req_n // 2, count, columns), jnp.float32),
            pltpu.SemaphoreType.DMA((4, max(req_n, head_n))),
            pltpu.SemaphoreType.DMA((3,)),
            pltpu.SemaphoreType.DMA((2,)),
        ],
        compiler_params=pltpu.CompilerParams(
            collective_id=0, has_side_effects=True, vmem_limit_bytes=30 * 1024 * 1024
        ),
    )(
        pltpu.with_memory_space_constraint(hidden_in, pltpu.HBM),
        pltpu.with_memory_space_constraint(gain, pltpu.HBM),
        pltpu.with_memory_space_constraint(w_qkv, pltpu.HBM),
        cosine, sine, pltpu.with_memory_space_constraint(lengths, pltpu.HBM), k_cache, v_cache,
    )


def output_kernel(req_n, head_n, a_ref, w_hbm, s_ref, o_ref, w_ref, att_buf, part, sums_buf,
                  sems, w_sem):
    me_head = lax.axis_index("head")
    me_req = lax.axis_index("req")
    w_copy = pltpu.make_async_copy(w_hbm, w_ref, w_sem)
    w_copy.start()
    greet((("req", me_req, req_n), ("head", me_head, head_n)))
    own = lambda peer: a_ref
    req_peers = ordered_peers(me_req, ((req_n // 4, 1), (2, 2), (2, 0.5)))
    sends = send_all("req", req_peers, own, att_buf, sems.at[0], sems.at[1], me_req)
    receive_all("req", req_peers, own, att_buf, sems.at[0], sems.at[1], sends)
    att_buf[me_req] = a_ref[...]
    every = jnp.concatenate(
        [att_buf[s].astype(jnp.float32) for s in range(req_n)], axis=0
    ).astype(jnp.bfloat16)
    w_copy.wait()
    part[...] = jnp.dot(every, w_ref[...], preferred_element_type=jnp.float32)
    rows = o_ref.shape[0]
    chunk = lambda peer: part.at[pl.ds(pl.multiple_of(peer * rows, rows), rows)]
    head_peers = ordered_peers(me_head, ((head_n // 2, 1), (2, 1)))
    sends = send_all("head", head_peers, chunk, sums_buf, sems.at[2], sems.at[3], me_head)
    receive_all("head", head_peers, chunk, sums_buf, sems.at[2], sems.at[3], sends)
    total = part[pl.ds(pl.multiple_of(me_head * rows, rows), rows), :]
    for k in range(1, head_n):
        total = total + sums_buf[lax.rem(me_head + head_n - k, head_n)]
    o_ref[...] = (s_ref[...].astype(jnp.float32) + total).astype(o_ref.dtype)


def output_block(attended, w_out, hidden_in, req_n, head_n):
    count, width = attended.shape
    rows, columns = hidden_in.shape
    return pl.pallas_call(
        functools.partial(output_kernel, req_n, head_n),
        out_shape=jax.ShapeDtypeStruct((rows, columns), hidden_in.dtype),
        in_specs=[
            pl.BlockSpec(memory_space=pltpu.VMEM),
            pl.BlockSpec(memory_space=pl.ANY),
            pl.BlockSpec(memory_space=pltpu.VMEM),
        ],
        out_specs=pl.BlockSpec(memory_space=pltpu.VMEM),
        scratch_shapes=[
            pltpu.VMEM(w_out.shape, w_out.dtype),
            pltpu.VMEM((req_n, count, width), attended.dtype),
            pltpu.VMEM((head_n * rows, columns), jnp.float32),
            pltpu.VMEM((head_n, rows, columns), jnp.float32),
            pltpu.SemaphoreType.DMA((4, max(req_n, head_n))),
            pltpu.SemaphoreType.DMA(()),
        ],
        compiler_params=pltpu.CompilerParams(
            collective_id=1, has_side_effects=True, vmem_limit_bytes=12 * 1024 * 1024
        ),
    )(attended, w_out, hidden_in)


def local(req_n, head_n, hidden_in, attn_gain, w_qkv, w_out, k_cache, v_cache, lengths):
    own_count = k_cache.shape[0]
    queries, new_keys, new_values, inside, k_cache, v_cache = project(
        hidden_in, attn_gain, w_qkv, lengths, k_cache, v_cache, req_n, head_n, own_count
    )
    slots = k_cache.shape[1]
    local_heads = k_cache.shape[2] // HD
    queries = jnp.transpose(queries.astype(jnp.bfloat16), (1, 0, 2))[:, None]
    new_keys = new_keys[:, None]
    new_values = new_values[:, None]
    cached_keys = k_cache.reshape(own_count, slots, local_heads, HD)
    cached_values = v_cache.reshape(own_count, slots, local_heads, HD)
    factor = HD ** (-0.5)
    attended = attend_padded(
        queries, new_keys, new_values, cached_keys, cached_values, inside != 0, factor
    )
    flat_rows = attended.reshape(own_count, local_heads * GROUP * HD)
    return output_block(flat_rows, w_out, hidden_in, req_n, head_n)


def solution(mesh):
    return jax.shard_map(
        functools.partial(local, mesh.shape["req"], mesh.shape["head"]),
        mesh=mesh,
        in_specs=(
            P("head", "req"),
            P("req"),
            P("req", "head"),
            P("head", "req"),
            P("req", None, "head"),
            P("req", None, "head"),
            P("req"),
        ),
        out_specs=P("head", "req"),
        check_vma=False,
    )
```

```python
import functools
import itertools

import jax
import jax.numpy as jnp
from jax import lax
from jax.experimental import pallas as pl
from jax.experimental.pallas import tpu as pltpu
from jax.sharding import PartitionSpec as P

D = 8192
GROUP = 8
HD = 128


epsilon = 1e-05
rope_base = 500000.0


def rotate(vectors, positions):
    halfway = vectors.shape[-1] // 2
    frequency = jnp.exp(
        -jnp.log(rope_base) * 2.0 * jnp.arange(halfway, dtype=jnp.float32) / vectors.shape[-1]
    )
    angles = positions.astype(jnp.float32)[:, None] * frequency[None, :]
    target_shape = (angles.shape[0],) + (1,) * (vectors.ndim - 2) + (halfway,)
    cosine = jnp.cos(angles).reshape(target_shape)
    sine_part = jnp.sin(angles).reshape(target_shape)
    first = vectors[..., :halfway]
    second = vectors[..., halfway:]
    return jnp.concatenate(
        [first * cosine - second * sine_part, second * cosine + first * sine_part], axis=-1
    )


def own_part(own_score, running, totals, new_values):
    own_prob = lax.optimization_barrier(
        (jnp.exp(own_score - running) / totals).astype(jnp.bfloat16)
    )
    return own_prob.astype(jnp.float32)[..., None] * new_values.astype(jnp.float32)[:, :, None, :]


def attend_padded(queries, new_keys, new_values, cached_keys, cached_values, inside, factor):
    scores = (
        jnp.einsum("rkgd,rpkd->rkgp", queries, cached_keys, preferred_element_type=jnp.float32)
        * factor
    )
    scores = jnp.where(inside[:, None, None, :], scores, -1e30)
    own_score = (
        jnp.einsum("rkgd,rkd->rkg", queries, new_keys, preferred_element_type=jnp.float32) * factor
    )
    running = jnp.maximum(jnp.max(scores, axis=3), own_score)
    weights = jnp.where(inside[:, None, None, :], jnp.exp(scores - running[..., None]), 0.0)
    totals = jnp.sum(weights, axis=3) + jnp.exp(own_score - running)
    probs = (weights / totals[..., None]).astype(jnp.bfloat16)
    mixed = jnp.einsum("rkgp,rpkd->rkgd", probs, cached_values, preferred_element_type=jnp.float32)
    mixed = mixed + own_part(own_score, running, totals, new_values)
    return mixed.astype(jnp.bfloat16)


def greet(peers):
    barrier = pltpu.get_barrier_semaphore()
    for axis, ordered in peers:
        for peer, _ in ordered:
            pl.semaphore_signal(
                barrier, inc=1, device_id={axis: peer}, device_id_type=pl.DeviceIdType.MESH
            )
    pl.semaphore_wait(barrier, sum(len(ordered) for _, ordered in peers))


def ordered_peers(me, digits):
    sizes = [size for size, _ in digits]
    mine, rest = [], me
    for size in reversed(sizes):
        mine.append(lax.rem(rest, size))
        rest = rest // size
    mine = mine[::-1]
    offsets = [o for o in itertools.product(*[range(s) for s in sizes]) if any(o)]
    offsets.sort(key=lambda o: -sum(w * min(d, s - d) for d, (s, w) in zip(o, digits)))

    def compose(o, forward):
        index = 0
        for d, m, s in zip(o, mine, sizes):
            index = index * s + lax.rem(m + (d if forward else s - d), s)
        return index

    return [(compose(o, True), compose(o, False)) for o in offsets]


def send_all(axis, peers, block_of, dst, send_sems, recv_sems, me):
    sends = []
    for k, (peer, _) in enumerate(peers, start=1):
        copy = pltpu.make_async_remote_copy(
            src_ref=block_of(peer),
            dst_ref=dst.at[me],
            send_sem=send_sems.at[k],
            recv_sem=recv_sems.at[k],
            device_id={axis: peer},
            device_id_type=pl.DeviceIdType.MESH,
        )
        copy.start()
        sends.append(copy)
    return sends


def receive_all(axis, peers, block_of, dst, send_sems, recv_sems, sends):
    for k, (_, source) in enumerate(peers, start=1):
        arrival = pltpu.make_async_remote_copy(
            src_ref=block_of(source),
            dst_ref=dst.at[source],
            send_sem=send_sems.at[k],
            recv_sem=recv_sems.at[k],
            device_id={axis: source},
            device_id_type=pl.DeviceIdType.MESH,
        )
        arrival.wait_recv()
    for copy in sends:
        copy.wait_send()


def project_kernel(req_n, head_n, x_hbm, gain_hbm, w_hbm, cos_ref, sin_ref, len_ref, keys_hbm,
                   values_hbm, q_ref, k_ref, v_ref, inside_ref, keys_ref, values_ref,
                   w_ref, gain_ref, rows_buf, part, pair_buf, mixed, sums_buf, sems, w_sem, key_sem):
    me_head = lax.axis_index("head")
    me_req = lax.axis_index("req")
    chips = req_n // 2
    me_core = lax.rem(me_req, 2)
    me_chip = me_req // 2
    partner = me_req + 1 - 2 * me_core
    w_copy = pltpu.make_async_copy(w_hbm, w_ref, w_sem.at[0])
    w_copy.start()
    x_copy = pltpu.make_async_copy(x_hbm, rows_buf.at[me_head], w_sem.at[1])
    x_copy.start()
    gain_copy = pltpu.make_async_copy(gain_hbm, gain_ref, w_sem.at[2])
    gain_copy.start()
    key_copy = pltpu.make_async_copy(keys_hbm, keys_ref, key_sem.at[0])
    key_copy.start()
    value_copy = pltpu.make_async_copy(values_hbm, values_ref, key_sem.at[1])
    value_copy.start()
    chip_peers = [
        (chip * 2 + me_core, None)
        for chip, _ in ordered_peers(me_chip, ((chips // 2, 1), (2, 2)))
    ]
    head_peers = ordered_peers(me_head, ((head_n // 2, 1), (2, 1)))
    greet((("req", chip_peers), ("head", head_peers), ("req", [(partner, None)])))
    own = lambda peer: x_hbm
    sends = send_all("head", head_peers, own, rows_buf, sems.at[0], sems.at[1], me_head)
    receive_all("head", head_peers, own, rows_buf, sems.at[0], sems.at[1], sends)
    x_copy.wait()
    gain_copy.wait()
    block_rows = x_hbm.shape[0]
    states = rows_buf[...].reshape(head_n * block_rows, x_hbm.shape[1]).astype(jnp.float32)
    scaled = (states * gain_ref[...].astype(jnp.float32)[None, :]).astype(jnp.bfloat16)
    columns = w_ref.shape[1]
    square = jnp.sum(states * states, axis=1, keepdims=True)
    w_copy.wait()
    packed = jnp.concatenate(
        [jnp.dot(scaled, w_ref[...], preferred_element_type=jnp.float32),
         jnp.broadcast_to(square, (square.shape[0], part.shape[-1] - columns))],
        axis=1,
    )
    count = k_ref.shape[0]
    packed = packed.reshape(chips, 2, count, part.shape[-1])
    part[0] = packed[:, 0]
    part[1] = packed[:, 1]
    pair = pltpu.make_async_remote_copy(
        src_ref=part.at[1 - me_core],
        dst_ref=pair_buf,
        send_sem=sems.at[2, 0],
        recv_sem=sems.at[3, 0],
        device_id={"req": partner},
        device_id_type=pl.DeviceIdType.MESH,
    )
    pair.start()
    pair.wait()
    mixed[...] = part[me_core] + pair_buf[...]
    z_n = chips // 2
    me_z, me_x = me_chip // 2, lax.rem(me_chip, 2)
    offsets = sorted(
        [(dz, dx) for dz in range(z_n) for dx in range(2) if dz or dx],
        key=lambda o: -(min(o[0], z_n - o[0]) + 2 * o[1]),
    )
    sends = []
    for k, (dz, dx) in enumerate(offsets, start=1):
        chip = lax.rem(me_z + dz, z_n) * 2 + lax.rem(me_x + dx, 2)
        copy = pltpu.make_async_remote_copy(
            src_ref=mixed.at[chip],
            dst_ref=sums_buf.at[me_chip],
            send_sem=sems.at[2, k],
            recv_sem=sems.at[3, k],
            device_id={"req": chip * 2 + me_core},
            device_id_type=pl.DeviceIdType.MESH,
        )
        copy.start()
        sends.append(copy)
    for k, (dz, dx) in enumerate(offsets, start=1):
        chip = lax.rem(me_z + z_n - dz, z_n) * 2 + lax.rem(me_x + 2 - dx, 2)
        arrival = pltpu.make_async_remote_copy(
            src_ref=mixed.at[chip],
            dst_ref=sums_buf.at[chip],
            send_sem=sems.at[2, k],
            recv_sem=sems.at[3, k],
            device_id={"req": chip * 2 + me_core},
            device_id_type=pl.DeviceIdType.MESH,
        )
        arrival.wait_recv()
    for copy in sends:
        copy.wait_send()
    total = mixed[me_chip]
    for k in range(1, chips):
        total = total + sums_buf[lax.rem(me_chip + chips - k, chips)]
    mean_square = total[:, columns:columns + 1] / D
    projected = total[:, :columns] * lax.rsqrt(mean_square + epsilon)
    cosine, sine = cos_ref[...], sin_ref[...]
    rotated = lambda block: block * cosine + pltpu.roll(block, HD // 2, 1) * sine
    for g in range(GROUP):
        q_ref[g] = rotated(projected[:, g * HD:(g + 1) * HD]).astype(jnp.bfloat16).astype(jnp.float32)
    k_ref[...] = rotated(projected[:, GROUP * HD:(GROUP + 1) * HD]).astype(k_ref.dtype)
    v_ref[...] = projected[:, (GROUP + 1) * HD:].astype(v_ref.dtype)
    slot = lax.broadcasted_iota(jnp.int32, (1, inside_ref.shape[1]), 1)
    for b in range(inside_ref.shape[0]):
        inside_ref[pl.ds(b, 1), :] = (slot < len_ref[b]).astype(inside_ref.dtype)
    key_copy.wait()
    value_copy.wait()


def project(hidden_in, gain, w_qkv, lengths, k_cache, v_cache, req_n, head_n, count):
    rows, width = hidden_in.shape
    columns = w_qkv.shape[1] + 128
    halfway = HD // 2
    frequency = jnp.exp(
        -jnp.log(rope_base) * 2.0 * jnp.arange(halfway, dtype=jnp.float32) / HD
    )
    angles = lengths.astype(jnp.float32)[:, None] * frequency[None, :]
    cosine = jnp.concatenate([jnp.cos(angles), jnp.cos(angles)], axis=1)
    sine = jnp.concatenate([-jnp.sin(angles), jnp.sin(angles)], axis=1)
    return pl.pallas_call(
        functools.partial(project_kernel, req_n, head_n),
        out_shape=(
            jax.ShapeDtypeStruct((GROUP, count, HD), jnp.float32),
            jax.ShapeDtypeStruct((count, HD), jnp.bfloat16),
            jax.ShapeDtypeStruct((count, HD), jnp.bfloat16),
            jax.ShapeDtypeStruct((count, k_cache.shape[1]), jnp.int32),
            jax.ShapeDtypeStruct(k_cache.shape, k_cache.dtype),
            jax.ShapeDtypeStruct(v_cache.shape, v_cache.dtype),
        ),
        in_specs=[pl.BlockSpec(memory_space=pltpu.HBM)] * 3
        + [pl.BlockSpec(memory_space=pltpu.VMEM)] * 2
        + [pl.BlockSpec(memory_space=pltpu.SMEM)]
        + [pl.BlockSpec(memory_space=pl.ANY)] * 2,
        out_specs=(pl.BlockSpec(memory_space=pltpu.VMEM),) * 6,
        scratch_shapes=[
            pltpu.VMEM(w_qkv.shape, w_qkv.dtype),
            pltpu.VMEM(gain.shape, gain.dtype),
            pltpu.VMEM((head_n, rows, width), hidden_in.dtype),
            pltpu.VMEM((2, req_n // 2, count, columns), jnp.float32),
            pltpu.VMEM((req_n // 2, count, columns), jnp.float32),
            pltpu.VMEM((req_n // 2, count, columns), jnp.float32),
            pltpu.VMEM((req_n // 2, count, columns), jnp.float32),
            pltpu.SemaphoreType.DMA((4, max(req_n, head_n))),
            pltpu.SemaphoreType.DMA((3,)),
            pltpu.SemaphoreType.DMA((2,)),
        ],
        compiler_params=pltpu.CompilerParams(
            collective_id=0, has_side_effects=True, vmem_limit_bytes=30 * 1024 * 1024
        ),
    )(
        pltpu.with_memory_space_constraint(hidden_in, pltpu.HBM),
        pltpu.with_memory_space_constraint(gain, pltpu.HBM),
        pltpu.with_memory_space_constraint(w_qkv, pltpu.HBM),
        cosine, sine, pltpu.with_memory_space_constraint(lengths, pltpu.HBM), k_cache, v_cache,
    )


def output_kernel(req_n, head_n, a_ref, w_hbm, s_ref, o_ref, w_ref, att_buf, part, sums_buf,
                  sems, w_sem):
    me_head = lax.axis_index("head")
    me_req = lax.axis_index("req")
    w_copy = pltpu.make_async_copy(w_hbm, w_ref, w_sem)
    w_copy.start()
    req_peers = ordered_peers(me_req, ((req_n // 4, 1), (2, 2), (2, 0.5)))
    head_peers = ordered_peers(me_head, ((head_n // 2, 1), (2, 1)))
    greet((("req", req_peers), ("head", head_peers)))
    own = lambda peer: a_ref
    sends = send_all("req", req_peers, own, att_buf, sems.at[0], sems.at[1], me_req)
    receive_all("req", req_peers, own, att_buf, sems.at[0], sems.at[1], sends)
    att_buf[me_req] = a_ref[...]
    every = jnp.concatenate(
        [att_buf[s].astype(jnp.float32) for s in range(req_n)], axis=0
    ).astype(jnp.bfloat16)
    w_copy.wait()
    part[...] = jnp.dot(every, w_ref[...], preferred_element_type=jnp.float32)
    rows = o_ref.shape[0]
    chunk = lambda peer: part.at[pl.ds(pl.multiple_of(peer * rows, rows), rows)]
    head_peers = ordered_peers(me_head, ((head_n // 2, 1), (2, 1)))
    sends = send_all("head", head_peers, chunk, sums_buf, sems.at[2], sems.at[3], me_head)
    receive_all("head", head_peers, chunk, sums_buf, sems.at[2], sems.at[3], sends)
    total = part[pl.ds(pl.multiple_of(me_head * rows, rows), rows), :]
    for k in range(1, head_n):
        total = total + sums_buf[lax.rem(me_head + head_n - k, head_n)]
    o_ref[...] = (s_ref[...].astype(jnp.float32) + total).astype(o_ref.dtype)


def output_block(attended, w_out, hidden_in, req_n, head_n):
    count, width = attended.shape
    rows, columns = hidden_in.shape
    return pl.pallas_call(
        functools.partial(output_kernel, req_n, head_n),
        out_shape=jax.ShapeDtypeStruct((rows, columns), hidden_in.dtype),
        in_specs=[
            pl.BlockSpec(memory_space=pltpu.VMEM),
            pl.BlockSpec(memory_space=pl.ANY),
            pl.BlockSpec(memory_space=pltpu.VMEM),
        ],
        out_specs=pl.BlockSpec(memory_space=pltpu.VMEM),
        scratch_shapes=[
            pltpu.VMEM(w_out.shape, w_out.dtype),
            pltpu.VMEM((req_n, count, width), attended.dtype),
            pltpu.VMEM((head_n * rows, columns), jnp.float32),
            pltpu.VMEM((head_n, rows, columns), jnp.float32),
            pltpu.SemaphoreType.DMA((4, max(req_n, head_n))),
            pltpu.SemaphoreType.DMA(()),
        ],
        compiler_params=pltpu.CompilerParams(
            collective_id=1, has_side_effects=True, vmem_limit_bytes=12 * 1024 * 1024
        ),
    )(attended, w_out, hidden_in)


def local(req_n, head_n, hidden_in, attn_gain, w_qkv, w_out, k_cache, v_cache, lengths):
    own_count = k_cache.shape[0]
    queries, new_keys, new_values, inside, k_cache, v_cache = project(
        hidden_in, attn_gain, w_qkv, lengths, k_cache, v_cache, req_n, head_n, own_count
    )
    slots = k_cache.shape[1]
    local_heads = k_cache.shape[2] // HD
    queries = jnp.transpose(queries.astype(jnp.bfloat16), (1, 0, 2))[:, None]
    new_keys = new_keys[:, None]
    new_values = new_values[:, None]
    cached_keys = k_cache.reshape(own_count, slots, local_heads, HD)
    cached_values = v_cache.reshape(own_count, slots, local_heads, HD)
    factor = HD ** (-0.5)
    attended = attend_padded(
        queries, new_keys, new_values, cached_keys, cached_values, inside != 0, factor
    )
    flat_rows = attended.reshape(own_count, local_heads * GROUP * HD)
    return output_block(flat_rows, w_out, hidden_in, req_n, head_n)


def solution(mesh):
    return jax.shard_map(
        functools.partial(local, mesh.shape["req"], mesh.shape["head"]),
        mesh=mesh,
        in_specs=(
            P("head", "req"),
            P("req"),
            P("req", "head"),
            P("head", "req"),
            P("req", None, "head"),
            P("req", None, "head"),
            P("req"),
        ),
        out_specs=P("head", "req"),
        check_vma=False,
    )
```

```python
import functools
import itertools

import jax
import jax.numpy as jnp
from jax import lax
from jax.experimental import pallas as pl
from jax.experimental.pallas import tpu as pltpu
from jax.sharding import PartitionSpec as P

D = 8192
GROUP = 8
HD = 128


epsilon = 1e-05
rope_base = 500000.0


def rotate(vectors, positions):
    halfway = vectors.shape[-1] // 2
    frequency = jnp.exp(
        -jnp.log(rope_base) * 2.0 * jnp.arange(halfway, dtype=jnp.float32) / vectors.shape[-1]
    )
    angles = positions.astype(jnp.float32)[:, None] * frequency[None, :]
    target_shape = (angles.shape[0],) + (1,) * (vectors.ndim - 2) + (halfway,)
    cosine = jnp.cos(angles).reshape(target_shape)
    sine_part = jnp.sin(angles).reshape(target_shape)
    first = vectors[..., :halfway]
    second = vectors[..., halfway:]
    return jnp.concatenate(
        [first * cosine - second * sine_part, second * cosine + first * sine_part], axis=-1
    )


def own_part(own_score, running, totals, new_values):
    own_prob = lax.optimization_barrier(
        (jnp.exp(own_score - running) / totals).astype(jnp.bfloat16)
    )
    return own_prob.astype(jnp.float32)[..., None] * new_values.astype(jnp.float32)[:, :, None, :]


def attend_padded(queries, new_keys, new_values, cached_keys, cached_values, inside, factor):
    scores = (
        jnp.einsum("rkgd,rpkd->rkgp", queries, cached_keys, preferred_element_type=jnp.float32)
        * factor
    )
    scores = jnp.where(inside[:, None, None, :], scores, -1e30)
    own_score = (
        jnp.einsum("rkgd,rkd->rkg", queries, new_keys, preferred_element_type=jnp.float32) * factor
    )
    running = jnp.maximum(jnp.max(scores, axis=3), own_score)
    weights = jnp.where(inside[:, None, None, :], jnp.exp(scores - running[..., None]), 0.0)
    totals = jnp.sum(weights, axis=3) + jnp.exp(own_score - running)
    probs = (weights / totals[..., None]).astype(jnp.bfloat16)
    mixed = jnp.einsum("rkgp,rpkd->rkgd", probs, cached_values, preferred_element_type=jnp.float32)
    mixed = mixed + own_part(own_score, running, totals, new_values)
    return mixed.astype(jnp.bfloat16)


def greet(peers):
    barrier = pltpu.get_barrier_semaphore()
    for axis, ordered in peers:
        for peer, _ in ordered:
            pl.semaphore_signal(
                barrier, inc=1, device_id={axis: peer}, device_id_type=pl.DeviceIdType.MESH
            )
    pl.semaphore_wait(barrier, sum(len(ordered) for _, ordered in peers))


def ordered_peers(me, digits):
    sizes = [size for size, _ in digits]
    mine, rest = [], me
    for size in reversed(sizes):
        mine.append(lax.rem(rest, size))
        rest = rest // size
    mine = mine[::-1]
    offsets = [o for o in itertools.product(*[range(s) for s in sizes]) if any(o)]
    offsets.sort(key=lambda o: -sum(w * min(d, s - d) for d, (s, w) in zip(o, digits)))

    def compose(o, forward):
        index = 0
        for d, m, s in zip(o, mine, sizes):
            index = index * s + lax.rem(m + (d if forward else s - d), s)
        return index

    return [(compose(o, True), compose(o, False)) for o in offsets]


def send_all(axis, peers, block_of, dst, send_sems, recv_sems, me):
    sends = []
    for k, (peer, _) in enumerate(peers, start=1):
        copy = pltpu.make_async_remote_copy(
            src_ref=block_of(peer),
            dst_ref=dst.at[me],
            send_sem=send_sems.at[k],
            recv_sem=recv_sems.at[k],
            device_id={axis: peer},
            device_id_type=pl.DeviceIdType.MESH,
        )
        copy.start()
        sends.append(copy)
    return sends


def receive_all(axis, peers, block_of, dst, send_sems, recv_sems, sends):
    for k, (_, source) in enumerate(peers, start=1):
        arrival = pltpu.make_async_remote_copy(
            src_ref=block_of(source),
            dst_ref=dst.at[source],
            send_sem=send_sems.at[k],
            recv_sem=recv_sems.at[k],
            device_id={axis: source},
            device_id_type=pl.DeviceIdType.MESH,
        )
        arrival.wait_recv()
    for copy in sends:
        copy.wait_send()


def project_kernel(req_n, head_n, x_hbm, gain_hbm, w_hbm, cos_ref, sin_ref, len_ref, keys_hbm,
                   values_hbm, q_ref, k_ref, v_ref, inside_ref, keys_ref, values_ref,
                   w_ref, gain_ref, rows_buf, part, pair_buf, mixed, sums_buf, sems, w_sem, key_sem):
    me_head = lax.axis_index("head")
    me_req = lax.axis_index("req")
    chips = req_n // 2
    me_core = lax.rem(me_req, 2)
    me_chip = me_req // 2
    partner = me_req + 1 - 2 * me_core
    w_copy = pltpu.make_async_copy(w_hbm, w_ref, w_sem.at[0])
    w_copy.start()
    x_copy = pltpu.make_async_copy(x_hbm, rows_buf.at[me_head], w_sem.at[1])
    x_copy.start()
    gain_copy = pltpu.make_async_copy(gain_hbm, gain_ref, w_sem.at[2])
    gain_copy.start()
    key_copy = pltpu.make_async_copy(keys_hbm, keys_ref, key_sem.at[0])
    key_copy.start()
    value_copy = pltpu.make_async_copy(values_hbm, values_ref, key_sem.at[1])
    value_copy.start()
    chip_peers = [
        (chip * 2 + me_core, None)
        for chip, _ in ordered_peers(me_chip, ((chips // 2, 1), (2, 2)))
    ]
    head_peers = ordered_peers(me_head, ((head_n // 2, 1), (2, 1)))
    greet((("req", chip_peers), ("head", head_peers), ("req", [(partner, None)])))
    own = lambda peer: x_hbm
    sends = send_all("head", head_peers, own, rows_buf, sems.at[0], sems.at[1], me_head)
    receive_all("head", head_peers, own, rows_buf, sems.at[0], sems.at[1], sends)
    x_copy.wait()
    gain_copy.wait()
    block_rows = x_hbm.shape[0]
    states = rows_buf[...].reshape(head_n * block_rows, x_hbm.shape[1]).astype(jnp.float32)
    scaled = (states * gain_ref[...].astype(jnp.float32)[None, :]).astype(jnp.bfloat16)
    columns = w_ref.shape[1]
    square = jnp.sum(states * states, axis=1, keepdims=True)
    w_copy.wait()
    packed = jnp.concatenate(
        [jnp.dot(scaled, w_ref[...], preferred_element_type=jnp.float32),
         jnp.broadcast_to(square, (square.shape[0], part.shape[-1] - columns))],
        axis=1,
    )
    count = k_ref.shape[0]
    packed = packed.reshape(chips, 2, count, part.shape[-1])
    part[0] = packed[:, 0]
    part[1] = packed[:, 1]
    width = part.shape[-1]
    split = (width // 2 + 127) // 128 * 128
    parts = ((0, split), (split, width - split))
    pairs = []
    for h, (lo, size) in enumerate(parts):
        pair = pltpu.make_async_remote_copy(
            src_ref=part.at[1 - me_core, :, :, pl.ds(lo, size)],
            dst_ref=pair_buf.at[:, :, pl.ds(lo, size)],
            send_sem=sems.at[2 * h, 0],
            recv_sem=sems.at[2 * h + 1, 0],
            device_id={"req": partner},
            device_id_type=pl.DeviceIdType.MESH,
        )
        pair.start()
        pairs.append(pair)
    z_n = chips // 2
    me_z, me_x = me_chip // 2, lax.rem(me_chip, 2)
    offsets = sorted(
        [(dz, dx) for dz in range(z_n) for dx in range(2) if dz or dx],
        key=lambda o: -(min(o[0], z_n - o[0]) + 2 * o[1]),
    )
    sends = []
    for h, (lo, size) in enumerate(parts):
        pairs[h].wait()
        columns_h = pl.ds(lo, size)
        mixed[:, :, columns_h] = part[me_core, :, :, columns_h] + pair_buf[:, :, columns_h]
        for k, (dz, dx) in enumerate(offsets, start=1):
            chip = lax.rem(me_z + dz, z_n) * 2 + lax.rem(me_x + dx, 2)
            copy = pltpu.make_async_remote_copy(
                src_ref=mixed.at[chip, :, columns_h],
                dst_ref=sums_buf.at[me_chip, :, columns_h],
                send_sem=sems.at[2, h * chips + k],
                recv_sem=sems.at[3, h * chips + k],
                device_id={"req": chip * 2 + me_core},
                device_id_type=pl.DeviceIdType.MESH,
            )
            copy.start()
            sends.append(copy)
    for h, (lo, size) in enumerate(parts):
        for k, (dz, dx) in enumerate(offsets, start=1):
            chip = lax.rem(me_z + z_n - dz, z_n) * 2 + lax.rem(me_x + 2 - dx, 2)
            arrival = pltpu.make_async_remote_copy(
                src_ref=mixed.at[chip, :, pl.ds(lo, size)],
                dst_ref=sums_buf.at[chip, :, pl.ds(lo, size)],
                send_sem=sems.at[2, h * chips + k],
                recv_sem=sems.at[3, h * chips + k],
                device_id={"req": chip * 2 + me_core},
                device_id_type=pl.DeviceIdType.MESH,
            )
            arrival.wait_recv()
    for copy in sends:
        copy.wait_send()
    total = mixed[me_chip]
    for k in range(1, chips):
        total = total + sums_buf[lax.rem(me_chip + chips - k, chips)]
    mean_square = total[:, columns:columns + 1] / D
    projected = total[:, :columns] * lax.rsqrt(mean_square + epsilon)
    cosine, sine = cos_ref[...], sin_ref[...]
    rotated = lambda block: block * cosine + pltpu.roll(block, HD // 2, 1) * sine
    for g in range(GROUP):
        q_ref[g] = rotated(projected[:, g * HD:(g + 1) * HD]).astype(jnp.bfloat16).astype(jnp.float32)
    k_ref[...] = rotated(projected[:, GROUP * HD:(GROUP + 1) * HD]).astype(k_ref.dtype)
    v_ref[...] = projected[:, (GROUP + 1) * HD:].astype(v_ref.dtype)
    slot = lax.broadcasted_iota(jnp.int32, (1, inside_ref.shape[1]), 1)
    for b in range(inside_ref.shape[0]):
        inside_ref[pl.ds(b, 1), :] = (slot < len_ref[b]).astype(inside_ref.dtype)
    key_copy.wait()
    value_copy.wait()


def project(hidden_in, gain, w_qkv, lengths, k_cache, v_cache, req_n, head_n, count):
    rows, width = hidden_in.shape
    columns = w_qkv.shape[1] + 128
    halfway = HD // 2
    frequency = jnp.exp(
        -jnp.log(rope_base) * 2.0 * jnp.arange(halfway, dtype=jnp.float32) / HD
    )
    angles = lengths.astype(jnp.float32)[:, None] * frequency[None, :]
    cosine = jnp.concatenate([jnp.cos(angles), jnp.cos(angles)], axis=1)
    sine = jnp.concatenate([-jnp.sin(angles), jnp.sin(angles)], axis=1)
    return pl.pallas_call(
        functools.partial(project_kernel, req_n, head_n),
        out_shape=(
            jax.ShapeDtypeStruct((GROUP, count, HD), jnp.float32),
            jax.ShapeDtypeStruct((count, HD), jnp.bfloat16),
            jax.ShapeDtypeStruct((count, HD), jnp.bfloat16),
            jax.ShapeDtypeStruct((count, k_cache.shape[1]), jnp.int32),
            jax.ShapeDtypeStruct(k_cache.shape, k_cache.dtype),
            jax.ShapeDtypeStruct(v_cache.shape, v_cache.dtype),
        ),
        in_specs=[pl.BlockSpec(memory_space=pltpu.HBM)] * 3
        + [pl.BlockSpec(memory_space=pltpu.VMEM)] * 2
        + [pl.BlockSpec(memory_space=pltpu.SMEM)]
        + [pl.BlockSpec(memory_space=pl.ANY)] * 2,
        out_specs=(pl.BlockSpec(memory_space=pltpu.VMEM),) * 6,
        scratch_shapes=[
            pltpu.VMEM(w_qkv.shape, w_qkv.dtype),
            pltpu.VMEM(gain.shape, gain.dtype),
            pltpu.VMEM((head_n, rows, width), hidden_in.dtype),
            pltpu.VMEM((2, req_n // 2, count, columns), jnp.float32),
            pltpu.VMEM((req_n // 2, count, columns), jnp.float32),
            pltpu.VMEM((req_n // 2, count, columns), jnp.float32),
            pltpu.VMEM((req_n // 2, count, columns), jnp.float32),
            pltpu.SemaphoreType.DMA((4, max(req_n, head_n))),
            pltpu.SemaphoreType.DMA((3,)),
            pltpu.SemaphoreType.DMA((2,)),
        ],
        compiler_params=pltpu.CompilerParams(
            collective_id=0, has_side_effects=True, vmem_limit_bytes=30 * 1024 * 1024
        ),
    )(
        pltpu.with_memory_space_constraint(hidden_in, pltpu.HBM),
        pltpu.with_memory_space_constraint(gain, pltpu.HBM),
        pltpu.with_memory_space_constraint(w_qkv, pltpu.HBM),
        cosine, sine, pltpu.with_memory_space_constraint(lengths, pltpu.HBM), k_cache, v_cache,
    )


def output_kernel(req_n, head_n, a_ref, w_hbm, s_ref, o_ref, w_ref, att_buf, part, sums_buf,
                  sems, w_sem):
    me_head = lax.axis_index("head")
    me_req = lax.axis_index("req")
    w_copy = pltpu.make_async_copy(w_hbm, w_ref, w_sem)
    w_copy.start()
    req_peers = ordered_peers(me_req, ((req_n // 4, 1), (2, 2), (2, 0.5)))
    head_peers = ordered_peers(me_head, ((head_n // 2, 1), (2, 1)))
    greet((("req", req_peers), ("head", head_peers)))
    own = lambda peer: a_ref
    sends = send_all("req", req_peers, own, att_buf, sems.at[0], sems.at[1], me_req)
    receive_all("req", req_peers, own, att_buf, sems.at[0], sems.at[1], sends)
    att_buf[me_req] = a_ref[...]
    every = jnp.concatenate(
        [att_buf[s].astype(jnp.float32) for s in range(req_n)], axis=0
    ).astype(jnp.bfloat16)
    w_copy.wait()
    part[...] = jnp.dot(every, w_ref[...], preferred_element_type=jnp.float32)
    rows = o_ref.shape[0]
    chunk = lambda peer: part.at[pl.ds(pl.multiple_of(peer * rows, rows), rows)]
    head_peers = ordered_peers(me_head, ((head_n // 2, 1), (2, 1)))
    sends = send_all("head", head_peers, chunk, sums_buf, sems.at[2], sems.at[3], me_head)
    receive_all("head", head_peers, chunk, sums_buf, sems.at[2], sems.at[3], sends)
    total = part[pl.ds(pl.multiple_of(me_head * rows, rows), rows), :]
    for k in range(1, head_n):
        total = total + sums_buf[lax.rem(me_head + head_n - k, head_n)]
    o_ref[...] = (s_ref[...].astype(jnp.float32) + total).astype(o_ref.dtype)


def output_block(attended, w_out, hidden_in, req_n, head_n):
    count, width = attended.shape
    rows, columns = hidden_in.shape
    return pl.pallas_call(
        functools.partial(output_kernel, req_n, head_n),
        out_shape=jax.ShapeDtypeStruct((rows, columns), hidden_in.dtype),
        in_specs=[
            pl.BlockSpec(memory_space=pltpu.VMEM),
            pl.BlockSpec(memory_space=pl.ANY),
            pl.BlockSpec(memory_space=pltpu.VMEM),
        ],
        out_specs=pl.BlockSpec(memory_space=pltpu.VMEM),
        scratch_shapes=[
            pltpu.VMEM(w_out.shape, w_out.dtype),
            pltpu.VMEM((req_n, count, width), attended.dtype),
            pltpu.VMEM((head_n * rows, columns), jnp.float32),
            pltpu.VMEM((head_n, rows, columns), jnp.float32),
            pltpu.SemaphoreType.DMA((4, max(req_n, head_n))),
            pltpu.SemaphoreType.DMA(()),
        ],
        compiler_params=pltpu.CompilerParams(
            collective_id=1, has_side_effects=True, vmem_limit_bytes=12 * 1024 * 1024
        ),
    )(attended, w_out, hidden_in)


def local(req_n, head_n, hidden_in, attn_gain, w_qkv, w_out, k_cache, v_cache, lengths):
    own_count = k_cache.shape[0]
    queries, new_keys, new_values, inside, k_cache, v_cache = project(
        hidden_in, attn_gain, w_qkv, lengths, k_cache, v_cache, req_n, head_n, own_count
    )
    slots = k_cache.shape[1]
    local_heads = k_cache.shape[2] // HD
    queries = jnp.transpose(queries.astype(jnp.bfloat16), (1, 0, 2))[:, None]
    new_keys = new_keys[:, None]
    new_values = new_values[:, None]
    cached_keys = k_cache.reshape(own_count, slots, local_heads, HD)
    cached_values = v_cache.reshape(own_count, slots, local_heads, HD)
    factor = HD ** (-0.5)
    attended = attend_padded(
        queries, new_keys, new_values, cached_keys, cached_values, inside != 0, factor
    )
    flat_rows = attended.reshape(own_count, local_heads * GROUP * HD)
    return output_block(flat_rows, w_out, hidden_in, req_n, head_n)


def solution(mesh):
    return jax.shard_map(
        functools.partial(local, mesh.shape["req"], mesh.shape["head"]),
        mesh=mesh,
        in_specs=(
            P("head", "req"),
            P("req"),
            P("req", "head"),
            P("head", "req"),
            P("req", None, "head"),
            P("req", None, "head"),
            P("req"),
        ),
        out_specs=P("head", "req"),
        check_vma=False,
    )
```

```python
import functools
import itertools

import jax
import jax.numpy as jnp
from jax import lax
from jax.experimental import pallas as pl
from jax.experimental.pallas import tpu as pltpu
from jax.sharding import PartitionSpec as P

D = 8192
GROUP = 8
HD = 128


epsilon = 1e-05
rope_base = 500000.0


def rotate(vectors, positions):
    halfway = vectors.shape[-1] // 2
    frequency = jnp.exp(
        -jnp.log(rope_base) * 2.0 * jnp.arange(halfway, dtype=jnp.float32) / vectors.shape[-1]
    )
    angles = positions.astype(jnp.float32)[:, None] * frequency[None, :]
    target_shape = (angles.shape[0],) + (1,) * (vectors.ndim - 2) + (halfway,)
    cosine = jnp.cos(angles).reshape(target_shape)
    sine_part = jnp.sin(angles).reshape(target_shape)
    first = vectors[..., :halfway]
    second = vectors[..., halfway:]
    return jnp.concatenate(
        [first * cosine - second * sine_part, second * cosine + first * sine_part], axis=-1
    )


def own_part(own_score, running, totals, new_values):
    own_prob = lax.optimization_barrier(
        (jnp.exp(own_score - running) / totals).astype(jnp.bfloat16)
    )
    return own_prob.astype(jnp.float32)[..., None] * new_values.astype(jnp.float32)[:, :, None, :]


def attend_padded(queries, new_keys, new_values, cached_keys, cached_values, inside, factor):
    scores = (
        jnp.einsum("rkgd,rpkd->rkgp", queries, cached_keys, preferred_element_type=jnp.float32)
        * factor
    )
    scores = jnp.where(inside[:, None, None, :], scores, -1e30)
    own_score = (
        jnp.einsum("rkgd,rkd->rkg", queries, new_keys, preferred_element_type=jnp.float32) * factor
    )
    running = jnp.maximum(jnp.max(scores, axis=3), own_score)
    weights = jnp.where(inside[:, None, None, :], jnp.exp(scores - running[..., None]), 0.0)
    totals = jnp.sum(weights, axis=3) + jnp.exp(own_score - running)
    probs = (weights / totals[..., None]).astype(jnp.bfloat16)
    mixed = jnp.einsum("rkgp,rpkd->rkgd", probs, cached_values, preferred_element_type=jnp.float32)
    mixed = mixed + own_part(own_score, running, totals, new_values)
    return mixed.astype(jnp.bfloat16)


def greet(peers):
    barrier = pltpu.get_barrier_semaphore()
    for axis, ordered in peers:
        for peer, _ in ordered:
            pl.semaphore_signal(
                barrier, inc=1, device_id={axis: peer}, device_id_type=pl.DeviceIdType.MESH
            )
    pl.semaphore_wait(barrier, sum(len(ordered) for _, ordered in peers))


def ordered_peers(me, digits):
    sizes = [size for size, _ in digits]
    mine, rest = [], me
    for size in reversed(sizes):
        mine.append(lax.rem(rest, size))
        rest = rest // size
    mine = mine[::-1]
    offsets = [o for o in itertools.product(*[range(s) for s in sizes]) if any(o)]
    offsets.sort(key=lambda o: -sum(w * min(d, s - d) for d, (s, w) in zip(o, digits)))

    def compose(o, forward):
        index = 0
        for d, m, s in zip(o, mine, sizes):
            index = index * s + lax.rem(m + (d if forward else s - d), s)
        return index

    return [(compose(o, True), compose(o, False)) for o in offsets]


def send_all(axis, peers, block_of, dst, send_sems, recv_sems, me):
    sends = []
    for k, (peer, _) in enumerate(peers, start=1):
        copy = pltpu.make_async_remote_copy(
            src_ref=block_of(peer),
            dst_ref=dst.at[me],
            send_sem=send_sems.at[k],
            recv_sem=recv_sems.at[k],
            device_id={axis: peer},
            device_id_type=pl.DeviceIdType.MESH,
        )
        copy.start()
        sends.append(copy)
    return sends


def receive_all(axis, peers, block_of, dst, send_sems, recv_sems, sends):
    for k, (_, source) in enumerate(peers, start=1):
        arrival = pltpu.make_async_remote_copy(
            src_ref=block_of(source),
            dst_ref=dst.at[source],
            send_sem=send_sems.at[k],
            recv_sem=recv_sems.at[k],
            device_id={axis: source},
            device_id_type=pl.DeviceIdType.MESH,
        )
        arrival.wait_recv()
    for copy in sends:
        copy.wait_send()


def project_kernel(req_n, head_n, x_hbm, gain_hbm, w_hbm, cos_ref, sin_ref, len_ref, keys_hbm,
                   values_hbm, q_ref, k_ref, v_ref, inside_ref, keys_ref, values_ref,
                   w_ref, gain_ref, rows_buf, part, pair_buf, mixed, sums_buf, sems, w_sem, key_sem):
    me_head = lax.axis_index("head")
    me_req = lax.axis_index("req")
    chips = req_n // 2
    me_core = lax.rem(me_req, 2)
    me_chip = me_req // 2
    partner = me_req + 1 - 2 * me_core
    w_copy = pltpu.make_async_copy(w_hbm, w_ref, w_sem.at[0])
    w_copy.start()
    x_copy = pltpu.make_async_copy(x_hbm, rows_buf.at[me_head], w_sem.at[1])
    x_copy.start()
    gain_copy = pltpu.make_async_copy(gain_hbm, gain_ref, w_sem.at[2])
    gain_copy.start()
    key_copy = pltpu.make_async_copy(keys_hbm, keys_ref, key_sem.at[0])
    key_copy.start()
    value_copy = pltpu.make_async_copy(values_hbm, values_ref, key_sem.at[1])
    value_copy.start()
    chip_peers = [
        (chip * 2 + me_core, None)
        for chip, _ in ordered_peers(me_chip, ((chips // 2, 1), (2, 2)))
    ]
    head_peers = ordered_peers(me_head, ((head_n // 2, 1), (2, 1)))
    greet((("req", chip_peers), ("head", head_peers), ("req", [(partner, None)])))
    own = lambda peer: x_hbm
    sends = send_all("head", head_peers, own, rows_buf, sems.at[0], sems.at[1], me_head)
    receive_all("head", head_peers, own, rows_buf, sems.at[0], sems.at[1], sends)
    x_copy.wait()
    gain_copy.wait()
    block_rows = x_hbm.shape[0]
    states = rows_buf[...].reshape(head_n * block_rows, x_hbm.shape[1]).astype(jnp.float32)
    scaled = (states * gain_ref[...].astype(jnp.float32)[None, :]).astype(jnp.bfloat16)
    columns = w_ref.shape[1]
    square = jnp.sum(states * states, axis=1, keepdims=True)
    w_copy.wait()
    packed = jnp.concatenate(
        [jnp.dot(scaled, w_ref[...], preferred_element_type=jnp.float32),
         jnp.broadcast_to(square, (square.shape[0], part.shape[-1] - columns))],
        axis=1,
    )
    count = k_ref.shape[0]
    packed = packed.reshape(chips, 2, count, part.shape[-1])
    part[0] = packed[:, 0]
    part[1] = packed[:, 1]
    pair = pltpu.make_async_remote_copy(
        src_ref=part.at[1 - me_core],
        dst_ref=pair_buf,
        send_sem=sems.at[2, 0],
        recv_sem=sems.at[3, 0],
        device_id={"req": partner},
        device_id_type=pl.DeviceIdType.MESH,
    )
    pair.start()
    pair.wait()
    mixed[...] = part[me_core] + pair_buf[...]
    z_n = chips // 2
    me_z, me_x = me_chip // 2, lax.rem(me_chip, 2)
    offsets = sorted(
        [(dz, dx) for dz in range(z_n) for dx in range(2) if dz or dx],
        key=lambda o: -(min(o[0], z_n - o[0]) + 2 * o[1]),
    )
    sends = []
    for k, (dz, dx) in enumerate(offsets, start=1):
        chip = lax.rem(me_z + dz, z_n) * 2 + lax.rem(me_x + dx, 2)
        copy = pltpu.make_async_remote_copy(
            src_ref=mixed.at[chip],
            dst_ref=sums_buf.at[me_chip],
            send_sem=sems.at[2, k],
            recv_sem=sems.at[3, k],
            device_id={"req": chip * 2 + me_core},
            device_id_type=pl.DeviceIdType.MESH,
        )
        copy.start()
        sends.append(copy)
    for k, (dz, dx) in enumerate(offsets, start=1):
        chip = lax.rem(me_z + z_n - dz, z_n) * 2 + lax.rem(me_x + 2 - dx, 2)
        arrival = pltpu.make_async_remote_copy(
            src_ref=mixed.at[chip],
            dst_ref=sums_buf.at[chip],
            send_sem=sems.at[2, k],
            recv_sem=sems.at[3, k],
            device_id={"req": chip * 2 + me_core},
            device_id_type=pl.DeviceIdType.MESH,
        )
        arrival.wait_recv()
    for copy in sends:
        copy.wait_send()
    total = mixed[me_chip]
    for k in range(1, chips):
        total = total + sums_buf[lax.rem(me_chip + chips - k, chips)]
    mean_square = total[:, columns:columns + 1] / D
    projected = total[:, :columns] * lax.rsqrt(mean_square + epsilon)
    cosine, sine = cos_ref[...], sin_ref[...]
    rotated = lambda block: block * cosine + pltpu.roll(block, HD // 2, 1) * sine
    for g in range(GROUP):
        q_ref[g] = rotated(projected[:, g * HD:(g + 1) * HD]).astype(jnp.bfloat16).astype(jnp.float32)
    k_ref[...] = rotated(projected[:, GROUP * HD:(GROUP + 1) * HD]).astype(k_ref.dtype)
    v_ref[...] = projected[:, (GROUP + 1) * HD:].astype(v_ref.dtype)
    slot = lax.broadcasted_iota(jnp.int32, (1, inside_ref.shape[1]), 1)
    for b in range(inside_ref.shape[0]):
        inside_ref[pl.ds(b, 1), :] = (slot < len_ref[b]).astype(inside_ref.dtype)
    key_copy.wait()
    value_copy.wait()


def project(hidden_in, gain, w_qkv, lengths, k_cache, v_cache, req_n, head_n, count):
    rows, width = hidden_in.shape
    columns = w_qkv.shape[1] + 128
    halfway = HD // 2
    frequency = jnp.exp(
        -jnp.log(rope_base) * 2.0 * jnp.arange(halfway, dtype=jnp.float32) / HD
    )
    angles = lengths.astype(jnp.float32)[:, None] * frequency[None, :]
    cosine = jnp.concatenate([jnp.cos(angles), jnp.cos(angles)], axis=1)
    sine = jnp.concatenate([-jnp.sin(angles), jnp.sin(angles)], axis=1)
    return pl.pallas_call(
        functools.partial(project_kernel, req_n, head_n),
        out_shape=(
            jax.ShapeDtypeStruct((GROUP, count, HD), jnp.float32),
            jax.ShapeDtypeStruct((count, HD), jnp.bfloat16),
            jax.ShapeDtypeStruct((count, HD), jnp.bfloat16),
            jax.ShapeDtypeStruct((count, k_cache.shape[1]), jnp.int32),
            jax.ShapeDtypeStruct(k_cache.shape, k_cache.dtype),
            jax.ShapeDtypeStruct(v_cache.shape, v_cache.dtype),
        ),
        in_specs=[pl.BlockSpec(memory_space=pltpu.HBM)] * 3
        + [pl.BlockSpec(memory_space=pltpu.VMEM)] * 2
        + [pl.BlockSpec(memory_space=pltpu.SMEM)]
        + [pl.BlockSpec(memory_space=pl.ANY)] * 2,
        out_specs=(pl.BlockSpec(memory_space=pltpu.VMEM),) * 6,
        scratch_shapes=[
            pltpu.VMEM(w_qkv.shape, w_qkv.dtype),
            pltpu.VMEM(gain.shape, gain.dtype),
            pltpu.VMEM((head_n, rows, width), hidden_in.dtype),
            pltpu.VMEM((2, req_n // 2, count, columns), jnp.float32),
            pltpu.VMEM((req_n // 2, count, columns), jnp.float32),
            pltpu.VMEM((req_n // 2, count, columns), jnp.float32),
            pltpu.VMEM((req_n // 2, count, columns), jnp.float32),
            pltpu.SemaphoreType.DMA((4, max(req_n, head_n))),
            pltpu.SemaphoreType.DMA((3,)),
            pltpu.SemaphoreType.DMA((2,)),
        ],
        compiler_params=pltpu.CompilerParams(
            collective_id=0, has_side_effects=True, vmem_limit_bytes=30 * 1024 * 1024
        ),
    )(
        pltpu.with_memory_space_constraint(hidden_in, pltpu.HBM),
        pltpu.with_memory_space_constraint(gain, pltpu.HBM),
        pltpu.with_memory_space_constraint(w_qkv, pltpu.HBM),
        cosine, sine, pltpu.with_memory_space_constraint(lengths, pltpu.HBM), k_cache, v_cache,
    )


def output_kernel(req_n, head_n, a_ref, w_ref, s_ref, o_ref, att_buf, part, sums_buf, sems):
    me_head = lax.axis_index("head")
    me_req = lax.axis_index("req")
    req_peers = ordered_peers(me_req, ((req_n // 4, 1), (2, 2), (2, 0.5)))
    head_peers = ordered_peers(me_head, ((head_n // 2, 1), (2, 1)))
    greet((("req", req_peers), ("head", head_peers)))
    own = lambda peer: a_ref
    sends = send_all("req", req_peers, own, att_buf, sems.at[0], sems.at[1], me_req)
    receive_all("req", req_peers, own, att_buf, sems.at[0], sems.at[1], sends)
    att_buf[me_req] = a_ref[...]
    every = jnp.concatenate(
        [att_buf[s].astype(jnp.float32) for s in range(req_n)], axis=0
    ).astype(jnp.bfloat16)
    part[...] = jnp.dot(every, w_ref[...], preferred_element_type=jnp.float32)
    rows = o_ref.shape[0]
    chunk = lambda peer: part.at[pl.ds(pl.multiple_of(peer * rows, rows), rows)]
    head_peers = ordered_peers(me_head, ((head_n // 2, 1), (2, 1)))
    sends = send_all("head", head_peers, chunk, sums_buf, sems.at[2], sems.at[3], me_head)
    receive_all("head", head_peers, chunk, sums_buf, sems.at[2], sems.at[3], sends)
    total = part[pl.ds(pl.multiple_of(me_head * rows, rows), rows), :]
    for k in range(1, head_n):
        total = total + sums_buf[lax.rem(me_head + head_n - k, head_n)]
    o_ref[...] = (s_ref[...].astype(jnp.float32) + total).astype(o_ref.dtype)


def output_block(attended, w_out, hidden_in, req_n, head_n):
    count, width = attended.shape
    rows, columns = hidden_in.shape
    return pl.pallas_call(
        functools.partial(output_kernel, req_n, head_n),
        out_shape=jax.ShapeDtypeStruct((rows, columns), hidden_in.dtype),
        in_specs=[pl.BlockSpec(memory_space=pltpu.VMEM)] * 3,
        out_specs=pl.BlockSpec(memory_space=pltpu.VMEM),
        scratch_shapes=[
            pltpu.VMEM((req_n, count, width), attended.dtype),
            pltpu.VMEM((head_n * rows, columns), jnp.float32),
            pltpu.VMEM((head_n, rows, columns), jnp.float32),
            pltpu.SemaphoreType.DMA((4, max(req_n, head_n))),

        ],
        compiler_params=pltpu.CompilerParams(
            collective_id=1, has_side_effects=True, vmem_limit_bytes=12 * 1024 * 1024
        ),
    )(attended, w_out, hidden_in)


def local(req_n, head_n, hidden_in, attn_gain, w_qkv, w_out, k_cache, v_cache, lengths):
    own_count = k_cache.shape[0]
    queries, new_keys, new_values, inside, k_cache, v_cache = project(
        hidden_in, attn_gain, w_qkv, lengths, k_cache, v_cache, req_n, head_n, own_count
    )
    slots = k_cache.shape[1]
    local_heads = k_cache.shape[2] // HD
    queries = jnp.transpose(queries.astype(jnp.bfloat16), (1, 0, 2))[:, None]
    new_keys = new_keys[:, None]
    new_values = new_values[:, None]
    cached_keys = k_cache.reshape(own_count, slots, local_heads, HD)
    cached_values = v_cache.reshape(own_count, slots, local_heads, HD)
    factor = HD ** (-0.5)
    attended = attend_padded(
        queries, new_keys, new_values, cached_keys, cached_values, inside != 0, factor
    )
    flat_rows = attended.reshape(own_count, local_heads * GROUP * HD)
    return output_block(flat_rows, w_out, hidden_in, req_n, head_n)


def solution(mesh):
    return jax.shard_map(
        functools.partial(local, mesh.shape["req"], mesh.shape["head"]),
        mesh=mesh,
        in_specs=(
            P("head", "req"),
            P("req"),
            P("req", "head"),
            P("head", "req"),
            P("req", None, "head"),
            P("req", None, "head"),
            P("req"),
        ),
        out_specs=P("head", "req"),
        check_vma=False,
    )
```

```python
import functools
import itertools

import jax
import jax.numpy as jnp
from jax import lax
from jax.experimental import pallas as pl
from jax.experimental.pallas import tpu as pltpu
from jax.sharding import PartitionSpec as P

D = 8192
GROUP = 8
HD = 128


epsilon = 1e-05
rope_base = 500000.0


def rotate(vectors, positions):
    halfway = vectors.shape[-1] // 2
    frequency = jnp.exp(
        -jnp.log(rope_base) * 2.0 * jnp.arange(halfway, dtype=jnp.float32) / vectors.shape[-1]
    )
    angles = positions.astype(jnp.float32)[:, None] * frequency[None, :]
    target_shape = (angles.shape[0],) + (1,) * (vectors.ndim - 2) + (halfway,)
    cosine = jnp.cos(angles).reshape(target_shape)
    sine_part = jnp.sin(angles).reshape(target_shape)
    first = vectors[..., :halfway]
    second = vectors[..., halfway:]
    return jnp.concatenate(
        [first * cosine - second * sine_part, second * cosine + first * sine_part], axis=-1
    )


def own_part(own_score, running, totals, new_values):
    own_prob = lax.optimization_barrier(
        (jnp.exp(own_score - running) / totals).astype(jnp.bfloat16)
    )
    return own_prob.astype(jnp.float32)[..., None] * new_values.astype(jnp.float32)[:, :, None, :]


def attend_padded(queries, new_keys, new_values, cached_keys, cached_values, inside, factor):
    scores = (
        jnp.einsum("rkgd,rpkd->rkgp", queries, cached_keys, preferred_element_type=jnp.float32)
        * factor
    )
    scores = jnp.where(inside[:, None, None, :], scores, -1e30)
    own_score = (
        jnp.einsum("rkgd,rkd->rkg", queries, new_keys, preferred_element_type=jnp.float32) * factor
    )
    running = jnp.maximum(jnp.max(scores, axis=3), own_score)
    weights = jnp.where(inside[:, None, None, :], jnp.exp(scores - running[..., None]), 0.0)
    totals = jnp.sum(weights, axis=3) + jnp.exp(own_score - running)
    probs = (weights / totals[..., None]).astype(jnp.bfloat16)
    mixed = jnp.einsum("rkgp,rpkd->rkgd", probs, cached_values, preferred_element_type=jnp.float32)
    mixed = mixed + own_part(own_score, running, totals, new_values)
    return mixed.astype(jnp.bfloat16)


def greet(peers):
    barrier = pltpu.get_barrier_semaphore()
    for axis, ordered in peers:
        for peer, _ in ordered:
            pl.semaphore_signal(
                barrier, inc=1, device_id={axis: peer}, device_id_type=pl.DeviceIdType.MESH
            )
    pl.semaphore_wait(barrier, sum(len(ordered) for _, ordered in peers))


def ordered_peers(me, digits):
    sizes = [size for size, _ in digits]
    mine, rest = [], me
    for size in reversed(sizes):
        mine.append(lax.rem(rest, size))
        rest = rest // size
    mine = mine[::-1]
    offsets = [o for o in itertools.product(*[range(s) for s in sizes]) if any(o)]
    offsets.sort(key=lambda o: -sum(w * min(d, s - d) for d, (s, w) in zip(o, digits)))

    def compose(o, forward):
        index = 0
        for d, m, s in zip(o, mine, sizes):
            index = index * s + lax.rem(m + (d if forward else s - d), s)
        return index

    return [(compose(o, True), compose(o, False)) for o in offsets]


def send_all(axis, peers, block_of, dst, send_sems, recv_sems, me):
    sends = []
    for k, (peer, _) in enumerate(peers, start=1):
        copy = pltpu.make_async_remote_copy(
            src_ref=block_of(peer),
            dst_ref=dst.at[me],
            send_sem=send_sems.at[k],
            recv_sem=recv_sems.at[k],
            device_id={axis: peer},
            device_id_type=pl.DeviceIdType.MESH,
        )
        copy.start()
        sends.append(copy)
    return sends


def receive_all(axis, peers, block_of, dst, send_sems, recv_sems, sends):
    for k, (_, source) in enumerate(peers, start=1):
        arrival = pltpu.make_async_remote_copy(
            src_ref=block_of(source),
            dst_ref=dst.at[source],
            send_sem=send_sems.at[k],
            recv_sem=recv_sems.at[k],
            device_id={axis: source},
            device_id_type=pl.DeviceIdType.MESH,
        )
        arrival.wait_recv()
    for copy in sends:
        copy.wait_send()


def project_kernel(req_n, head_n, x_hbm, gain_hbm, w_hbm, cos_ref, sin_ref, len_ref, keys_hbm,
                   values_hbm, q_ref, k_ref, v_ref, inside_ref, keys_ref, values_ref,
                   w_ref, gain_ref, rows_buf, part, pair_buf, mixed, sums_buf, sems, w_sem, key_sem):
    me_head = lax.axis_index("head")
    me_req = lax.axis_index("req")
    chips = req_n // 2
    me_core = lax.rem(me_req, 2)
    me_chip = me_req // 2
    partner = me_req + 1 - 2 * me_core
    w_copy = pltpu.make_async_copy(w_hbm, w_ref, w_sem.at[0])
    w_copy.start()
    x_copy = pltpu.make_async_copy(x_hbm, rows_buf.at[me_head], w_sem.at[1])
    x_copy.start()
    gain_copy = pltpu.make_async_copy(gain_hbm, gain_ref, w_sem.at[2])
    gain_copy.start()
    key_copy = pltpu.make_async_copy(keys_hbm, keys_ref, key_sem.at[0])
    key_copy.start()
    value_copy = pltpu.make_async_copy(values_hbm, values_ref, key_sem.at[1])
    value_copy.start()
    chip_peers = [
        (chip * 2 + me_core, None)
        for chip, _ in ordered_peers(me_chip, ((chips // 2, 1), (2, 2)))
    ]
    head_peers = ordered_peers(me_head, ((head_n // 2, 1), (2, 1)))
    greet((("req", chip_peers), ("head", head_peers), ("req", [(partner, None)])))
    own = lambda peer: x_hbm
    sends = send_all("head", head_peers, own, rows_buf, sems.at[0], sems.at[1], me_head)
    receive_all("head", head_peers, own, rows_buf, sems.at[0], sems.at[1], sends)
    x_copy.wait()
    gain_copy.wait()
    block_rows = x_hbm.shape[0]
    states = rows_buf[...].reshape(head_n * block_rows, x_hbm.shape[1]).astype(jnp.float32)
    scaled = (states * gain_ref[...].astype(jnp.float32)[None, :]).astype(jnp.bfloat16)
    columns = w_ref.shape[1]
    square = jnp.sum(states * states, axis=1, keepdims=True)
    w_copy.wait()
    packed = jnp.concatenate(
        [jnp.dot(scaled, w_ref[...], preferred_element_type=jnp.float32),
         jnp.broadcast_to(square, (square.shape[0], part.shape[-1] - columns))],
        axis=1,
    )
    count = k_ref.shape[0]
    packed = packed.reshape(chips, 2, count, part.shape[-1])
    part[0] = packed[:, 0]
    part[1] = packed[:, 1]
    pair = pltpu.make_async_remote_copy(
        src_ref=part.at[1 - me_core],
        dst_ref=pair_buf,
        send_sem=sems.at[2, 0],
        recv_sem=sems.at[3, 0],
        device_id={"req": partner},
        device_id_type=pl.DeviceIdType.MESH,
    )
    pair.start()
    pair.wait()
    z_n = chips // 2
    me_z, me_x = me_chip // 2, lax.rem(me_chip, 2)
    offsets = sorted(
        [(dz, dx) for dz in range(z_n) for dx in range(2) if dz or dx],
        key=lambda o: -(min(o[0], z_n - o[0]) + 2 * o[1]),
    )
    sends = []
    for k, (dz, dx) in enumerate(offsets, start=1):
        chip = lax.rem(me_z + dz, z_n) * 2 + lax.rem(me_x + dx, 2)
        mixed[chip] = part[me_core, chip] + pair_buf[chip]
        copy = pltpu.make_async_remote_copy(
            src_ref=mixed.at[chip],
            dst_ref=sums_buf.at[me_chip],
            send_sem=sems.at[2, k],
            recv_sem=sems.at[3, k],
            device_id={"req": chip * 2 + me_core},
            device_id_type=pl.DeviceIdType.MESH,
        )
        copy.start()
        sends.append(copy)
    for k, (dz, dx) in enumerate(offsets, start=1):
        chip = lax.rem(me_z + z_n - dz, z_n) * 2 + lax.rem(me_x + 2 - dx, 2)
        arrival = pltpu.make_async_remote_copy(
            src_ref=mixed.at[chip],
            dst_ref=sums_buf.at[chip],
            send_sem=sems.at[2, k],
            recv_sem=sems.at[3, k],
            device_id={"req": chip * 2 + me_core},
            device_id_type=pl.DeviceIdType.MESH,
        )
        arrival.wait_recv()
    for copy in sends:
        copy.wait_send()
    total = part[me_core, me_chip] + pair_buf[me_chip]
    for k in range(1, chips):
        total = total + sums_buf[lax.rem(me_chip + chips - k, chips)]
    mean_square = total[:, columns:columns + 1] / D
    projected = total[:, :columns] * lax.rsqrt(mean_square + epsilon)
    cosine, sine = cos_ref[...], sin_ref[...]
    rotated = lambda block: block * cosine + pltpu.roll(block, HD // 2, 1) * sine
    for g in range(GROUP):
        q_ref[g] = rotated(projected[:, g * HD:(g + 1) * HD]).astype(jnp.bfloat16).astype(jnp.float32)
    k_ref[...] = rotated(projected[:, GROUP * HD:(GROUP + 1) * HD]).astype(k_ref.dtype)
    v_ref[...] = projected[:, (GROUP + 1) * HD:].astype(v_ref.dtype)
    slot = lax.broadcasted_iota(jnp.int32, (1, inside_ref.shape[1]), 1)
    for b in range(inside_ref.shape[0]):
        inside_ref[pl.ds(b, 1), :] = (slot < len_ref[b]).astype(inside_ref.dtype)
    key_copy.wait()
    value_copy.wait()


def project(hidden_in, gain, w_qkv, lengths, k_cache, v_cache, req_n, head_n, count):
    rows, width = hidden_in.shape
    columns = w_qkv.shape[1] + 128
    halfway = HD // 2
    frequency = jnp.exp(
        -jnp.log(rope_base) * 2.0 * jnp.arange(halfway, dtype=jnp.float32) / HD
    )
    angles = lengths.astype(jnp.float32)[:, None] * frequency[None, :]
    cosine = jnp.concatenate([jnp.cos(angles), jnp.cos(angles)], axis=1)
    sine = jnp.concatenate([-jnp.sin(angles), jnp.sin(angles)], axis=1)
    return pl.pallas_call(
        functools.partial(project_kernel, req_n, head_n),
        out_shape=(
            jax.ShapeDtypeStruct((GROUP, count, HD), jnp.float32),
            jax.ShapeDtypeStruct((count, HD), jnp.bfloat16),
            jax.ShapeDtypeStruct((count, HD), jnp.bfloat16),
            jax.ShapeDtypeStruct((count, k_cache.shape[1]), jnp.int32),
            jax.ShapeDtypeStruct(k_cache.shape, k_cache.dtype),
            jax.ShapeDtypeStruct(v_cache.shape, v_cache.dtype),
        ),
        in_specs=[pl.BlockSpec(memory_space=pltpu.HBM)] * 3
        + [pl.BlockSpec(memory_space=pltpu.VMEM)] * 2
        + [pl.BlockSpec(memory_space=pltpu.SMEM)]
        + [pl.BlockSpec(memory_space=pl.ANY)] * 2,
        out_specs=(pl.BlockSpec(memory_space=pltpu.VMEM),) * 6,
        scratch_shapes=[
            pltpu.VMEM(w_qkv.shape, w_qkv.dtype),
            pltpu.VMEM(gain.shape, gain.dtype),
            pltpu.VMEM((head_n, rows, width), hidden_in.dtype),
            pltpu.VMEM((2, req_n // 2, count, columns), jnp.float32),
            pltpu.VMEM((req_n // 2, count, columns), jnp.float32),
            pltpu.VMEM((req_n // 2, count, columns), jnp.float32),
            pltpu.VMEM((req_n // 2, count, columns), jnp.float32),
            pltpu.SemaphoreType.DMA((4, max(req_n, head_n))),
            pltpu.SemaphoreType.DMA((3,)),
            pltpu.SemaphoreType.DMA((2,)),
        ],
        compiler_params=pltpu.CompilerParams(
            collective_id=0, has_side_effects=True, vmem_limit_bytes=30 * 1024 * 1024
        ),
    )(
        pltpu.with_memory_space_constraint(hidden_in, pltpu.HBM),
        pltpu.with_memory_space_constraint(gain, pltpu.HBM),
        pltpu.with_memory_space_constraint(w_qkv, pltpu.HBM),
        cosine, sine, pltpu.with_memory_space_constraint(lengths, pltpu.HBM), k_cache, v_cache,
    )


def output_kernel(req_n, head_n, a_ref, w_hbm, s_ref, o_ref, w_ref, att_buf, part, sums_buf,
                  sems, w_sem):
    me_head = lax.axis_index("head")
    me_req = lax.axis_index("req")
    w_copy = pltpu.make_async_copy(w_hbm, w_ref, w_sem)
    w_copy.start()
    req_peers = ordered_peers(me_req, ((req_n // 4, 1), (2, 2), (2, 0.5)))
    head_peers = ordered_peers(me_head, ((head_n // 2, 1), (2, 1)))
    greet((("req", req_peers), ("head", head_peers)))
    own = lambda peer: a_ref
    sends = send_all("req", req_peers, own, att_buf, sems.at[0], sems.at[1], me_req)
    receive_all("req", req_peers, own, att_buf, sems.at[0], sems.at[1], sends)
    att_buf[me_req] = a_ref[...]
    every = jnp.concatenate(
        [att_buf[s].astype(jnp.float32) for s in range(req_n)], axis=0
    ).astype(jnp.bfloat16)
    w_copy.wait()
    part[...] = jnp.dot(every, w_ref[...], preferred_element_type=jnp.float32)
    rows = o_ref.shape[0]
    chunk = lambda peer: part.at[pl.ds(pl.multiple_of(peer * rows, rows), rows)]
    head_peers = ordered_peers(me_head, ((head_n // 2, 1), (2, 1)))
    sends = send_all("head", head_peers, chunk, sums_buf, sems.at[2], sems.at[3], me_head)
    receive_all("head", head_peers, chunk, sums_buf, sems.at[2], sems.at[3], sends)
    total = part[pl.ds(pl.multiple_of(me_head * rows, rows), rows), :]
    for k in range(1, head_n):
        total = total + sums_buf[lax.rem(me_head + head_n - k, head_n)]
    o_ref[...] = (s_ref[...].astype(jnp.float32) + total).astype(o_ref.dtype)


def output_block(attended, w_out, hidden_in, req_n, head_n):
    count, width = attended.shape
    rows, columns = hidden_in.shape
    return pl.pallas_call(
        functools.partial(output_kernel, req_n, head_n),
        out_shape=jax.ShapeDtypeStruct((rows, columns), hidden_in.dtype),
        in_specs=[
            pl.BlockSpec(memory_space=pltpu.VMEM),
            pl.BlockSpec(memory_space=pl.ANY),
            pl.BlockSpec(memory_space=pltpu.VMEM),
        ],
        out_specs=pl.BlockSpec(memory_space=pltpu.VMEM),
        scratch_shapes=[
            pltpu.VMEM(w_out.shape, w_out.dtype),
            pltpu.VMEM((req_n, count, width), attended.dtype),
            pltpu.VMEM((head_n * rows, columns), jnp.float32),
            pltpu.VMEM((head_n, rows, columns), jnp.float32),
            pltpu.SemaphoreType.DMA((4, max(req_n, head_n))),
            pltpu.SemaphoreType.DMA(()),
        ],
        compiler_params=pltpu.CompilerParams(
            collective_id=1, has_side_effects=True, vmem_limit_bytes=12 * 1024 * 1024
        ),
    )(attended, w_out, hidden_in)


def local(req_n, head_n, hidden_in, attn_gain, w_qkv, w_out, k_cache, v_cache, lengths):
    own_count = k_cache.shape[0]
    queries, new_keys, new_values, inside, k_cache, v_cache = project(
        hidden_in, attn_gain, w_qkv, lengths, k_cache, v_cache, req_n, head_n, own_count
    )
    slots = k_cache.shape[1]
    local_heads = k_cache.shape[2] // HD
    queries = jnp.transpose(queries.astype(jnp.bfloat16), (1, 0, 2))[:, None]
    new_keys = new_keys[:, None]
    new_values = new_values[:, None]
    cached_keys = k_cache.reshape(own_count, slots, local_heads, HD)
    cached_values = v_cache.reshape(own_count, slots, local_heads, HD)
    factor = HD ** (-0.5)
    attended = attend_padded(
        queries, new_keys, new_values, cached_keys, cached_values, inside != 0, factor
    )
    flat_rows = attended.reshape(own_count, local_heads * GROUP * HD)
    return output_block(flat_rows, w_out, hidden_in, req_n, head_n)


def solution(mesh):
    return jax.shard_map(
        functools.partial(local, mesh.shape["req"], mesh.shape["head"]),
        mesh=mesh,
        in_specs=(
            P("head", "req"),
            P("req"),
            P("req", "head"),
            P("head", "req"),
            P("req", None, "head"),
            P("req", None, "head"),
            P("req"),
        ),
        out_specs=P("head", "req"),
        check_vma=False,
    )
```

```python
import functools
import itertools

import jax
import jax.numpy as jnp
from jax import lax
from jax.experimental import pallas as pl
from jax.experimental.pallas import tpu as pltpu
from jax.sharding import PartitionSpec as P

D = 8192
GROUP = 8
HD = 128


epsilon = 1e-05
rope_base = 500000.0


def rotate(vectors, positions):
    halfway = vectors.shape[-1] // 2
    frequency = jnp.exp(
        -jnp.log(rope_base) * 2.0 * jnp.arange(halfway, dtype=jnp.float32) / vectors.shape[-1]
    )
    angles = positions.astype(jnp.float32)[:, None] * frequency[None, :]
    target_shape = (angles.shape[0],) + (1,) * (vectors.ndim - 2) + (halfway,)
    cosine = jnp.cos(angles).reshape(target_shape)
    sine_part = jnp.sin(angles).reshape(target_shape)
    first = vectors[..., :halfway]
    second = vectors[..., halfway:]
    return jnp.concatenate(
        [first * cosine - second * sine_part, second * cosine + first * sine_part], axis=-1
    )


def own_part(own_score, running, totals, new_values):
    own_prob = lax.optimization_barrier(
        (jnp.exp(own_score - running) / totals).astype(jnp.bfloat16)
    )
    return own_prob.astype(jnp.float32)[..., None] * new_values.astype(jnp.float32)[:, :, None, :]


def attend_padded(queries, new_keys, new_values, cached_keys, cached_values, inside, factor):
    scores = (
        jnp.einsum("rkgd,rpkd->rkgp", queries, cached_keys, preferred_element_type=jnp.float32)
        * factor
    )
    scores = jnp.where(inside[:, None, None, :], scores, -1e30)
    own_score = (
        jnp.einsum("rkgd,rkd->rkg", queries, new_keys, preferred_element_type=jnp.float32) * factor
    )
    running = jnp.maximum(jnp.max(scores, axis=3), own_score)
    weights = jnp.where(inside[:, None, None, :], jnp.exp(scores - running[..., None]), 0.0)
    totals = jnp.sum(weights, axis=3) + jnp.exp(own_score - running)
    probs = (weights / totals[..., None]).astype(jnp.bfloat16)
    mixed = jnp.einsum("rkgp,rpkd->rkgd", probs, cached_values, preferred_element_type=jnp.float32)
    mixed = mixed + own_part(own_score, running, totals, new_values)
    return mixed.astype(jnp.bfloat16)


def greet(peers):
    barrier = pltpu.get_barrier_semaphore()
    for axis, ordered in peers:
        for peer, _ in ordered:
            pl.semaphore_signal(
                barrier, inc=1, device_id={axis: peer}, device_id_type=pl.DeviceIdType.MESH
            )
    pl.semaphore_wait(barrier, sum(len(ordered) for _, ordered in peers))


def ordered_peers(me, digits):
    sizes = [size for size, _ in digits]
    mine, rest = [], me
    for size in reversed(sizes):
        mine.append(lax.rem(rest, size))
        rest = rest // size
    mine = mine[::-1]
    offsets = [o for o in itertools.product(*[range(s) for s in sizes]) if any(o)]
    offsets.sort(key=lambda o: -sum(w * min(d, s - d) for d, (s, w) in zip(o, digits)))

    def compose(o, forward):
        index = 0
        for d, m, s in zip(o, mine, sizes):
            index = index * s + lax.rem(m + (d if forward else s - d), s)
        return index

    return [(compose(o, True), compose(o, False)) for o in offsets]


def send_all(axis, peers, block_of, dst, send_sems, recv_sems, me):
    sends = []
    for k, (peer, _) in enumerate(peers, start=1):
        copy = pltpu.make_async_remote_copy(
            src_ref=block_of(peer),
            dst_ref=dst.at[me],
            send_sem=send_sems.at[k],
            recv_sem=recv_sems.at[k],
            device_id={axis: peer},
            device_id_type=pl.DeviceIdType.MESH,
        )
        copy.start()
        sends.append(copy)
    return sends


def receive_all(axis, peers, block_of, dst, send_sems, recv_sems, sends):
    for k, (_, source) in enumerate(peers, start=1):
        arrival = pltpu.make_async_remote_copy(
            src_ref=block_of(source),
            dst_ref=dst.at[source],
            send_sem=send_sems.at[k],
            recv_sem=recv_sems.at[k],
            device_id={axis: source},
            device_id_type=pl.DeviceIdType.MESH,
        )
        arrival.wait_recv()
    for copy in sends:
        copy.wait_send()


def project_kernel(req_n, head_n, x_hbm, gain_hbm, w_hbm, cos_ref, sin_ref, len_ref, keys_hbm,
                   values_hbm, q_ref, k_ref, v_ref, inside_ref, keys_ref, values_ref,
                   w_ref, gain_ref, rows_buf, part, pair_buf, mixed, sums_buf, sems, w_sem, key_sem):
    me_head = lax.axis_index("head")
    me_req = lax.axis_index("req")
    chips = req_n // 2
    me_core = lax.rem(me_req, 2)
    me_chip = me_req // 2
    partner = me_req + 1 - 2 * me_core
    w_copy = pltpu.make_async_copy(w_hbm, w_ref, w_sem.at[0])
    w_copy.start()
    x_copy = pltpu.make_async_copy(x_hbm, rows_buf.at[me_head], w_sem.at[1])
    x_copy.start()
    gain_copy = pltpu.make_async_copy(gain_hbm, gain_ref, w_sem.at[2])
    gain_copy.start()
    key_copy = pltpu.make_async_copy(keys_hbm, keys_ref, key_sem.at[0])
    key_copy.start()
    value_copy = pltpu.make_async_copy(values_hbm, values_ref, key_sem.at[1])
    value_copy.start()
    chip_peers = [
        (chip * 2 + me_core, None)
        for chip, _ in ordered_peers(me_chip, ((chips // 2, 1), (2, 2)))
    ]
    head_peers = ordered_peers(me_head, ((head_n // 2, 1), (2, 1)))
    greet((("req", chip_peers), ("head", head_peers), ("req", [(partner, None)])))
    own = lambda peer: x_hbm
    sends = send_all("head", head_peers, own, rows_buf, sems.at[0], sems.at[1], me_head)
    receive_all("head", head_peers, own, rows_buf, sems.at[0], sems.at[1], sends)
    x_copy.wait()
    gain_copy.wait()
    block_rows = x_hbm.shape[0]
    states = rows_buf[...].reshape(head_n * block_rows, x_hbm.shape[1]).astype(jnp.float32)
    scaled = (states * gain_ref[...].astype(jnp.float32)[None, :]).astype(jnp.bfloat16)
    columns = w_ref.shape[1]
    square = jnp.sum(states * states, axis=1, keepdims=True)
    w_copy.wait()
    count = k_ref.shape[0]
    scaled = scaled.reshape(chips, 2, count, scaled.shape[-1])
    square = square.reshape(chips, 2, count, 1)

    def half_rows(core):
        pick = lambda x: jnp.where(core == 0, x[:, 0], x[:, 1]).reshape(chips * count, x.shape[-1])
        squares = pick(square)
        packed = jnp.concatenate(
            [jnp.dot(pick(scaled), w_ref[...], preferred_element_type=jnp.float32),
             jnp.broadcast_to(squares, (squares.shape[0], part.shape[-1] - columns))],
            axis=1,
        )
        part[core] = packed.reshape(chips, count, part.shape[-1])

    half_rows(1 - me_core)
    pair = pltpu.make_async_remote_copy(
        src_ref=part.at[1 - me_core],
        dst_ref=pair_buf,
        send_sem=sems.at[2, 0],
        recv_sem=sems.at[3, 0],
        device_id={"req": partner},
        device_id_type=pl.DeviceIdType.MESH,
    )
    pair.start()
    half_rows(me_core)
    pair.wait()
    mixed[...] = part[me_core] + pair_buf[...]
    z_n = chips // 2
    me_z, me_x = me_chip // 2, lax.rem(me_chip, 2)
    offsets = sorted(
        [(dz, dx) for dz in range(z_n) for dx in range(2) if dz or dx],
        key=lambda o: -(min(o[0], z_n - o[0]) + 2 * o[1]),
    )
    sends = []
    for k, (dz, dx) in enumerate(offsets, start=1):
        chip = lax.rem(me_z + dz, z_n) * 2 + lax.rem(me_x + dx, 2)
        copy = pltpu.make_async_remote_copy(
            src_ref=mixed.at[chip],
            dst_ref=sums_buf.at[me_chip],
            send_sem=sems.at[2, k],
            recv_sem=sems.at[3, k],
            device_id={"req": chip * 2 + me_core},
            device_id_type=pl.DeviceIdType.MESH,
        )
        copy.start()
        sends.append(copy)
    for k, (dz, dx) in enumerate(offsets, start=1):
        chip = lax.rem(me_z + z_n - dz, z_n) * 2 + lax.rem(me_x + 2 - dx, 2)
        arrival = pltpu.make_async_remote_copy(
            src_ref=mixed.at[chip],
            dst_ref=sums_buf.at[chip],
            send_sem=sems.at[2, k],
            recv_sem=sems.at[3, k],
            device_id={"req": chip * 2 + me_core},
            device_id_type=pl.DeviceIdType.MESH,
        )
        arrival.wait_recv()
    for copy in sends:
        copy.wait_send()
    total = mixed[me_chip]
    for k in range(1, chips):
        total = total + sums_buf[lax.rem(me_chip + chips - k, chips)]
    mean_square = total[:, columns:columns + 1] / D
    projected = total[:, :columns] * lax.rsqrt(mean_square + epsilon)
    cosine, sine = cos_ref[...], sin_ref[...]
    rotated = lambda block: block * cosine + pltpu.roll(block, HD // 2, 1) * sine
    for g in range(GROUP):
        q_ref[g] = rotated(projected[:, g * HD:(g + 1) * HD]).astype(jnp.bfloat16).astype(jnp.float32)
    k_ref[...] = rotated(projected[:, GROUP * HD:(GROUP + 1) * HD]).astype(k_ref.dtype)
    v_ref[...] = projected[:, (GROUP + 1) * HD:].astype(v_ref.dtype)
    slot = lax.broadcasted_iota(jnp.int32, (1, inside_ref.shape[1]), 1)
    for b in range(inside_ref.shape[0]):
        inside_ref[pl.ds(b, 1), :] = (slot < len_ref[b]).astype(inside_ref.dtype)
    key_copy.wait()
    value_copy.wait()


def project(hidden_in, gain, w_qkv, lengths, k_cache, v_cache, req_n, head_n, count):
    rows, width = hidden_in.shape
    columns = w_qkv.shape[1] + 128
    halfway = HD // 2
    frequency = jnp.exp(
        -jnp.log(rope_base) * 2.0 * jnp.arange(halfway, dtype=jnp.float32) / HD
    )
    angles = lengths.astype(jnp.float32)[:, None] * frequency[None, :]
    cosine = jnp.concatenate([jnp.cos(angles), jnp.cos(angles)], axis=1)
    sine = jnp.concatenate([-jnp.sin(angles), jnp.sin(angles)], axis=1)
    return pl.pallas_call(
        functools.partial(project_kernel, req_n, head_n),
        out_shape=(
            jax.ShapeDtypeStruct((GROUP, count, HD), jnp.float32),
            jax.ShapeDtypeStruct((count, HD), jnp.bfloat16),
            jax.ShapeDtypeStruct((count, HD), jnp.bfloat16),
            jax.ShapeDtypeStruct((count, k_cache.shape[1]), jnp.int32),
            jax.ShapeDtypeStruct(k_cache.shape, k_cache.dtype),
            jax.ShapeDtypeStruct(v_cache.shape, v_cache.dtype),
        ),
        in_specs=[pl.BlockSpec(memory_space=pltpu.HBM)] * 3
        + [pl.BlockSpec(memory_space=pltpu.VMEM)] * 2
        + [pl.BlockSpec(memory_space=pltpu.SMEM)]
        + [pl.BlockSpec(memory_space=pl.ANY)] * 2,
        out_specs=(pl.BlockSpec(memory_space=pltpu.VMEM),) * 6,
        scratch_shapes=[
            pltpu.VMEM(w_qkv.shape, w_qkv.dtype),
            pltpu.VMEM(gain.shape, gain.dtype),
            pltpu.VMEM((head_n, rows, width), hidden_in.dtype),
            pltpu.VMEM((2, req_n // 2, count, columns), jnp.float32),
            pltpu.VMEM((req_n // 2, count, columns), jnp.float32),
            pltpu.VMEM((req_n // 2, count, columns), jnp.float32),
            pltpu.VMEM((req_n // 2, count, columns), jnp.float32),
            pltpu.SemaphoreType.DMA((4, max(req_n, head_n))),
            pltpu.SemaphoreType.DMA((3,)),
            pltpu.SemaphoreType.DMA((2,)),
        ],
        compiler_params=pltpu.CompilerParams(
            collective_id=0, has_side_effects=True, vmem_limit_bytes=30 * 1024 * 1024
        ),
    )(
        pltpu.with_memory_space_constraint(hidden_in, pltpu.HBM),
        pltpu.with_memory_space_constraint(gain, pltpu.HBM),
        pltpu.with_memory_space_constraint(w_qkv, pltpu.HBM),
        cosine, sine, pltpu.with_memory_space_constraint(lengths, pltpu.HBM), k_cache, v_cache,
    )


def output_kernel(req_n, head_n, a_ref, w_hbm, s_ref, o_ref, w_ref, att_buf, part, sums_buf,
                  sems, w_sem):
    me_head = lax.axis_index("head")
    me_req = lax.axis_index("req")
    w_copy = pltpu.make_async_copy(w_hbm, w_ref, w_sem)
    w_copy.start()
    req_peers = ordered_peers(me_req, ((req_n // 4, 1), (2, 2), (2, 0.5)))
    head_peers = ordered_peers(me_head, ((head_n // 2, 1), (2, 1)))
    greet((("req", req_peers), ("head", head_peers)))
    own = lambda peer: a_ref
    sends = send_all("req", req_peers, own, att_buf, sems.at[0], sems.at[1], me_req)
    receive_all("req", req_peers, own, att_buf, sems.at[0], sems.at[1], sends)
    att_buf[me_req] = a_ref[...]
    every = jnp.concatenate(
        [att_buf[s].astype(jnp.float32) for s in range(req_n)], axis=0
    ).astype(jnp.bfloat16)
    w_copy.wait()
    part[...] = jnp.dot(every, w_ref[...], preferred_element_type=jnp.float32)
    rows = o_ref.shape[0]
    chunk = lambda peer: part.at[pl.ds(pl.multiple_of(peer * rows, rows), rows)]
    head_peers = ordered_peers(me_head, ((head_n // 2, 1), (2, 1)))
    sends = send_all("head", head_peers, chunk, sums_buf, sems.at[2], sems.at[3], me_head)
    receive_all("head", head_peers, chunk, sums_buf, sems.at[2], sems.at[3], sends)
    total = part[pl.ds(pl.multiple_of(me_head * rows, rows), rows), :]
    for k in range(1, head_n):
        total = total + sums_buf[lax.rem(me_head + head_n - k, head_n)]
    o_ref[...] = (s_ref[...].astype(jnp.float32) + total).astype(o_ref.dtype)


def output_block(attended, w_out, hidden_in, req_n, head_n):
    count, width = attended.shape
    rows, columns = hidden_in.shape
    return pl.pallas_call(
        functools.partial(output_kernel, req_n, head_n),
        out_shape=jax.ShapeDtypeStruct((rows, columns), hidden_in.dtype),
        in_specs=[
            pl.BlockSpec(memory_space=pltpu.VMEM),
            pl.BlockSpec(memory_space=pl.ANY),
            pl.BlockSpec(memory_space=pltpu.VMEM),
        ],
        out_specs=pl.BlockSpec(memory_space=pltpu.VMEM),
        scratch_shapes=[
            pltpu.VMEM(w_out.shape, w_out.dtype),
            pltpu.VMEM((req_n, count, width), attended.dtype),
            pltpu.VMEM((head_n * rows, columns), jnp.float32),
            pltpu.VMEM((head_n, rows, columns), jnp.float32),
            pltpu.SemaphoreType.DMA((4, max(req_n, head_n))),
            pltpu.SemaphoreType.DMA(()),
        ],
        compiler_params=pltpu.CompilerParams(
            collective_id=1, has_side_effects=True, vmem_limit_bytes=12 * 1024 * 1024
        ),
    )(attended, w_out, hidden_in)


def local(req_n, head_n, hidden_in, attn_gain, w_qkv, w_out, k_cache, v_cache, lengths):
    own_count = k_cache.shape[0]
    queries, new_keys, new_values, inside, k_cache, v_cache = project(
        hidden_in, attn_gain, w_qkv, lengths, k_cache, v_cache, req_n, head_n, own_count
    )
    slots = k_cache.shape[1]
    local_heads = k_cache.shape[2] // HD
    queries = jnp.transpose(queries.astype(jnp.bfloat16), (1, 0, 2))[:, None]
    new_keys = new_keys[:, None]
    new_values = new_values[:, None]
    cached_keys = k_cache.reshape(own_count, slots, local_heads, HD)
    cached_values = v_cache.reshape(own_count, slots, local_heads, HD)
    factor = HD ** (-0.5)
    attended = attend_padded(
        queries, new_keys, new_values, cached_keys, cached_values, inside != 0, factor
    )
    flat_rows = attended.reshape(own_count, local_heads * GROUP * HD)
    return output_block(flat_rows, w_out, hidden_in, req_n, head_n)


def solution(mesh):
    return jax.shard_map(
        functools.partial(local, mesh.shape["req"], mesh.shape["head"]),
        mesh=mesh,
        in_specs=(
            P("head", "req"),
            P("req"),
            P("req", "head"),
            P("head", "req"),
            P("req", None, "head"),
            P("req", None, "head"),
            P("req"),
        ),
        out_specs=P("head", "req"),
        check_vma=False,
    )
```

```python
import functools
import itertools

import jax
import jax.numpy as jnp
from jax import lax
from jax.experimental import pallas as pl
from jax.experimental.pallas import tpu as pltpu
from jax.sharding import PartitionSpec as P

D = 8192
GROUP = 8
HD = 128


epsilon = 1e-05
rope_base = 500000.0


def rotate(vectors, positions):
    halfway = vectors.shape[-1] // 2
    frequency = jnp.exp(
        -jnp.log(rope_base) * 2.0 * jnp.arange(halfway, dtype=jnp.float32) / vectors.shape[-1]
    )
    angles = positions.astype(jnp.float32)[:, None] * frequency[None, :]
    target_shape = (angles.shape[0],) + (1,) * (vectors.ndim - 2) + (halfway,)
    cosine = jnp.cos(angles).reshape(target_shape)
    sine_part = jnp.sin(angles).reshape(target_shape)
    first = vectors[..., :halfway]
    second = vectors[..., halfway:]
    return jnp.concatenate(
        [first * cosine - second * sine_part, second * cosine + first * sine_part], axis=-1
    )


def own_part(own_score, running, totals, new_values):
    own_prob = lax.optimization_barrier(
        (jnp.exp(own_score - running) / totals).astype(jnp.bfloat16)
    )
    return own_prob.astype(jnp.float32)[..., None] * new_values.astype(jnp.float32)[:, :, None, :]


def attend_padded(queries, new_keys, new_values, cached_keys, cached_values, inside, factor):
    scores = (
        jnp.einsum("rkgd,rpkd->rkgp", queries, cached_keys, preferred_element_type=jnp.float32)
        * factor
    )
    scores = jnp.where(inside[:, None, None, :], scores, -1e30)
    own_score = (
        jnp.einsum("rkgd,rkd->rkg", queries, new_keys, preferred_element_type=jnp.float32) * factor
    )
    running = jnp.maximum(jnp.max(scores, axis=3), own_score)
    weights = jnp.where(inside[:, None, None, :], jnp.exp(scores - running[..., None]), 0.0)
    totals = jnp.sum(weights, axis=3) + jnp.exp(own_score - running)
    probs = (weights / totals[..., None]).astype(jnp.bfloat16)
    mixed = jnp.einsum("rkgp,rpkd->rkgd", probs, cached_values, preferred_element_type=jnp.float32)
    mixed = mixed + own_part(own_score, running, totals, new_values)
    return mixed.astype(jnp.bfloat16)


def greet(peers):
    barrier = pltpu.get_barrier_semaphore()
    for axis, ordered in peers:
        for peer, _ in ordered:
            pl.semaphore_signal(
                barrier, inc=1, device_id={axis: peer}, device_id_type=pl.DeviceIdType.MESH
            )
    pl.semaphore_wait(barrier, sum(len(ordered) for _, ordered in peers))


def ordered_peers(me, digits):
    sizes = [size for size, _ in digits]
    mine, rest = [], me
    for size in reversed(sizes):
        mine.append(lax.rem(rest, size))
        rest = rest // size
    mine = mine[::-1]
    offsets = [o for o in itertools.product(*[range(s) for s in sizes]) if any(o)]
    offsets.sort(key=lambda o: -sum(w * min(d, s - d) for d, (s, w) in zip(o, digits)))

    def compose(o, forward):
        index = 0
        for d, m, s in zip(o, mine, sizes):
            index = index * s + lax.rem(m + (d if forward else s - d), s)
        return index

    return [(compose(o, True), compose(o, False)) for o in offsets]


def send_all(axis, peers, block_of, dst, send_sems, recv_sems, me):
    sends = []
    for k, (peer, _) in enumerate(peers, start=1):
        copy = pltpu.make_async_remote_copy(
            src_ref=block_of(peer),
            dst_ref=dst.at[me],
            send_sem=send_sems.at[k],
            recv_sem=recv_sems.at[k],
            device_id={axis: peer},
            device_id_type=pl.DeviceIdType.MESH,
        )
        copy.start()
        sends.append(copy)
    return sends


def receive_all(axis, peers, block_of, dst, send_sems, recv_sems, sends):
    for k, (_, source) in enumerate(peers, start=1):
        arrival = pltpu.make_async_remote_copy(
            src_ref=block_of(source),
            dst_ref=dst.at[source],
            send_sem=send_sems.at[k],
            recv_sem=recv_sems.at[k],
            device_id={axis: source},
            device_id_type=pl.DeviceIdType.MESH,
        )
        arrival.wait_recv()
    for copy in sends:
        copy.wait_send()


def project_kernel(req_n, head_n, x_hbm, gain_hbm, w_hbm, cos_ref, sin_ref, len_ref, keys_hbm,
                   values_hbm, q_ref, k_ref, v_ref, inside_ref, keys_ref, values_ref,
                   w_ref, gain_ref, rows_buf, part, pair_buf, mixed, sums_buf, sems, w_sem, key_sem):
    me_head = lax.axis_index("head")
    me_req = lax.axis_index("req")
    chips = req_n // 2
    me_core = lax.rem(me_req, 2)
    me_chip = me_req // 2
    partner = me_req + 1 - 2 * me_core
    w_copy = pltpu.make_async_copy(w_hbm, w_ref, w_sem.at[0])
    w_copy.start()
    x_copy = pltpu.make_async_copy(x_hbm, rows_buf.at[me_head], w_sem.at[1])
    x_copy.start()
    gain_copy = pltpu.make_async_copy(gain_hbm, gain_ref, w_sem.at[2])
    gain_copy.start()
    key_copy = pltpu.make_async_copy(keys_hbm, keys_ref, key_sem.at[0])
    key_copy.start()
    value_copy = pltpu.make_async_copy(values_hbm, values_ref, key_sem.at[1])
    value_copy.start()
    chip_peers = [
        (chip * 2 + me_core, None)
        for chip, _ in ordered_peers(me_chip, ((chips // 2, 1), (2, 2)))
    ]
    head_peers = ordered_peers(me_head, ((head_n // 2, 1), (2, 1)))
    greet((("req", chip_peers), ("head", head_peers), ("req", [(partner, None)])))
    own = lambda peer: x_hbm
    sends = send_all("head", head_peers, own, rows_buf, sems.at[0], sems.at[1], me_head)
    receive_all("head", head_peers, own, rows_buf, sems.at[0], sems.at[1], sends)
    x_copy.wait()
    gain_copy.wait()
    block_rows = x_hbm.shape[0]
    states = rows_buf[...].reshape(head_n * block_rows, x_hbm.shape[1]).astype(jnp.float32)
    scaled = (states * gain_ref[...].astype(jnp.float32)[None, :]).astype(jnp.bfloat16)
    columns = w_ref.shape[1]
    square = jnp.sum(states * states, axis=1, keepdims=True)
    w_copy.wait()
    packed = jnp.concatenate(
        [jnp.dot(scaled, w_ref[...], preferred_element_type=jnp.float32),
         jnp.broadcast_to(square, (square.shape[0], part.shape[-1] - columns))],
        axis=1,
    )
    count = k_ref.shape[0]
    packed = packed.reshape(chips, 2, count, part.shape[-1])
    part[0] = packed[:, 0]
    part[1] = packed[:, 1]
    pair = pltpu.make_async_remote_copy(
        src_ref=part.at[1 - me_core],
        dst_ref=pair_buf,
        send_sem=sems.at[2, 0],
        recv_sem=sems.at[3, 0],
        device_id={"req": partner},
        device_id_type=pl.DeviceIdType.MESH,
    )
    pair.start()
    pair.wait()
    mixed[...] = part[me_core] + pair_buf[...]
    z_n = chips // 2
    me_z, me_x = me_chip // 2, lax.rem(me_chip, 2)
    offsets = sorted(
        [(dz, dx) for dz in range(z_n) for dx in range(2) if dz or dx],
        key=lambda o: -(min(o[0], z_n - o[0]) + 2 * o[1]),
    )
    sends = []
    for k, (dz, dx) in enumerate(offsets, start=1):
        chip = lax.rem(me_z + dz, z_n) * 2 + lax.rem(me_x + dx, 2)
        copy = pltpu.make_async_remote_copy(
            src_ref=mixed.at[chip],
            dst_ref=sums_buf.at[me_chip],
            send_sem=sems.at[2, k],
            recv_sem=sems.at[3, k],
            device_id={"req": chip * 2 + me_core},
            device_id_type=pl.DeviceIdType.MESH,
        )
        copy.start()
        sends.append(copy)
    for k, (dz, dx) in enumerate(offsets, start=1):
        chip = lax.rem(me_z + z_n - dz, z_n) * 2 + lax.rem(me_x + 2 - dx, 2)
        arrival = pltpu.make_async_remote_copy(
            src_ref=mixed.at[chip],
            dst_ref=sums_buf.at[chip],
            send_sem=sems.at[2, k],
            recv_sem=sems.at[3, k],
            device_id={"req": chip * 2 + me_core},
            device_id_type=pl.DeviceIdType.MESH,
        )
        arrival.wait_recv()
    for copy in sends:
        copy.wait_send()
    total = mixed[me_chip]
    for k in range(1, chips):
        total = total + sums_buf[lax.rem(me_chip + chips - k, chips)]
    mean_square = total[:, columns:columns + 1] / D
    projected = total[:, :columns] * lax.rsqrt(mean_square + epsilon)
    cosine, sine = cos_ref[...], sin_ref[...]
    rotated = lambda block: block * cosine + pltpu.roll(block, HD // 2, 1) * sine
    for g in range(GROUP):
        q_ref[g] = rotated(projected[:, g * HD:(g + 1) * HD]).astype(jnp.bfloat16).astype(jnp.float32)
    k_ref[...] = rotated(projected[:, GROUP * HD:(GROUP + 1) * HD]).astype(k_ref.dtype)
    v_ref[...] = projected[:, (GROUP + 1) * HD:].astype(v_ref.dtype)
    slot = lax.broadcasted_iota(jnp.int32, (1, inside_ref.shape[1]), 1)
    for b in range(inside_ref.shape[0]):
        inside_ref[pl.ds(b, 1), :] = (slot < len_ref[b]).astype(inside_ref.dtype)
    key_copy.wait()
    value_copy.wait()


def project(hidden_in, gain, w_qkv, lengths, k_cache, v_cache, req_n, head_n, count):
    rows, width = hidden_in.shape
    columns = w_qkv.shape[1] + 128
    halfway = HD // 2
    frequency = jnp.exp(
        -jnp.log(rope_base) * 2.0 * jnp.arange(halfway, dtype=jnp.float32) / HD
    )
    angles = lengths.astype(jnp.float32)[:, None] * frequency[None, :]
    cosine = jnp.concatenate([jnp.cos(angles), jnp.cos(angles)], axis=1)
    sine = jnp.concatenate([-jnp.sin(angles), jnp.sin(angles)], axis=1)
    return pl.pallas_call(
        functools.partial(project_kernel, req_n, head_n),
        out_shape=(
            jax.ShapeDtypeStruct((GROUP, count, HD), jnp.float32),
            jax.ShapeDtypeStruct((count, HD), jnp.bfloat16),
            jax.ShapeDtypeStruct((count, HD), jnp.bfloat16),
            jax.ShapeDtypeStruct((count, k_cache.shape[1]), jnp.int32),
            jax.ShapeDtypeStruct(k_cache.shape, k_cache.dtype),
            jax.ShapeDtypeStruct(v_cache.shape, v_cache.dtype),
        ),
        in_specs=[pl.BlockSpec(memory_space=pltpu.HBM)] * 3
        + [pl.BlockSpec(memory_space=pltpu.VMEM)] * 2
        + [pl.BlockSpec(memory_space=pltpu.SMEM)]
        + [pl.BlockSpec(memory_space=pl.ANY)] * 2,
        out_specs=(pl.BlockSpec(memory_space=pltpu.VMEM),) * 6,
        scratch_shapes=[
            pltpu.VMEM(w_qkv.shape, w_qkv.dtype),
            pltpu.VMEM(gain.shape, gain.dtype),
            pltpu.VMEM((head_n, rows, width), hidden_in.dtype),
            pltpu.VMEM((2, req_n // 2, count, columns), jnp.float32),
            pltpu.VMEM((req_n // 2, count, columns), jnp.float32),
            pltpu.VMEM((req_n // 2, count, columns), jnp.float32),
            pltpu.VMEM((req_n // 2, count, columns), jnp.float32),
            pltpu.SemaphoreType.DMA((4, max(req_n, head_n))),
            pltpu.SemaphoreType.DMA((3,)),
            pltpu.SemaphoreType.DMA((2,)),
        ],
        compiler_params=pltpu.CompilerParams(
            collective_id=0, has_side_effects=True, vmem_limit_bytes=30 * 1024 * 1024
        ),
    )(
        pltpu.with_memory_space_constraint(hidden_in, pltpu.HBM),
        pltpu.with_memory_space_constraint(gain, pltpu.HBM),
        pltpu.with_memory_space_constraint(w_qkv, pltpu.HBM),
        cosine, sine, pltpu.with_memory_space_constraint(lengths, pltpu.HBM), k_cache, v_cache,
    )


def output_kernel(req_n, head_n, a_ref, w_hbm, s_ref, o_ref, w_ref, att_buf, part, sums_buf,
                  sems, w_sem):
    me_head = lax.axis_index("head")
    me_req = lax.axis_index("req")
    w_copy = pltpu.make_async_copy(w_hbm, w_ref, w_sem)
    w_copy.start()
    req_peers = ordered_peers(me_req, ((req_n // 4, 1), (2, 2), (2, 0.5)))
    head_peers = ordered_peers(me_head, ((head_n // 2, 1), (2, 1)))
    greet((("req", req_peers), ("head", head_peers)))
    own = lambda peer: a_ref
    sends = send_all("req", req_peers, own, att_buf, sems.at[0], sems.at[1], me_req)
    receive_all("req", req_peers, own, att_buf, sems.at[0], sems.at[1], sends)
    att_buf[me_req] = a_ref[...]
    every = jnp.concatenate(
        [att_buf[s].astype(jnp.float32) for s in range(req_n)], axis=0
    ).astype(jnp.bfloat16)
    w_copy.wait()
    part[...] = jnp.dot(every, w_ref[...], preferred_element_type=jnp.float32)
    rows = o_ref.shape[0]
    chunk = lambda peer: part.at[pl.ds(pl.multiple_of(peer * rows, rows), rows)]
    head_peers = ordered_peers(me_head, ((head_n // 2, 1), (2, 1)))
    sends = send_all("head", head_peers, chunk, sums_buf, sems.at[2], sems.at[3], me_head)
    receive_all("head", head_peers, chunk, sums_buf, sems.at[2], sems.at[3], sends)
    total = part[pl.ds(pl.multiple_of(me_head * rows, rows), rows), :]
    for k in range(1, head_n):
        total = total + sums_buf[lax.rem(me_head + head_n - k, head_n)]
    o_ref[...] = total


def output_block(attended, w_out, hidden_in, req_n, head_n):
    count, width = attended.shape
    rows, columns = hidden_in.shape
    return pl.pallas_call(
        functools.partial(output_kernel, req_n, head_n),
        out_shape=jax.ShapeDtypeStruct((rows, columns), jnp.float32),
        in_specs=[
            pl.BlockSpec(memory_space=pltpu.VMEM),
            pl.BlockSpec(memory_space=pl.ANY),
            pl.BlockSpec(memory_space=pltpu.VMEM),
        ],
        out_specs=pl.BlockSpec(memory_space=pltpu.VMEM),
        scratch_shapes=[
            pltpu.VMEM(w_out.shape, w_out.dtype),
            pltpu.VMEM((req_n, count, width), attended.dtype),
            pltpu.VMEM((head_n * rows, columns), jnp.float32),
            pltpu.VMEM((head_n, rows, columns), jnp.float32),
            pltpu.SemaphoreType.DMA((4, max(req_n, head_n))),
            pltpu.SemaphoreType.DMA(()),
        ],
        compiler_params=pltpu.CompilerParams(
            collective_id=1, has_side_effects=True, vmem_limit_bytes=12 * 1024 * 1024
        ),
    )(attended, w_out, hidden_in)


def local(req_n, head_n, hidden_in, attn_gain, w_qkv, w_out, k_cache, v_cache, lengths):
    own_count = k_cache.shape[0]
    queries, new_keys, new_values, inside, k_cache, v_cache = project(
        hidden_in, attn_gain, w_qkv, lengths, k_cache, v_cache, req_n, head_n, own_count
    )
    slots = k_cache.shape[1]
    local_heads = k_cache.shape[2] // HD
    queries = jnp.transpose(queries.astype(jnp.bfloat16), (1, 0, 2))[:, None]
    new_keys = new_keys[:, None]
    new_values = new_values[:, None]
    cached_keys = k_cache.reshape(own_count, slots, local_heads, HD)
    cached_values = v_cache.reshape(own_count, slots, local_heads, HD)
    factor = HD ** (-0.5)
    attended = attend_padded(
        queries, new_keys, new_values, cached_keys, cached_values, inside != 0, factor
    )
    flat_rows = attended.reshape(own_count, local_heads * GROUP * HD)
    output = output_block(flat_rows, w_out, hidden_in, req_n, head_n)
    return (hidden_in.astype(jnp.float32) + output).astype(jnp.bfloat16)


def solution(mesh):
    return jax.shard_map(
        functools.partial(local, mesh.shape["req"], mesh.shape["head"]),
        mesh=mesh,
        in_specs=(
            P("head", "req"),
            P("req"),
            P("req", "head"),
            P("head", "req"),
            P("req", None, "head"),
            P("req", None, "head"),
            P("req"),
        ),
        out_specs=P("head", "req"),
        check_vma=False,
    )
```
